256 devices in a mesh: section: 4 (over y_hi, core), gx: 64 (over z, y_lo, x).
Axes of the slice: x: 4, y: 4 (y_hi: 2, y_lo: 2; y = y_hi * 2 + y_lo), z: 8, core: 2. Of those that a mesh axis runs over, the one named last changes fastest.
Arguments:
- samples: bfloat16 [2, 1024, 32, 4096], P(None, 'gx', 'section'), may hold values from -8 to 8
- positions: float32 [2, 1024], replicated, may hold values from 0 to 8
- beam_dir: int32 [64], replicated, may hold values from 0 to 63, each once
- load_exp: int32 [4096], P(('section', 'gx')), may hold values from 0 to 3
Outputs:
- beams_out: bfloat16 [2, 64, 32, 4096], P(None, 'gx', 'section')
The draws below stay inside these ranges and needn't reach their ends.
Inputs may be any that keep to these rules, and one draw needn't show every extreme that they name: `beam_dir`: every direction index 0 to 63 belongs to exactly one beam.
All inputs are finite; a program needn't handle non-finite values.
Results may differ from the reference program's by a relative error of at most 0.018.
Values may be sent and summed in bfloat16 or wider, within the bound.
No kernel may reach another device: no remote copies, remote signals or barrier semaphores. Data moves between devices by JAX's collectives and lax.ppermute only.
A program may use at most 128 MiB of HBM per device.

```python
import math
import jax
import jax.numpy as jnp
from jax import lax

M = 1024
RADIX = 64
F = 4096
B = 64
TAPS = 4
ITERS = 2
K = 32


def draw_samples(key, part):
    gain_key = jax.random.fold_in(key, 11)
    noise_key = jax.random.fold_in(key, 12)
    gains = jnp.exp(jax.random.uniform(gain_key, (1, M, 1, 1), jnp.float32, math.log(0.3), math.log(3.0)))
    values = gains * jax.random.normal(noise_key, (2, M, K, F), jnp.float32)
    return jnp.clip(values, -8.0, 8.0).astype(jnp.bfloat16)


def with_ends(values, rng, least, largest):
    spot = [jax.random.randint(jax.random.fold_in(rng, axis), (), 0, length) for axis, length in enumerate(values.shape)]
    widest = values.shape.index(max(values.shape))
    neighbour = spot[:widest] + [(spot[widest] + 1) % values.shape[widest]] + spot[widest + 1:]
    return values.at[tuple(spot)].set(least).at[tuple(neighbour)].set(largest)


def setup_inputs(seed: int = 0) -> dict:
    key_of = jax.random.split(jax.random.key(seed), 5)
    samples = draw_samples(jax.random.fold_in(key_of[4], 71), 0)
    positions = jnp.clip(jax.random.uniform(key_of[1], (2, M), jnp.float32, 0.0, 8.0), 0.0, 8.0)
    beam_dir = jax.random.permutation(key_of[2], B).astype(jnp.int32)
    load_exp = with_ends(jax.random.randint(key_of[3], (F,), 0, 4), jax.random.fold_in(key_of[3], 1), 0, 3).astype(jnp.int32)
    return {"samples": samples, "positions": positions, "beam_dir": beam_dir, "load_exp": load_exp}


def prototype(taps_count, length):
    total_len = taps_count * length
    position = jnp.arange(total_len, dtype=jnp.int32).astype(jnp.float32) + 0.5
    window = 0.5 - 0.5 * jnp.cos(2.0 * math.pi / total_len * position)
    shaped = jnp.sinc((position - 0.5 * total_len) / length) * window
    return shaped.reshape(taps_count, length)

def dft_tables(radix_size):
    length = radix_size * radix_size
    counter = jnp.arange(radix_size, dtype=jnp.int32)
    products = counter[:, None] * counter[None, :]
    angles = 2.0 * math.pi / radix_size * (products % radix_size).astype(jnp.float32)
    twiddle = 2.0 * math.pi / length * products.astype(jnp.float32)
    return (jnp.cos(angles).astype(jnp.bfloat16), jnp.sin(angles).astype(jnp.bfloat16), jnp.cos(twiddle), jnp.sin(twiddle))

def contract(matrix, values, pattern):
    return jnp.einsum(pattern, matrix.astype(jnp.float32), values.astype(jnp.float32), precision=lax.Precision.HIGHEST)

def transform(real_part, imag_part, direction_sign, radix_size):
    cosine, sine_table, twist_cos, twist_sin = dft_tables(radix_size)
    leading = real_part.shape[:-1]
    first_real = real_part.reshape(leading + (radix_size, radix_size))
    first_imag = imag_part.reshape(leading + (radix_size, radix_size))
    pattern_one = 'fa,...ab->...fb'
    mid_real = contract(cosine, first_real, pattern_one) - direction_sign * contract(sine_table, first_imag, pattern_one)
    mid_imag = contract(cosine, first_imag, pattern_one) + direction_sign * contract(sine_table, first_real, pattern_one)
    turned_real = (mid_real * twist_cos - direction_sign * mid_imag * twist_sin).astype(jnp.bfloat16)
    turned_imag = (mid_imag * twist_cos + direction_sign * mid_real * twist_sin).astype(jnp.bfloat16)
    pattern_two = 'gb,...fb->...gf'
    out_real = contract(cosine, turned_real, pattern_two) - direction_sign * contract(sine_table, turned_imag, pattern_two)
    out_imag = contract(cosine, turned_imag, pattern_two) + direction_sign * contract(sine_table, turned_real, pattern_two)
    inverse = 1.0 / radix_size
    full_shape = leading + (radix_size * radix_size,)
    return ((out_real * inverse).astype(jnp.bfloat16).reshape(full_shape), (out_imag * inverse).astype(jnp.bfloat16).reshape(full_shape))

def product(pattern, left, right):
    return jnp.einsum(pattern, left.astype(jnp.float32), right.astype(jnp.float32), precision=lax.Precision.HIGHEST)

def beamform(spectra_block, loading, angular, projection):
    x_real = spectra_block[:, 0]
    x_imag = spectra_block[:, 1]
    snapshots = x_real.shape[1]
    phases = angular[:, None, None] * projection[None]
    steer_real = jnp.cos(phases)
    steer_imag = -jnp.sin(phases)
    sol_real = jnp.zeros_like(steer_real)
    sol_imag = jnp.zeros_like(steer_imag)
    res_real, res_imag = (steer_real, steer_imag)
    dir_real, dir_imag = (steer_real, steer_imag)
    residual_power = lax.optimization_barrier(jnp.sum(res_real * res_real + res_imag * res_imag, axis=-1))
    load_col = loading[:, None]
    for sweep_index in range(ITERS):
        low_real = dir_real.astype(jnp.bfloat16)
        low_imag = dir_imag.astype(jnp.bfloat16)
        proj_real = (product('jbm,jkm->jbk', low_real, x_real) + product('jbm,jkm->jbk', low_imag, x_imag)).astype(jnp.bfloat16)
        proj_imag = (product('jbm,jkm->jbk', low_imag, x_real) - product('jbm,jkm->jbk', low_real, x_imag)).astype(jnp.bfloat16)
        image_real = (product('jbk,jkm->jbm', proj_real, x_real) - product('jbk,jkm->jbm', proj_imag, x_imag)) / snapshots + load_col[..., None] * low_real.astype(jnp.float32)
        image_imag = (product('jbk,jkm->jbm', proj_real, x_imag) + product('jbk,jkm->jbm', proj_imag, x_real)) / snapshots + load_col[..., None] * low_imag.astype(jnp.float32)
        proj_wide_real = proj_real.astype(jnp.float32)
        proj_wide_imag = proj_imag.astype(jnp.float32)
        low_wide_real = low_real.astype(jnp.float32)
        low_wide_imag = low_imag.astype(jnp.float32)
        curvature = lax.optimization_barrier(jnp.sum(proj_wide_real * proj_wide_real + proj_wide_imag * proj_wide_imag, axis=-1)) / snapshots + load_col * lax.optimization_barrier(jnp.sum(low_wide_real * low_wide_real + low_wide_imag * low_wide_imag, axis=-1))
        step_size = (residual_power / curvature)[..., None]
        sol_real = sol_real + step_size * dir_real
        sol_imag = sol_imag + step_size * dir_imag
        res_real = res_real - step_size * image_real
        res_imag = res_imag - step_size * image_imag
        new_power = lax.optimization_barrier(jnp.sum(res_real * res_real + res_imag * res_imag, axis=-1))
        ratio = (new_power / residual_power)[..., None]
        dir_real = res_real + ratio * dir_real
        dir_imag = res_imag + ratio * dir_imag
        residual_power = new_power
    mean_sq = lax.optimization_barrier(jnp.mean(sol_real * sol_real + sol_imag * sol_imag, axis=-1)) + 1e-06
    normalizer = lax.rsqrt(sol_real.shape[-1] * mean_sq)[..., None]
    weight_real = (sol_real * normalizer).astype(jnp.bfloat16)
    weight_imag = (sol_imag * normalizer).astype(jnp.bfloat16)
    output_real = (product('jbm,jkm->jbk', weight_real, x_real) + product('jbm,jkm->jbk', weight_imag, x_imag)).astype(jnp.bfloat16)
    output_imag = (product('jbm,jkm->jbk', weight_real, x_imag) - product('jbm,jkm->jbk', weight_imag, x_real)).astype(jnp.bfloat16)
    return jnp.stack([output_real, output_imag], axis=1)

def reference(samples, positions, beam_dir, load_exp):
    shaping = prototype(TAPS, F)
    history = TAPS - 1
    input_block = 16

    def channelize(block_index):
        segment = lax.dynamic_slice_in_dim(samples, block_index * input_block, input_block, 1).astype(jnp.float32)
        padded = jnp.pad(segment, ((0, 0), (0, 0), (history, 0), (0, 0)))
        filtered = shaping[0] * padded[:, :, history:history + K, :]
        for tap_index in range(1, TAPS):
            filtered = filtered + shaping[tap_index] * padded[:, :, history - tap_index:history - tap_index + K, :]
        filtered = filtered.astype(jnp.bfloat16)
        spec_real, spec_imag = transform(filtered[0], filtered[1], -1.0, RADIX)
        return jnp.stack([spec_real, spec_imag])
    blocks = lax.map(channelize, jnp.arange(M // input_block, dtype=jnp.int32))
    spectra = jnp.transpose(blocks, (4, 1, 3, 0, 2)).reshape(F, 2, K, M)
    angle_beam = math.pi / B * (beam_dir.astype(jnp.float32) + 0.5) - 0.5 * math.pi
    projection = jnp.sin(angle_beam)[:, None] * positions[0][None, :] + jnp.cos(angle_beam)[:, None] * positions[1][None, :]
    loading = jnp.exp2(load_exp.astype(jnp.float32))
    freq_all = 2.0 * math.pi * (0.75 + 0.5 * jnp.arange(F, dtype=jnp.int32).astype(jnp.float32) / F)
    channel_block = 16
    block_count = F // channel_block
    outputs = lax.map(lambda members: beamform(members[0], members[1], members[2], projection), (spectra.reshape(block_count, channel_block, 2, K, M), loading.reshape(block_count, channel_block), freq_all.reshape(block_count, channel_block)))
    beam_spec = outputs.reshape(F, 2, B, K)
    ordered = jnp.transpose(beam_spec, (1, 2, 3, 0))
    time_real, time_imag = transform(ordered[0], ordered[1], 1.0, RADIX)
    series = jnp.stack([time_real, time_imag]).astype(jnp.float32)
    padded = jnp.pad(series, ((0, 0), (0, 0), (history, 0), (0, 0)))
    summed = shaping[TAPS - 1] * padded[:, :, history:history + K, :]
    for tap_index in range(1, TAPS):
        summed = summed + shaping[TAPS - 1 - tap_index] * padded[:, :, history - tap_index:history - tap_index + K, :]
    return summed.astype(jnp.bfloat16)
```

```python
import math

import numpy as np
import jax
import jax.numpy as jnp
from jax import lax
from jax.experimental import pallas as pl
from jax.experimental.pallas import tpu as pltpu
from jax.sharding import PartitionSpec as P

TAPS = 4
LANES = 128
COLS = 32
AXES = ("section", "gx")


def prototype_table():
    total = TAPS * COLS * LANES
    position = np.arange(total, dtype=np.float64) + 0.5
    window = 0.5 - 0.5 * np.cos(2.0 * np.pi / total * position)
    shaped = np.sinc((position - 0.5 * total) / (COLS * LANES)) * window
    return shaped.reshape(TAPS, COLS, LANES).astype(np.float32)


def lane_transform(sign, scale):
    l = np.arange(LANES)
    angle = 2.0 * np.pi * ((l[:, None] * l[None, :]) % LANES) / LANES
    c, s = np.cos(angle) * scale, sign * np.sin(angle) * scale
    return np.block([[c, s], [-s, c]])


def forward_columns():
    lane = np.arange(LANES)
    order = (lane // 16) + 8 * (lane % 16)
    table = lane_transform(-1.0, 1.0 / 64.0)
    return table[:, np.concatenate([order, LANES + order])]


def inverse_rows():
    table = lane_transform(1.0, 1.0 / 64.0)
    b, c, e = np.meshgrid(np.arange(8), np.arange(2), np.arange(16), indexing="ij")
    return table[(c * LANES + b + 8 * e).reshape(-1)]


def twiddle(re, im, k, n, sign):
    k = k % n
    if k == 0:
        return re, im
    if 4 * k == n:
        return (im, -re) if sign < 0 else (-im, re)
    if 8 * k == n:
        c = math.sqrt(0.5)
        return ((re + im) * c, (im - re) * c) if sign < 0 else ((re - im) * c, (im + re) * c)
    if 8 * k == 3 * n:
        c = math.sqrt(0.5)
        return ((im - re) * c, (-im - re) * c) if sign < 0 else ((-re - im) * c, (re - im) * c)
    c, s = math.cos(2 * math.pi * k / n), sign * math.sin(2 * math.pi * k / n)
    return re * c - im * s, re * s + im * c


def fft(values, sign):
    n = len(values)
    if n == 1:
        return values
    even = fft(values[0::2], sign)
    odd = fft(values[1::2], sign)
    low, high = [], []
    for k in range(n // 2):
        tr, ti = twiddle(odd[k][0], odd[k][1], k, n, sign)
        er, ei = even[k]
        low.append((er + tr, ei + ti))
        high.append((er - tr, ei - ti))
    return low + high


def shifted_sum(x, h, taps):
    row = lax.broadcasted_iota(jnp.int32, x.shape, 0)
    out = taps[0] * x
    for p in range(1, TAPS):
        out = out + taps[p] * pltpu.roll(jnp.where(row >= 8 - p, h, x), p, 0)
    return out


def analysis_kernel(x_ref, h_ref, proto_ref, tw_ref, w_ref, o_ref, z_ref):
    def one_input(m, _):
        values = []
        for j in range(COLS):
            cut = slice(j * LANES, (j + 1) * LANES)
            taps = [proto_ref[p, j : j + 1, :] for p in range(TAPS)]
            pair = []
            for c in range(2):
                x = x_ref[c, m, :, cut].astype(jnp.float32)
                h3 = h_ref[c, m, :, cut].astype(jnp.float32)
                h = jnp.concatenate([x[:5], h3], axis=0)
                pair.append(shifted_sum(x, h, taps))
            values.append(tuple(pair))
        for a, (re, im) in enumerate(fft(values, -1.0)):
            cs = tw_ref[0, m, a : a + 1, :]
            sn = tw_ref[1, m, a : a + 1, :]
            z_ref[m, a, :, :LANES] = re * cs - im * sn
            z_ref[m, a, :, LANES:] = re * sn + im * cs
        return 0

    lax.fori_loop(0, 8, one_input, 0)
    seg = lax.broadcasted_iota(jnp.int32, (1, 8, 2 * LANES), 2) % LANES // 16
    bits = [(seg // (1 << t)) % 2 == 1 for t in range(3)]

    def some_columns(i, _):
        a0 = i * 4
        z = z_ref[:, pl.ds(a0, 4)].reshape(8 * 4 * 8, 2 * LANES).astype(jnp.bfloat16)
        out = jnp.dot(z, w_ref[...], preferred_element_type=jnp.float32)
        out = out.reshape(8, 4, 8, 2 * LANES)
        v = [out[r] for r in range(8)]
        for t in range(3):
            mask = jnp.broadcast_to(bits[t], (4, 8, 2 * LANES))
            v = [jnp.where(mask, v[(r + (1 << t)) % 8], v[r]) for r in range(8)]
        for b in range(8):
            w = v[(-b) % 8].astype(jnp.bfloat16)
            for ai in range(4):
                a = a0 + ai
                dest = (a % 16) * 16 + 2 * b + a // 16
                for c in range(2):
                    o_ref[dest, 0, c] = w[ai, :, c * LANES : (c + 1) * LANES]
        return 0

    lax.fori_loop(0, 8, some_columns, 0)


def beam_kernel(b_ref, lam_ref, r_ref, s_ref, y_ref, x_ref):
    b = b_ref[0]
    lane = lax.broadcasted_iota(jnp.int32, (8, LANES), 1)
    shift = (lane % 16 - jnp.where(lane // 16 < b, 1, 0) + 16) % 16
    bits = [(shift // (1 << t)) % 2 == 1 for t in range(4)]

    for pair in range(2):
        for c in range(2):

            def separate(i, _, pair=pair, c=c):
                g2 = i // 2
                mh = i % 2
                halves = []
                for half in range(2):
                    base = (pair * 2 + half) * 64 + g2 * 16
                    v = [r_ref[base + g, mh, c].astype(jnp.float32) for g in range(16)]
                    for t in range(4):
                        v = [jnp.where(bits[t], v[(r + (1 << t)) % 16], v[r]) for r in range(16)]
                    halves.append(v)
                col = pl.multiple_of(i * LANES, LANES)
                far = pl.multiple_of(i * LANES + 1024, LANES)
                for e in range(16):
                    r = (-e) % 16
                    w = jnp.concatenate([halves[0][r], halves[1][r]], axis=0)
                    w16 = w.astype(jnp.bfloat16)
                    top = slice(pair * 16, pair * 16 + 16)
                    bot = slice(32 + pair * 16, 32 + pair * 16 + 16)
                    if c == 0:
                        x_ref[e, top, pl.ds(col, LANES)] = w16
                        x_ref[e, bot, pl.ds(far, LANES)] = w16
                    else:
                        x_ref[e, top, pl.ds(far, LANES)] = w16
                        x_ref[e, bot, pl.ds(col, LANES)] = (-w).astype(jnp.bfloat16)
                return 0

            lax.fori_loop(0, 8, separate, 0)

    total = 1024.0
    snapshots = 32.0
    sign = jnp.where(lax.broadcasted_iota(jnp.int32, (64, 64), 1) < 32, 1.0, -1.0)

    def channel(e, _):
        x = x_ref[e]
        dims = (((1,), (1,)), ((), ()))
        h = lax.dot_general(s_ref[e], x, dims, preferred_element_type=jnp.float32)
        gram = lax.dot_general(x, x, dims, preferred_element_type=jnp.float32)
        gh = jnp.dot(h, gram, precision=lax.Precision.HIGHEST, preferred_element_type=jnp.float32)
        lam = lam_ref[e]
        hh = jnp.sum(h * h, axis=1, keepdims=True)
        hgh = jnp.sum(h * gh, axis=1, keepdims=True)
        alpha = total / (hh / snapshots + lam * total)
        rho = 1.0 - alpha * lam
        t = alpha / snapshots
        new = rho * rho * total - 2.0 * rho * t * hh + t * t * hgh
        along = rho + new / total
        proj = along * h - t * gh
        size = along * along * total - 2.0 * along * t * hh + t * t * hgh
        curv = jnp.sum(proj * proj, axis=1, keepdims=True) / snapshots + lam * size
        alpha2 = new / curv
        main = alpha + alpha2 * along
        rest = alpha2 * t
        power = main * main * total - 2.0 * main * rest * hh + rest * rest * hgh
        norm = lax.rsqrt(power + total * 1e-6)
        y_ref[e] = (sign * ((norm * main) * h - (norm * rest) * gh)).astype(jnp.bfloat16)
        return 0

    lax.fori_loop(0, 16, channel, 0)


def synthesis_kernel(t_ref, proto_ref, tw_ref, w_ref, o_ref, z_ref, s_ref):
    full = jnp.dot(t_ref[...], w_ref[...], preferred_element_type=jnp.float32)
    z_ref[...] = full.reshape(COLS, 16, 2 * LANES)

    def half(i, _):
        rows = pl.ds(pl.multiple_of(i * 8, 8), 8)
        values = []
        for a in range(COLS):
            re = z_ref[a, rows, :LANES]
            im = z_ref[a, rows, LANES:]
            cs = tw_ref[0, a : a + 1, :]
            sn = tw_ref[1, a : a + 1, :]
            values.append((re * cs - im * sn, re * sn + im * cs))
        for j, (re, im) in enumerate(fft(values, 1.0)):
            s_ref[0, i, j] = re.astype(jnp.bfloat16).astype(jnp.float32)
            s_ref[1, i, j] = im.astype(jnp.bfloat16).astype(jnp.float32)
        return 0

    lax.fori_loop(0, 2, half, 0)
    for c in range(2):
        for j in range(COLS):
            taps = [proto_ref[TAPS - 1 - p, j : j + 1, :] for p in range(TAPS)]
            out = shifted_sum(s_ref[c, 1, j], s_ref[c, 0, j], taps)
            o_ref[c, 0, :, j * LANES : (j + 1) * LANES] = out.astype(jnp.bfloat16)


def body(samples, positions, beam_dir, load_exp):
    sections = lax.axis_size("section")
    groups = lax.axis_size("gx")
    device = lax.axis_index(AXES).astype(jnp.int32)
    place = device % groups
    own_b = (device % 16) // 2
    own_a = device // 16 + 16 * (device % 2)

    proto = jnp.asarray(prototype_table())
    w_forward = jnp.asarray(forward_columns(), jnp.bfloat16)
    w_inverse = jnp.asarray(inverse_rows(), jnp.bfloat16)

    hist = lax.ppermute(
        samples[:, :, 8 - (TAPS - 1) :, :], "section", [(i, i + 1) for i in range(sections - 1)]
    )

    mu = jnp.arange(8, dtype=jnp.int32)[:, None, None]
    a_index = jnp.arange(COLS, dtype=jnp.int32)[None, :, None]
    l_index = jnp.arange(LANES, dtype=jnp.int32)[None, None, :]
    count = (a_index * l_index - 32 * (mu + 8 * (place % 16)) * l_index) & 4095
    angle = (2.0 * math.pi / 4096.0) * count.astype(jnp.float32)
    tw_forward = jnp.stack([jnp.cos(angle), -jnp.sin(angle)])
    n_angle = 2.0 * np.pi / 4096.0 * (np.arange(COLS)[:, None] * np.arange(LANES)[None, :])
    tw_inverse = jnp.asarray(np.stack([np.cos(n_angle), np.sin(n_angle)]), jnp.float32)

    message = pl.pallas_call(
        analysis_kernel,
        grid=(2,),
        in_specs=[
            pl.BlockSpec((2, 8, 8, 4096), lambda i: (0, i, 0, 0)),
            pl.BlockSpec((2, 8, TAPS - 1, 4096), lambda i: (0, i, 0, 0)),
            pl.BlockSpec((TAPS, COLS, LANES), lambda i: (0, 0, 0)),
            pl.BlockSpec((2, 8, COLS, LANES), lambda i: (0, 0, 0, 0)),
            pl.BlockSpec((2 * LANES, 2 * LANES), lambda i: (0, 0)),
        ],
        out_specs=pl.BlockSpec((256, 1, 2, 8, LANES), lambda i: (0, i, 0, 0, 0)),
        out_shape=jax.ShapeDtypeStruct((256, 2, 2, 8, LANES), jnp.bfloat16),
        scratch_shapes=[pltpu.VMEM((8, COLS, 8, 2 * LANES), jnp.float32)],
        name="analysis",
    )(samples, hist, proto, tw_forward, w_forward)

    message, positions, load_exp, beam_dir = lax.optimization_barrier(
        (message, positions, load_exp, beam_dir)
    )
    received = lax.all_to_all(message, AXES, 0, 0, tiled=True)

    slot = (jnp.arange(16, dtype=jnp.int32) == device // 16).astype(jnp.float32)
    table = slot[:, None] * load_exp.astype(jnp.float32)[None, :]
    for t in range(4):
        step = 16 << t
        table = table + lax.ppermute(table, AXES, [(i, i ^ step) for i in range(sections * groups)])
    mine = jnp.sum(table * (jnp.arange(16, dtype=jnp.int32) == device // 16)[None, :], axis=1)
    lam = jnp.exp2(mine)

    spread = positions.reshape(2, 4, 16, 2, 8).transpose(0, 1, 3, 4, 2)
    spread = jnp.roll(spread, own_b, axis=3)
    early = (jnp.arange(8, dtype=jnp.int32) < own_b)[None, None, None, :, None]
    rolled = [jnp.roll(spread, e, axis=4) for e in range(16)]
    ordered = jnp.stack([jnp.where(early, rolled[(e + 1) % 16], rolled[e]) for e in range(16)])
    ordered = ordered.reshape(16, 2, 1024)
    channel = own_a + 32 * own_b + 256 * jnp.arange(16, dtype=jnp.int32)
    angular = 2.0 * math.pi * (0.75 + 0.5 * channel.astype(jnp.float32) / 4096)
    beams = beam_dir.shape[0]
    angle_beam = math.pi / beams * (beam_dir.astype(jnp.float32) + 0.5) - 0.5 * math.pi
    projection = (
        jnp.sin(angle_beam)[None, :, None] * ordered[:, 0][:, None, :]
        + jnp.cos(angle_beam)[None, :, None] * ordered[:, 1][:, None, :]
    )
    phases = angular[:, None, None] * projection
    steer = jnp.concatenate([jnp.cos(phases), -jnp.sin(phases)], axis=-1).astype(jnp.bfloat16)

    formed = pl.pallas_call(
        beam_kernel,
        in_specs=[
            pl.BlockSpec(memory_space=pltpu.SMEM),
            pl.BlockSpec(memory_space=pltpu.SMEM),
            pl.BlockSpec(memory_space=pltpu.VMEM),
            pl.BlockSpec(memory_space=pltpu.VMEM),
        ],
        out_specs=pl.BlockSpec(memory_space=pltpu.VMEM),
        out_shape=jax.ShapeDtypeStruct((16, beams, 64), jnp.bfloat16),
        scratch_shapes=[pltpu.VMEM((16, 64, 2048), jnp.bfloat16)],
        name="beams",
    )(own_b[None], lam, received, steer)

    padded = jnp.pad(formed.reshape(16, beams, 2, 32), ((0, 0), (0, 0), (0, 0), (8, 0)))
    windows = jnp.stack([padded[..., 8 * s : 8 * s + 16] for s in range(sections)])
    back = windows.transpose(0, 2, 4, 3, 1).reshape(sections * groups, 4, LANES)
    returned = lax.all_to_all(back, AXES, 0, 0, tiled=True)
    opened = returned.reshape(16, 8, 2, 16, 32).transpose(2, 0, 3, 1, 4).reshape(COLS * 16, 256)

    return pl.pallas_call(
        synthesis_kernel,
        in_specs=[pl.BlockSpec(memory_space=pltpu.VMEM)] * 4,
        out_specs=pl.BlockSpec(memory_space=pltpu.VMEM),
        out_shape=jax.ShapeDtypeStruct((2, 1, 8, 4096), jnp.bfloat16),
        scratch_shapes=[
            pltpu.VMEM((COLS, 16, 2 * LANES), jnp.float32),
            pltpu.VMEM((2, 2, COLS, 8, LANES), jnp.float32),
        ],
        name="synthesis",
    )(opened, proto, tw_inverse, w_inverse)


def solution(mesh):
    placed = (P(None, "gx", "section", None), P(), P(), P(AXES))
    return jax.shard_map(
        body, mesh=mesh, in_specs=placed, out_specs=P(None, "gx", "section", None), check_vma=False
    )
```

```python
import functools
import math

import numpy as np
import jax
import jax.numpy as jnp
from jax import lax
from jax.experimental import pallas as pl
from jax.experimental.pallas import tpu as pltpu
from jax.sharding import PartitionSpec as P

TAPS = 4
LANES = 128
COLS = 32
AXES = ("section", "gx")
TURN_HIGH = 6.28125
TURN_LOW = 2.0 * math.pi - TURN_HIGH
SINE = [(-1.0) ** i / math.factorial(2 * i + 1) for i in range(7)]
COSINE = [(-1.0) ** i / math.factorial(2 * i) for i in range(8)]


def horner(coefficients, x):
    out = coefficients[-1]
    for value in reversed(coefficients[:-1]):
        out = out * x + value
    return out


def prototype_table():
    total = TAPS * COLS * LANES
    position = np.arange(total, dtype=np.float64) + 0.5
    window = 0.5 - 0.5 * np.cos(2.0 * np.pi / total * position)
    shaped = np.sinc((position - 0.5 * total) / (COLS * LANES)) * window
    return shaped.reshape(TAPS, COLS, LANES).astype(np.float32)


def lane_transform(sign, scale):
    l = np.arange(LANES)
    angle = 2.0 * np.pi * ((l[:, None] * l[None, :]) % LANES) / LANES
    c, s = np.cos(angle) * scale, sign * np.sin(angle) * scale
    return np.block([[c, s], [-s, c]])


def forward_columns():
    lane = np.arange(LANES)
    order = (lane // 16) + 8 * (lane % 16)
    table = lane_transform(-1.0, 1.0 / 64.0)
    return table[:, np.concatenate([order, LANES + order])]


def inverse_rows():
    table = lane_transform(1.0, 1.0 / 64.0)
    b, c, e = np.meshgrid(np.arange(8), np.arange(2), np.arange(16), indexing="ij")
    return table[(c * LANES + b + 8 * e).reshape(-1)]


def twiddle(re, im, k, n, sign):
    k = k % n
    if k == 0:
        return re, im
    if 4 * k == n:
        return (im, -re) if sign < 0 else (-im, re)
    if 8 * k == n:
        c = math.sqrt(0.5)
        return ((re + im) * c, (im - re) * c) if sign < 0 else ((re - im) * c, (im + re) * c)
    if 8 * k == 3 * n:
        c = math.sqrt(0.5)
        return ((im - re) * c, (-im - re) * c) if sign < 0 else ((-re - im) * c, (re - im) * c)
    c, s = math.cos(2 * math.pi * k / n), sign * math.sin(2 * math.pi * k / n)
    return re * c - im * s, re * s + im * c


def fft(values, sign):
    n = len(values)
    if n == 1:
        return values
    even = fft(values[0::2], sign)
    odd = fft(values[1::2], sign)
    low, high = [], []
    for k in range(n // 2):
        tr, ti = twiddle(odd[k][0], odd[k][1], k, n, sign)
        er, ei = even[k]
        low.append((er + tr, ei + ti))
        high.append((er - tr, ei - ti))
    return low + high


def filtered_rows(now, before, taps, period):
    row = lax.broadcasted_iota(jnp.int32, now.shape, 0) % period
    out = taps[0] * now
    for p in range(1, TAPS):
        out = out + taps[p] * pltpu.roll(jnp.where(row >= period - p, before, now), p, 0)
    return out


def analysis_kernel(late, x_ref, h_ref, proto_ref, tw_ref, w_ref, *rest):
    o_ref, z_ref, hist_ref = rest[-3:]
    row = lax.broadcasted_iota(jnp.int32, (8, LANES), 0)
    low = row < 4
    if not late:
        for c in range(2):
            for t in range(TAPS - 1):
                for j in range(COLS):
                    cut = slice(j * LANES, (j + 1) * LANES)
                    hist_ref[c, t, j] = h_ref[c, t, :, cut].astype(jnp.float32)

    def one_pair(m, _):
        values = []
        for j in range(COLS):
            cut = slice(j * LANES, (j + 1) * LANES)
            taps = [proto_ref[p, j : j + 1, :] for p in range(TAPS)]
            pair = []
            for c in range(2):
                first = x_ref[c, m, :, cut].astype(jnp.float32)
                second = x_ref[c, m + 8, :, cut].astype(jnp.float32)
                if late:
                    turned = pltpu.roll(first, 4, 0)
                    now = jnp.where(low, turned, second)
                    before = jnp.where(low, second, turned)
                else:
                    now = jnp.where(low, first, pltpu.roll(second, 4, 0))
                    before = hist_ref[c, 2, j, pl.ds(m, 1), :]
                    for t in (1, 0):
                        before = jnp.where(row == 5 + t, hist_ref[c, t, j, pl.ds(m, 1), :], before)
                    for t in (2, 1, 0):
                        before = jnp.where(
                            row == 1 + t, hist_ref[c, t, j, pl.ds(m + 8, 1), :], before
                        )
                pair.append(filtered_rows(now, before, taps, 4))
            values.append(tuple(pair))
        for a, (re, im) in enumerate(fft(values, -1.0)):
            cs = tw_ref[0, m, a : a + 1, :]
            sn = tw_ref[1, m, a : a + 1, :]
            z_ref[m, a, :, :LANES] = re * cs - im * sn
            z_ref[m, a, :, LANES:] = re * sn + im * cs
        return 0

    lax.fori_loop(0, 8, one_pair, 0)
    seg = lax.broadcasted_iota(jnp.int32, (1, 8, 2 * LANES), 2) % LANES // 16
    bits = [(seg // (1 << t)) % 2 == 1 for t in range(3)]

    def some_columns(i, _):
        a0 = i * 4
        z = z_ref[:, pl.ds(a0, 4)].reshape(8 * 4 * 8, 2 * LANES).astype(jnp.bfloat16)
        out = jnp.dot(z, w_ref[...], preferred_element_type=jnp.float32)
        out = out.reshape(8, 4, 8, 2 * LANES)
        v = [out[r] for r in range(8)]
        for t in range(3):
            mask = jnp.broadcast_to(bits[t], (4, 8, 2 * LANES))
            v = [jnp.where(mask, v[(r + (1 << t)) % 8], v[r]) for r in range(8)]
        for b in range(8):
            w = v[(-b) % 8].astype(jnp.bfloat16)
            for ai in range(4):
                a = a0 + ai
                dest = (a % 16) * 16 + 2 * b + a // 16
                for c in range(2):
                    o_ref[dest, 0, c] = w[ai, :, c * LANES : (c + 1) * LANES]
        return 0

    lax.fori_loop(0, 8, some_columns, 0)


def analysis(late, samples, hist, proto, tw, w, earlier):
    operands = [samples, hist, proto, tw, w]
    specs = [pl.BlockSpec(memory_space=pltpu.VMEM)] * 5
    extra = {}
    if earlier is not None:
        operands.append(earlier)
        specs = specs + [pl.BlockSpec(memory_space=pl.ANY)]
        extra = {"input_output_aliases": {5: 0}}
    half = 1 if late else 0
    return pl.pallas_call(
        functools.partial(analysis_kernel, late),
        grid=(1,),
        in_specs=specs,
        out_specs=pl.BlockSpec((256, 1, 2, 8, LANES), lambda i: (0, half, 0, 0, 0)),
        out_shape=jax.ShapeDtypeStruct((256, 2, 2, 8, LANES), jnp.bfloat16),
        scratch_shapes=[
            pltpu.VMEM((8, COLS, 8, 2 * LANES), jnp.float32),
            pltpu.VMEM((2, TAPS - 1, COLS, 16, LANES), jnp.float32),
        ],
        name="analysis_late" if late else "analysis_early",
        **extra,
    )(*operands)


def steer_kernel(b_ref, omega_ref, pos_ref, beam_ref, o_ref):
    e = pl.program_id(0)
    b = b_ref[0]
    lane = lax.broadcasted_iota(jnp.int32, (8, LANES), 1)
    inner = lane % 16

    def within(x, sh):
        return jnp.where(inner >= sh, pltpu.roll(x, sh, 1), pltpu.roll(x, sh + (LANES - 16), 1))

    coords = []
    for d in range(2):
        x = pltpu.roll(pos_ref[d], b * 16, 1)
        coords.append(jnp.where(lane // 16 < b, within(x, (e + 1) % 16), within(x, e)))
    omega = omega_ref[e]
    sin_b = jnp.broadcast_to(beam_ref[:, 0:1], (64, LANES))
    cos_b = jnp.broadcast_to(beam_ref[:, 1:2], (64, LANES))
    for i in range(8):
        phase = omega * (sin_b * coords[0][i : i + 1, :] + cos_b * coords[1][i : i + 1, :])
        turns = jnp.round(phase * (0.5 / math.pi))
        rest = (phase - turns * TURN_HIGH) - turns * TURN_LOW
        half = 0.5 * rest
        sq = half * half
        sn = half * horner(SINE, sq)
        cs = horner(COSINE, sq)
        col = slice(i * LANES, (i + 1) * LANES)
        far = slice(1024 + i * LANES, 1024 + (i + 1) * LANES)
        o_ref[0, :, col] = (1.0 - 2.0 * sn * sn).astype(jnp.bfloat16)
        o_ref[0, :, far] = (-2.0 * sn * cs).astype(jnp.bfloat16)


def beam_kernel(b_ref, lam_ref, r_ref, s_ref, y_ref, x_ref):
    step = pl.program_id(0)

    @pl.when(step < 4)
    def _():
        b = b_ref[0]
        lane = lax.broadcasted_iota(jnp.int32, (8, LANES), 1)
        low = lax.broadcasted_iota(jnp.int32, (8, LANES), 0) < 4
        shift = (lane % 16 - jnp.where(lane // 16 < b, 1, 0) + 16) % 16
        bits = [(shift // (1 << t)) % 2 == 1 for t in range(4)]

        def network(section, half, c):
            v = [r_ref[section, 0, g, half, c].astype(jnp.float32) for g in range(16)]
            for t in range(4):
                v = [jnp.where(bits[t], v[(r + (1 << t)) % 16], v[r]) for r in range(16)]
            return v

        def separate(pair, _):
            top = pl.ds(pl.multiple_of(pair * 16, 16), 16)
            bot = pl.ds(pl.multiple_of(32 + pair * 16, 16), 16)
            near = [pl.multiple_of(step * 256 + mh * LANES, LANES) for mh in range(2)]
            far = [pl.multiple_of(1024 + step * 256 + mh * LANES, LANES) for mh in range(2)]
            for c in range(2):
                tiles = [[None] * 16, [None] * 16]
                for one in range(2):
                    v0 = network(pair * 2 + one, 0, c)
                    v1 = network(pair * 2 + one, 1, c)
                    for r in range(16):
                        first = jnp.where(low, v0[r], pltpu.roll(v1[r], 4, 0))
                        second = jnp.where(low, pltpu.roll(v0[r], 4, 0), v1[r])
                        for mh, value in enumerate((first, second)):
                            if one == 0:
                                tiles[mh][r] = value
                            else:
                                tiles[mh][r] = jnp.concatenate([tiles[mh][r], value], axis=0)
                for mh in range(2):
                    for e in range(16):
                        w = tiles[mh][(-e) % 16]
                        w16 = w.astype(jnp.bfloat16)
                        if c == 0:
                            x_ref[e, top, pl.ds(near[mh], LANES)] = w16
                            x_ref[e, bot, pl.ds(far[mh], LANES)] = w16
                        else:
                            x_ref[e, top, pl.ds(far[mh], LANES)] = w16
                            x_ref[e, bot, pl.ds(near[mh], LANES)] = (-w).astype(jnp.bfloat16)
            return 0

        lax.fori_loop(0, 2, separate, 0)

    @pl.when(step >= 4)
    def _():
        total = 1024.0
        snapshots = 32.0
        sign = jnp.where(lax.broadcasted_iota(jnp.int32, (64, 64), 1) < 32, 1.0, -1.0)
        first = (step - 4) * 4
        dims = (((1,), (1,)), ((), ()))
        hs, gs = [], []
        for i in range(4):
            x = x_ref[first + i]
            both = jnp.concatenate([s_ref[i], x], axis=0)
            out = lax.dot_general(both, x, dims, preferred_element_type=jnp.float32)
            hs.append(out[:64])
            gs.append(out[64:])
        ghs = [
            jnp.dot(h, g, precision=lax.Precision.HIGHEST, preferred_element_type=jnp.float32)
            for h, g in zip(hs, gs)
        ]
        for i in range(4):
            h, gh = hs[i], ghs[i]
            lam = lam_ref[first + i]
            hh = jnp.sum(h * h, axis=1, keepdims=True)
            hgh = jnp.sum(h * gh, axis=1, keepdims=True)
            alpha = total / (hh / snapshots + lam * total)
            rho = 1.0 - alpha * lam
            t = alpha / snapshots
            new = rho * rho * total - 2.0 * rho * t * hh + t * t * hgh
            along = rho + new / total
            proj = along * h - t * gh
            size = along * along * total - 2.0 * along * t * hh + t * t * hgh
            curv = jnp.sum(proj * proj, axis=1, keepdims=True) / snapshots + lam * size
            alpha2 = new / curv
            main = alpha + alpha2 * along
            rest = alpha2 * t
            power = main * main * total - 2.0 * main * rest * hh + rest * rest * hgh
            norm = lax.rsqrt(power + total * 1e-6)
            y_ref[i] = (sign * ((norm * main) * h - (norm * rest) * gh)).astype(jnp.bfloat16)


def synthesis_kernel(t_ref, proto_ref, tw_ref, w_ref, o_ref, z_ref, s_ref):
    full = jnp.dot(t_ref[...], w_ref[...], preferred_element_type=jnp.float32)
    z_ref[...] = full.reshape(COLS, 16, 2 * LANES)

    def half(i, _):
        rows = pl.ds(pl.multiple_of(i * 8, 8), 8)
        values = []
        for a in range(COLS):
            re = z_ref[a, rows, :LANES]
            im = z_ref[a, rows, LANES:]
            cs = tw_ref[0, a : a + 1, :]
            sn = tw_ref[1, a : a + 1, :]
            values.append((re * cs - im * sn, re * sn + im * cs))
        for j, (re, im) in enumerate(fft(values, 1.0)):
            s_ref[0, i, j] = re.astype(jnp.bfloat16).astype(jnp.float32)
            s_ref[1, i, j] = im.astype(jnp.bfloat16).astype(jnp.float32)
        return 0

    lax.fori_loop(0, 2, half, 0)
    for c in range(2):
        for j in range(COLS):
            taps = [proto_ref[TAPS - 1 - p, j : j + 1, :] for p in range(TAPS)]
            out = filtered_rows(s_ref[c, 1, j], s_ref[c, 0, j], taps, 8)
            o_ref[c, 0, :, j * LANES : (j + 1) * LANES] = out.astype(jnp.bfloat16)


def body(samples, positions, beam_dir, load_exp):
    sections = lax.axis_size("section")
    groups = lax.axis_size("gx")
    device = lax.axis_index(AXES).astype(jnp.int32)
    place = device % groups
    own_b = (device % 16) // 2
    own_a = device // 16 + 16 * (device % 2)

    proto = jnp.asarray(prototype_table())
    w_forward = jnp.asarray(forward_columns(), jnp.bfloat16)
    w_inverse = jnp.asarray(inverse_rows(), jnp.bfloat16)

    hist = lax.ppermute(
        samples[:, :, 8 - (TAPS - 1) :, :].transpose(0, 2, 1, 3),
        "section",
        [(i, i + 1) for i in range(sections - 1)],
    )

    mu = jnp.arange(8, dtype=jnp.int32)[:, None, None]
    a_index = jnp.arange(COLS, dtype=jnp.int32)[None, :, None]
    l_index = jnp.arange(LANES, dtype=jnp.int32)[None, None, :]
    count = (a_index * l_index - 32 * (mu + 8 * (place % 16)) * l_index) & 4095
    angle = (2.0 * math.pi / 4096.0) * count.astype(jnp.float32)
    tw_forward = jnp.stack([jnp.cos(angle), -jnp.sin(angle)])
    n_angle = 2.0 * np.pi / 4096.0 * (np.arange(COLS)[:, None] * np.arange(LANES)[None, :])
    tw_inverse = jnp.asarray(np.stack([np.cos(n_angle), np.sin(n_angle)]), jnp.float32)

    message = analysis(True, samples, jnp.zeros((2, TAPS - 1, 16, LANES), jnp.bfloat16), proto, tw_forward, w_forward, None)
    message = analysis(False, samples, hist, proto, tw_forward, w_forward, message)

    message, positions, load_exp, beam_dir = lax.optimization_barrier(
        (message, positions, load_exp, beam_dir)
    )
    received = lax.all_to_all(message, AXES, 0, 0, tiled=True)

    exponents = load_exp.astype(jnp.float32)
    rows = [exponents]
    for t in range(1, 16):
        rows.append(lax.ppermute(exponents, AXES, [(i, i ^ (16 * t)) for i in range(256)]))
    own = device // 16
    slots = jnp.arange(16, dtype=jnp.int32)
    picked = jnp.sum(jnp.stack(rows) * (slots == own)[None, :], axis=1)
    mine = jnp.sum(jnp.where((slots ^ own)[:, None] == slots[None, :], picked[None, :], 0.0), axis=1)
    lam = jnp.exp2(mine)

    spread = positions.reshape(2, 4, 16, 2, 8).transpose(0, 1, 3, 4, 2).reshape(2, 8, LANES)
    channel = own_a + 32 * own_b + 256 * jnp.arange(16, dtype=jnp.int32)
    angular = 2.0 * math.pi * (0.75 + 0.5 * channel.astype(jnp.float32) / 4096)
    beams = beam_dir.shape[0]
    angle_beam = math.pi / beams * (beam_dir.astype(jnp.float32) + 0.5) - 0.5 * math.pi
    directions = jnp.stack([jnp.sin(angle_beam), jnp.cos(angle_beam)], axis=1)
    steer = pl.pallas_call(
        steer_kernel,
        grid=(16,),
        in_specs=[
            pl.BlockSpec(memory_space=pltpu.SMEM),
            pl.BlockSpec(memory_space=pltpu.SMEM),
            pl.BlockSpec((2, 8, LANES), lambda e: (0, 0, 0)),
            pl.BlockSpec((beams, 2), lambda e: (0, 0)),
        ],
        out_specs=pl.BlockSpec((1, beams, 2048), lambda e: (e, 0, 0)),
        out_shape=jax.ShapeDtypeStruct((16, beams, 2048), jnp.bfloat16),
        name="steer",
    )(own_b[None], angular, spread, directions)

    formed = pl.pallas_call(
        beam_kernel,
        grid=(8,),
        in_specs=[
            pl.BlockSpec(memory_space=pltpu.SMEM),
            pl.BlockSpec(memory_space=pltpu.SMEM),
            pl.BlockSpec((4, 1, 16, 2, 2, 8, LANES), lambda i: (0, jnp.minimum(i, 3), 0, 0, 0, 0, 0)),
            pl.BlockSpec((4, beams, 2048), lambda i: (jnp.maximum(i - 4, 0), 0, 0)),
        ],
        out_specs=pl.BlockSpec((4, beams, 64), lambda i: (jnp.maximum(i - 4, 0), 0, 0)),
        out_shape=jax.ShapeDtypeStruct((16, beams, 64), jnp.bfloat16),
        scratch_shapes=[pltpu.VMEM((16, 64, 2048), jnp.bfloat16)],
        name="beams",
    )(own_b[None], lam, received.reshape(4, 4, 16, 2, 2, 8, LANES), steer)

    padded = jnp.pad(formed.reshape(16, beams, 2, 32), ((0, 0), (0, 0), (0, 0), (8, 0)))
    windows = jnp.stack([padded[..., 8 * s : 8 * s + 16] for s in range(sections)])
    back = windows.transpose(0, 2, 4, 3, 1).reshape(sections * groups, 4, LANES)
    returned = lax.all_to_all(back, AXES, 0, 0, tiled=True)
    opened = returned.reshape(16, 8, 2, 16, 32).transpose(2, 0, 3, 1, 4).reshape(COLS * 16, 256)

    return pl.pallas_call(
        synthesis_kernel,
        in_specs=[pl.BlockSpec(memory_space=pltpu.VMEM)] * 4,
        out_specs=pl.BlockSpec(memory_space=pltpu.VMEM),
        out_shape=jax.ShapeDtypeStruct((2, 1, 8, 4096), jnp.bfloat16),
        scratch_shapes=[
            pltpu.VMEM((COLS, 16, 2 * LANES), jnp.float32),
            pltpu.VMEM((2, 2, COLS, 8, LANES), jnp.float32),
        ],
        name="synthesis",
    )(opened, proto, tw_inverse, w_inverse)


def solution(mesh):
    placed = (P(None, "gx", "section", None), P(), P(), P(AXES))
    return jax.shard_map(
        body, mesh=mesh, in_specs=placed, out_specs=P(None, "gx", "section", None), check_vma=False
    )
```

```python
import functools
import math

import numpy as np
import jax
import jax.numpy as jnp
from jax import lax
from jax.experimental import pallas as pl
from jax.experimental.pallas import tpu as pltpu
from jax.sharding import PartitionSpec as P

TAPS = 4
LANES = 128
COLS = 32
AXES = ("section", "gx")
TURN_HIGH = 6.28125
TURN_LOW = 2.0 * math.pi - TURN_HIGH
SINE = [(-1.0) ** i / math.factorial(2 * i + 1) for i in range(6)]
COSINE = [(-1.0) ** i / math.factorial(2 * i) for i in range(7)]


def horner(coefficients, x):
    out = coefficients[-1]
    for value in reversed(coefficients[:-1]):
        out = out * x + value
    return out


def prototype_table():
    total = TAPS * COLS * LANES
    position = np.arange(total, dtype=np.float64) + 0.5
    window = 0.5 - 0.5 * np.cos(2.0 * np.pi / total * position)
    shaped = np.sinc((position - 0.5 * total) / (COLS * LANES)) * window
    return shaped.reshape(TAPS, COLS, LANES).astype(np.float32)


def lane_transform(sign, scale):
    l = np.arange(LANES)
    angle = 2.0 * np.pi * ((l[:, None] * l[None, :]) % LANES) / LANES
    c, s = np.cos(angle) * scale, sign * np.sin(angle) * scale
    return np.block([[c, s], [-s, c]])


def forward_columns():
    lane = np.arange(LANES)
    order = (lane // 16) + 8 * (lane % 16)
    table = lane_transform(-1.0, 1.0 / 64.0)
    return table[:, np.concatenate([order, LANES + order])]


def swap_bits(v, distance):
    lane = lax.broadcasted_iota(jnp.int32, v[0].shape, len(v[0].shape) - 1)
    for t in range(3):
        step = distance << t
        mask = (lane // step) % 2 == 1
        out = list(v)
        for low in range(8):
            if low & (1 << t):
                continue
            high = low | (1 << t)
            out[low] = jnp.where(mask, pltpu.roll(v[high], step, 1), v[low])
            out[high] = jnp.where(mask, v[high], pltpu.roll(v[low], LANES - step, 1))
        v = out
    return v


def twiddle(re, im, k, n, sign):
    k = k % n
    if k == 0:
        return re, im
    if 4 * k == n:
        return (im, -re) if sign < 0 else (-im, re)
    if 8 * k == n:
        c = math.sqrt(0.5)
        return ((re + im) * c, (im - re) * c) if sign < 0 else ((re - im) * c, (im + re) * c)
    if 8 * k == 3 * n:
        c = math.sqrt(0.5)
        return ((im - re) * c, (-im - re) * c) if sign < 0 else ((-re - im) * c, (re - im) * c)
    c, s = math.cos(2 * math.pi * k / n), sign * math.sin(2 * math.pi * k / n)
    return re * c - im * s, re * s + im * c


def fft(values, sign):
    n = len(values)
    if n == 1:
        return values
    even = fft(values[0::2], sign)
    odd = fft(values[1::2], sign)
    low, high = [], []
    for k in range(n // 2):
        tr, ti = twiddle(odd[k][0], odd[k][1], k, n, sign)
        er, ei = even[k]
        low.append((er + tr, ei + ti))
        high.append((er - tr, ei - ti))
    return low + high


def filtered_rows(now, before, taps, period):
    row = lax.broadcasted_iota(jnp.int32, now.shape, 0) % period
    out = taps[0] * now
    for p in range(1, TAPS):
        out = out + taps[p] * pltpu.roll(jnp.where(row >= period - p, before, now), p, 0)
    return out


def analysis_kernel(late, x_ref, proto_ref, tw_ref, w_ref, *rest):
    if late:
        o_ref, z_ref = rest
    else:
        h_ref, _, o_ref, z_ref, hist_ref = rest
    row = lax.broadcasted_iota(jnp.int32, (8, LANES), 0)
    low = row < 4
    if not late:
        for c in range(2):
            for t in range(TAPS - 1):
                for j in range(COLS):
                    cut = slice(j * LANES, (j + 1) * LANES)
                    hist_ref[c, t, j] = h_ref[c, t, :, cut].astype(jnp.float32)

    def one_pair(m, _):
        values = []
        for j in range(COLS):
            cut = slice(j * LANES, (j + 1) * LANES)
            taps = [proto_ref[p, j : j + 1, :] for p in range(TAPS)]
            pair = []
            for c in range(2):
                first = x_ref[c, m, :, cut].astype(jnp.float32)
                second = x_ref[c, m + 8, :, cut].astype(jnp.float32)
                if late:
                    turned = pltpu.roll(first, 4, 0)
                    now = jnp.where(low, turned, second)
                    before = jnp.where(low, second, turned)
                else:
                    now = jnp.where(low, first, pltpu.roll(second, 4, 0))
                    before = hist_ref[c, 2, j, pl.ds(m, 1), :]
                    for t in (1, 0):
                        before = jnp.where(row == 5 + t, hist_ref[c, t, j, pl.ds(m, 1), :], before)
                    for t in (2, 1, 0):
                        before = jnp.where(
                            row == 1 + t, hist_ref[c, t, j, pl.ds(m + 8, 1), :], before
                        )
                pair.append(filtered_rows(now, before, taps, 4))
            values.append(tuple(pair))
        for a, (re, im) in enumerate(fft(values, -1.0)):
            cs = tw_ref[0, m, a : a + 1, :]
            sn = tw_ref[1, m, a : a + 1, :]
            z_ref[m, a, :, :LANES] = re * cs - im * sn
            z_ref[m, a, :, LANES:] = re * sn + im * cs
        return 0

    lax.fori_loop(0, 8, one_pair, 0)
    seg = lax.broadcasted_iota(jnp.int32, (1, 8, 2 * LANES), 2) % LANES // 16
    bits = [(seg // (1 << t)) % 2 == 1 for t in range(3)]

    def some_columns(i, _):
        a0 = i * 4
        z = z_ref[:, pl.ds(a0, 4)].reshape(8 * 4 * 8, 2 * LANES).astype(jnp.bfloat16)
        out = jnp.dot(z, w_ref[...], preferred_element_type=jnp.float32)
        out = out.reshape(8, 4, 8, 2 * LANES)
        v = [out[r] for r in range(8)]
        for t in range(3):
            mask = jnp.broadcast_to(bits[t], (4, 8, 2 * LANES))
            v = [jnp.where(mask, v[(r + (1 << t)) % 8], v[r]) for r in range(8)]
        for b in range(8):
            w = v[(-b) % 8].astype(jnp.bfloat16)
            for ai in range(4):
                a = a0 + ai
                dest = (a % 16) * 16 + 2 * b + a // 16
                for c in range(2):
                    o_ref[dest, 0, c] = w[ai, :, c * LANES : (c + 1) * LANES]
        return 0

    lax.fori_loop(0, 8, some_columns, 0)


def analysis(samples, proto, tw, w, hist=None, earlier=None):
    late = hist is None
    half = 1 if late else 0
    operands = [samples, proto, tw, w]
    scratch = [pltpu.VMEM((8, COLS, 8, 2 * LANES), jnp.float32)]
    specs = [pl.BlockSpec(memory_space=pltpu.VMEM)] * 4
    aliases = {}
    if not late:
        operands += [hist, earlier]
        specs += [pl.BlockSpec(memory_space=pltpu.VMEM), pl.BlockSpec(memory_space=pl.ANY)]
        scratch.append(pltpu.VMEM((2, TAPS - 1, COLS, 16, LANES), jnp.float32))
        aliases = {5: 0}
    return pl.pallas_call(
        functools.partial(analysis_kernel, late),
        grid=(1,),
        in_specs=specs,
        out_specs=pl.BlockSpec((256, 1, 2, 8, LANES), lambda i: (0, half, 0, 0, 0)),
        out_shape=jax.ShapeDtypeStruct((256, 2, 2, 8, LANES), jnp.bfloat16),
        scratch_shapes=scratch,
        input_output_aliases=aliases,
        name="analysis_late" if late else "analysis_early",
    )(*operands)


def steer_kernel(b_ref, omega_ref, pos_ref, beam_ref, o_ref):
    e = pl.program_id(0)
    b = b_ref[0]
    lane = lax.broadcasted_iota(jnp.int32, (8, LANES), 1)
    inner = lane % 16

    def within(x, sh):
        return jnp.where(inner >= sh, pltpu.roll(x, sh, 1), pltpu.roll(x, sh + (LANES - 16), 1))

    coords = []
    for d in range(2):
        x = pltpu.roll(pos_ref[d], b * 16, 1)
        coords.append(jnp.where(lane // 16 < b, within(x, (e + 1) % 16), within(x, e)))
    omega = omega_ref[e]
    sin_b = jnp.broadcast_to(beam_ref[:, 0:1], (64, LANES))
    cos_b = jnp.broadcast_to(beam_ref[:, 1:2], (64, LANES))
    for i in range(8):
        phase = omega * (sin_b * coords[0][i : i + 1, :] + cos_b * coords[1][i : i + 1, :])
        turns = jnp.round(phase * (0.5 / math.pi))
        rest = (phase - turns * TURN_HIGH) - turns * TURN_LOW
        half = 0.5 * rest
        sq = half * half
        sn = half * horner(SINE, sq)
        cs = horner(COSINE, sq)
        col = slice(i * LANES, (i + 1) * LANES)
        far = slice(1024 + i * LANES, 1024 + (i + 1) * LANES)
        o_ref[0, :, col] = (1.0 - 2.0 * sn * sn).astype(jnp.bfloat16)
        o_ref[0, :, far] = (-2.0 * sn * cs).astype(jnp.bfloat16)


def beam_kernel(b_ref, lam_ref, r_ref, s_ref, o_ref, x_ref, y_ref, m_ref):
    step = pl.program_id(0)

    @pl.when(step < 4)
    def _():
        b = b_ref[0]
        lane = lax.broadcasted_iota(jnp.int32, (8, LANES), 1)
        low = lax.broadcasted_iota(jnp.int32, (8, LANES), 0) < 4
        shift = (lane % 16 - jnp.where(lane // 16 < b, 1, 0) + 16) % 16
        bits = [(shift // (1 << t)) % 2 == 1 for t in range(4)]

        def network(section, half, c):
            v = [r_ref[section, step, g, half, c].astype(jnp.float32) for g in range(16)]
            for t in range(4):
                v = [jnp.where(bits[t], v[(r + (1 << t)) % 16], v[r]) for r in range(16)]
            return v

        def separate(pair, _):
            top = pl.ds(pl.multiple_of(pair * 16, 16), 16)
            bot = pl.ds(pl.multiple_of(32 + pair * 16, 16), 16)
            near = [pl.multiple_of(step * 256 + mh * LANES, LANES) for mh in range(2)]
            far = [pl.multiple_of(1024 + step * 256 + mh * LANES, LANES) for mh in range(2)]
            for c in range(2):
                tiles = [[None] * 16, [None] * 16]
                for one in range(2):
                    v0 = network(pair * 2 + one, 0, c)
                    v1 = network(pair * 2 + one, 1, c)
                    for r in range(16):
                        first = jnp.where(low, v0[r], pltpu.roll(v1[r], 4, 0))
                        second = jnp.where(low, pltpu.roll(v0[r], 4, 0), v1[r])
                        for mh, value in enumerate((first, second)):
                            if one == 0:
                                tiles[mh][r] = value
                            else:
                                tiles[mh][r] = jnp.concatenate([tiles[mh][r], value], axis=0)
                for mh in range(2):
                    for e in range(16):
                        w = tiles[mh][(-e) % 16]
                        w16 = w.astype(jnp.bfloat16)
                        if c == 0:
                            x_ref[e, top, pl.ds(near[mh], LANES)] = w16
                            x_ref[e, bot, pl.ds(far[mh], LANES)] = w16
                        else:
                            x_ref[e, top, pl.ds(far[mh], LANES)] = w16
                            x_ref[e, bot, pl.ds(near[mh], LANES)] = (-w).astype(jnp.bfloat16)
            return 0

        lax.fori_loop(0, 2, separate, 0)

    @pl.when(step >= 4)
    def _():
        total = 1024.0
        snapshots = 32.0
        sign = jnp.where(lax.broadcasted_iota(jnp.int32, (64, 64), 1) < 32, 1.0, -1.0)
        first = (step - 4) * 2
        order = [0, 1, 8, 9]
        ys = []
        dims = (((1,), (1,)), ((), ()))
        hs, gs = [], []
        for i in range(4):
            x = x_ref[first + order[i]]
            both = jnp.concatenate([s_ref[i], x], axis=0)
            out = lax.dot_general(both, x, dims, preferred_element_type=jnp.float32)
            hs.append(out[:64])
            gs.append(out[64:])
        ghs = [
            jnp.dot(h, g, precision=lax.Precision.HIGHEST, preferred_element_type=jnp.float32)
            for h, g in zip(hs, gs)
        ]
        for i in range(4):
            h, gh = hs[i], ghs[i]
            lam = lam_ref[first + order[i]]
            hh = jnp.sum(h * h, axis=1, keepdims=True)
            hgh = jnp.sum(h * gh, axis=1, keepdims=True)
            alpha = total / (hh / snapshots + lam * total)
            rho = 1.0 - alpha * lam
            t = alpha / snapshots
            new = rho * rho * total - 2.0 * rho * t * hh + t * t * hgh
            along = rho + new / total
            proj = along * h - t * gh
            size = along * along * total - 2.0 * along * t * hh + t * t * hgh
            curv = jnp.sum(proj * proj, axis=1, keepdims=True) / snapshots + lam * size
            alpha2 = new / curv
            main = alpha + alpha2 * along
            rest = alpha2 * t
            power = main * main * total - 2.0 * main * rest * hh + rest * rest * hgh
            norm = lax.rsqrt(power + total * 1e-6)
            ys.append(sign * ((norm * main) * h - (norm * rest) * gh))
        for i in range(2):
            y_ref[first + i] = jnp.concatenate([ys[i], ys[i + 2]], axis=1)

    @pl.when(step == 7)
    def _():
        v = swap_bits([y_ref[r] for r in range(8)], 8)
        near = lax.broadcasted_iota(jnp.int32, (64, LANES), 1) % 8 < 4
        for section in range(4):
            rows = [v[section], v[4 + section]]
            if section:
                rows.append(
                    jnp.where(near, pltpu.roll(v[section - 1], LANES - 4, 1), v[4 + section - 1])
                )
            else:
                rows.append(jnp.zeros((64, LANES), jnp.float32))
            rows.append(jnp.zeros((64, LANES), jnp.float32))
            for r in range(4):
                m_ref[pl.ds(section * 256 + r, 64, stride=4), :] = rows[r]
        o_ref[...] = m_ref[...].astype(jnp.bfloat16)


def synthesis_kernel(m_ref, proto_ref, tw_ref, w_ref, o_ref, r_ref, l_ref, z_ref, s_ref):
    r_ref[...] = m_ref[...].astype(jnp.float32)
    for a_hi in range(2):
        tiles = []
        for r in range(3):
            groups = []
            for group in range(2):
                v = [
                    r_ref[pl.ds((group * 128 + 2 * b + a_hi) * 4 + r, 8, stride=64), :]
                    for b in range(8)
                ]
                groups.append(swap_bits(v, 1))
            tiles.append(
                [jnp.concatenate([groups[0][k], groups[1][k]], axis=0) for k in range(8)]
            )
        for k in range(8):
            rows = slice(k * COLS + a_hi * 16, k * COLS + a_hi * 16 + 16)
            l_ref[rows, :LANES] = tiles[0][k].astype(jnp.bfloat16)
            l_ref[rows, LANES:] = tiles[1][k].astype(jnp.bfloat16)
        for k in range(4):
            rows = slice((8 + k) * COLS + a_hi * 16, (8 + k) * COLS + a_hi * 16 + 16)
            l_ref[rows, :LANES] = tiles[2][k].astype(jnp.bfloat16)
            l_ref[rows, LANES:] = tiles[2][4 + k].astype(jnp.bfloat16)
    full = jnp.dot(l_ref[...], w_ref[...], preferred_element_type=jnp.float32)
    for c in range(2):
        cut = slice(c * LANES, (c + 1) * LANES)
        z_ref[c, : 8 * COLS] = full[: 8 * COLS, cut]
        z_ref[c, 8 * COLS : 12 * COLS] = jnp.zeros((4 * COLS, LANES), jnp.float32)
        z_ref[c, 12 * COLS :] = full[8 * COLS :, cut]

    def half(i, _):
        values = []
        for a in range(COLS):
            rows = pl.ds(i * (8 * COLS) + a, 8, stride=COLS)
            re = z_ref[0, rows, :]
            im = z_ref[1, rows, :]
            cs = tw_ref[0, a : a + 1, :]
            sn = tw_ref[1, a : a + 1, :]
            values.append((re * cs - im * sn, re * sn + im * cs))
        for j, (re, im) in enumerate(fft(values, 1.0)):
            s_ref[0, i, j] = re.astype(jnp.bfloat16).astype(jnp.float32)
            s_ref[1, i, j] = im.astype(jnp.bfloat16).astype(jnp.float32)
        return 0

    for i in range(2):
        half(i, 0)
    for c in range(2):
        for j in range(COLS):
            taps = [proto_ref[TAPS - 1 - p, j : j + 1, :] for p in range(TAPS)]
            out = filtered_rows(s_ref[c, 0, j], s_ref[c, 1, j], taps, 8)
            o_ref[c, 0, :, j * LANES : (j + 1) * LANES] = out.astype(jnp.bfloat16)


def body(samples, positions, beam_dir, load_exp):
    sections = lax.axis_size("section")
    groups = lax.axis_size("gx")
    device = lax.axis_index(AXES).astype(jnp.int32)
    place = device % groups
    own_b = (device % 16) // 2
    own_a = device // 16 + 16 * (device % 2)

    proto = jnp.asarray(prototype_table())
    w_forward = jnp.asarray(forward_columns(), jnp.bfloat16)
    w_inverse = jnp.asarray(lane_transform(1.0, 1.0 / 64.0), jnp.bfloat16)

    last = samples[:, :, 8 - (TAPS - 1) :, :].transpose(0, 2, 1, 3)
    last, load_exp = lax.optimization_barrier((last, load_exp))
    hist = lax.ppermute(last, "section", [(i, i + 1) for i in range(sections - 1)])

    mu = jnp.arange(8, dtype=jnp.int32)[:, None, None]
    a_index = jnp.arange(COLS, dtype=jnp.int32)[None, :, None]
    l_index = jnp.arange(LANES, dtype=jnp.int32)[None, None, :]
    count = (a_index * l_index - 32 * (mu + 8 * (place % 16)) * l_index) & 4095
    angle = (2.0 * math.pi / 4096.0) * count.astype(jnp.float32)
    tw_forward = jnp.stack([jnp.cos(angle), -jnp.sin(angle)])
    n_angle = 2.0 * np.pi / 4096.0 * (np.arange(COLS)[:, None] * np.arange(LANES)[None, :])
    tw_inverse = jnp.asarray(np.stack([np.cos(n_angle), np.sin(n_angle)]), jnp.float32)

    devices = sections * groups
    exponents = load_exp.astype(jnp.float32)
    level = [exponents]
    for t in range(1, 4):
        level.append(lax.ppermute(exponents, AXES, [(i, i ^ (16 * t)) for i in range(devices)]))
    level = jnp.stack(level)

    samples = pltpu.with_memory_space_constraint(samples, pltpu.VMEM)
    hist = pltpu.with_memory_space_constraint(hist, pltpu.VMEM)
    message = analysis(samples, proto, tw_forward, w_forward)
    message, level = lax.optimization_barrier((message, level))
    message = analysis(samples, proto, tw_forward, w_forward, hist, message)

    message, positions, level, beam_dir = lax.optimization_barrier(
        (message, positions, level, beam_dir)
    )
    received = lax.all_to_all(message, AXES, 0, 0, tiled=True)

    rows = [level]
    for t in range(1, sections):
        rows.append(lax.ppermute(level, AXES, [(i, i ^ (groups * t)) for i in range(devices)]))
    own = device // 16
    slots = jnp.arange(16, dtype=jnp.int32)
    picked = jnp.sum(jnp.concatenate(rows) * (slots == own)[None, :], axis=1)
    mine = jnp.sum(jnp.where((slots ^ own)[:, None] == slots[None, :], picked[None, :], 0.0), axis=1)
    lam = jnp.exp2(mine)

    spread = positions.reshape(2, 4, 16, 2, 8).transpose(0, 1, 3, 4, 2).reshape(2, 8, LANES)
    channel = own_a + 32 * own_b + 256 * jnp.arange(16, dtype=jnp.int32)
    angular = 2.0 * math.pi * (0.75 + 0.5 * channel.astype(jnp.float32) / 4096)
    beams = beam_dir.shape[0]
    angle_beam = math.pi / beams * (beam_dir.astype(jnp.float32) + 0.5) - 0.5 * math.pi
    directions = jnp.stack([jnp.sin(angle_beam), jnp.cos(angle_beam)], axis=1)
    steer = pl.pallas_call(
        steer_kernel,
        grid=(16,),
        in_specs=[
            pl.BlockSpec(memory_space=pltpu.SMEM),
            pl.BlockSpec(memory_space=pltpu.SMEM),
            pl.BlockSpec((2, 8, LANES), lambda e: (0, 0, 0)),
            pl.BlockSpec((beams, 2), lambda e: (0, 0)),
        ],
        out_specs=pl.BlockSpec(
            (1, beams, 2048), lambda e: (4 * ((e % 8) // 2) + e % 2 + 2 * (e // 8), 0, 0)
        ),
        out_shape=jax.ShapeDtypeStruct((16, beams, 2048), jnp.bfloat16),
        name="steer",
    )(own_b[None], angular, spread, directions)

    received = pltpu.with_memory_space_constraint(
        received.reshape(4, 4, 16, 2, 2, 8, LANES), pltpu.VMEM
    )
    back = pl.pallas_call(
        beam_kernel,
        grid=(8,),
        in_specs=[
            pl.BlockSpec(memory_space=pltpu.SMEM),
            pl.BlockSpec(memory_space=pltpu.SMEM),
            pl.BlockSpec(memory_space=pltpu.VMEM),
            pl.BlockSpec((4, beams, 2048), lambda i: (jnp.maximum(i - 4, 0), 0, 0)),
        ],
        out_specs=pl.BlockSpec((4 * devices, LANES), lambda i: (0, 0)),
        out_shape=jax.ShapeDtypeStruct((4 * devices, LANES), jnp.bfloat16),
        scratch_shapes=[
            pltpu.VMEM((16, 64, 2048), jnp.bfloat16),
            pltpu.VMEM((8, beams, LANES), jnp.float32),
            pltpu.VMEM((4 * devices, LANES), jnp.float32),
        ],
        name="beams",
    )(own_b[None], lam, received, steer)

    returned = lax.all_to_all(back.reshape(devices, 4, LANES), AXES, 0, 0, tiled=True)
    return pl.pallas_call(
        synthesis_kernel,
        in_specs=[pl.BlockSpec(memory_space=pltpu.VMEM)] * 4,
        out_specs=pl.BlockSpec(memory_space=pltpu.VMEM),
        out_shape=jax.ShapeDtypeStruct((2, 1, 8, 4096), jnp.bfloat16),
        scratch_shapes=[
            pltpu.VMEM((4 * devices, LANES), jnp.float32),
            pltpu.VMEM((12 * COLS, 2 * LANES), jnp.bfloat16),
            pltpu.VMEM((2, 16 * COLS, LANES), jnp.float32),
            pltpu.VMEM((2, 2, COLS, 8, LANES), jnp.float32),
        ],
        name="synthesis",
    )(returned.reshape(4 * devices, LANES), proto, tw_inverse, w_inverse)


def solution(mesh):
    placed = (P(None, "gx", "section", None), P(), P(), P(AXES))
    return jax.shard_map(
        body, mesh=mesh, in_specs=placed, out_specs=P(None, "gx", "section", None), check_vma=False
    )
```

```python
import functools
import math

import numpy as np
import jax
import jax.numpy as jnp
from jax import lax
from jax.experimental import pallas as pl
from jax.experimental.pallas import tpu as pltpu
from jax.sharding import PartitionSpec as P

TAPS = 4
LANES = 128
COLS = 32
AXES = ("section", "gx")
VMEM_LIMIT = 32 << 20
SINE = [(-1.0) ** i * math.pi ** (2 * i + 1) / math.factorial(2 * i + 1) for i in range(6)]
COSINE = [(-1.0) ** i * math.pi ** (2 * i) / math.factorial(2 * i) for i in range(6)]


def horner(coefficients, x):
    out = coefficients[-1]
    for value in reversed(coefficients[:-1]):
        out = out * x + value
    return out


def prototype_table():
    total = TAPS * COLS * LANES
    position = np.arange(total, dtype=np.float64) + 0.5
    window = 0.5 - 0.5 * np.cos(2.0 * np.pi / total * position)
    shaped = np.sinc((position - 0.5 * total) / (COLS * LANES)) * window
    return shaped.reshape(TAPS, COLS, LANES).astype(np.float32)


def lane_transform(sign, scale):
    l = np.arange(LANES)
    angle = 2.0 * np.pi * ((l[:, None] * l[None, :]) % LANES) / LANES
    c, s = np.cos(angle) * scale, sign * np.sin(angle) * scale
    return np.block([[c, s], [-s, c]])


def forward_columns():
    lane = np.arange(LANES)
    order = (lane // 16) + 8 * (lane % 16)
    table = lane_transform(-1.0, 1.0 / 64.0)
    return table[:, np.concatenate([order, LANES + order])]


def swap_bits(v, distance):
    lane = lax.broadcasted_iota(jnp.int32, v[0].shape, len(v[0].shape) - 1)
    for t in range(3):
        step = distance << t
        mask = (lane // step) % 2 == 1
        out = list(v)
        for low in range(8):
            if low & (1 << t):
                continue
            high = low | (1 << t)
            out[low] = jnp.where(mask, pltpu.roll(v[high], step, 1), v[low])
            out[high] = jnp.where(mask, v[high], pltpu.roll(v[low], LANES - step, 1))
        v = out
    return v


def twiddle(re, im, k, n, sign):
    k = k % n
    if k == 0:
        return re, im
    if 4 * k == n:
        return (im, -re) if sign < 0 else (-im, re)
    if 8 * k == n:
        c = math.sqrt(0.5)
        return ((re + im) * c, (im - re) * c) if sign < 0 else ((re - im) * c, (im + re) * c)
    if 8 * k == 3 * n:
        c = math.sqrt(0.5)
        return ((im - re) * c, (-im - re) * c) if sign < 0 else ((-re - im) * c, (re - im) * c)
    c, s = math.cos(2 * math.pi * k / n), sign * math.sin(2 * math.pi * k / n)
    return re * c - im * s, re * s + im * c


def fft(values, sign):
    n = len(values)
    if n == 1:
        return values
    even = fft(values[0::2], sign)
    odd = fft(values[1::2], sign)
    low, high = [], []
    for k in range(n // 2):
        tr, ti = twiddle(odd[k][0], odd[k][1], k, n, sign)
        er, ei = even[k]
        low.append((er + tr, ei + ti))
        high.append((er - tr, ei - ti))
    return low + high


def filtered_rows(now, before, taps, period):
    row = lax.broadcasted_iota(jnp.int32, now.shape, 0) % period
    out = taps[0] * now
    for p in range(1, TAPS):
        out = out + taps[p] * pltpu.roll(jnp.where(row >= period - p, before, now), p, 0)
    return out


def unpack_kernel(place_ref, x_ref, xs_ref, h_ref):
    i = pl.program_id(0)
    for j in range(8):
        for c in range(2):
            for m in range(16):
                value = x_ref[c, m, :, j * LANES : (j + 1) * LANES]
                xs_ref[c, i * 8 + j, m * 8 : m * 8 + 8, :] = value.astype(jnp.float32)
            for t in range(TAPS - 1):
                value = xs_ref[c, i * 8 + j, pl.ds(8 - (TAPS - 1) + t, 16, stride=8), :]
                cut = pl.ds(pl.multiple_of(i * 1024 + j * LANES, LANES), LANES)
                h_ref[c, t, :, cut] = value.astype(jnp.bfloat16)


def unpack(place, samples):
    return pl.pallas_call(
        unpack_kernel,
        grid=(4,),
        in_specs=[
            pl.BlockSpec(memory_space=pltpu.SMEM),
            pl.BlockSpec((2, 16, 8, 1024), lambda i: (0, 0, 0, i)),
        ],
        out_specs=[pl.BlockSpec(memory_space=pltpu.VMEM)] * 2,
        out_shape=[
            pltpu.VMEM((2, COLS, 128, LANES), jnp.float32),
            pltpu.VMEM((2, TAPS - 1, 16, COLS * LANES), jnp.bfloat16),
        ],
        name="unpack",
        compiler_params=pltpu.CompilerParams(vmem_limit_bytes=VMEM_LIMIT),
    )(place, samples)


def analysis_kernel(late, place_ref, x_ref, proto_ref, turn_ref, shift_ref, w_ref, *rest):
    if late:
        o_ref, z_ref, tw_ref = rest
    else:
        h_ref, _, o_ref, z_ref, tw_ref, hist_ref = rest
        for c in range(2):
            for t in range(TAPS - 1):
                for j in range(COLS):
                    cut = slice(j * LANES, (j + 1) * LANES)
                    hist_ref[c, t, j] = h_ref[c, t, :, cut].astype(jnp.float32)

    def block(c, j, mh, k):
        if k < 0:
            return hist_ref[c, TAPS - 1 + k, j, mh * 8 : mh * 8 + 8, :]
        return x_ref[c, j, pl.ds(mh * 64 + k, 8, stride=8), :]

    shifts = pl.ds(pl.multiple_of(place_ref[0] * 8, 8), 8)
    shift_re, shift_im = shift_ref[0, shifts, :], shift_ref[1, shifts, :]
    for a in range(COLS):
        cs, sn = turn_ref[0, a : a + 1, :], turn_ref[1, a : a + 1, :]
        tw_ref[0, a] = shift_re * cs - shift_im * sn
        tw_ref[1, a] = shift_re * sn + shift_im * cs

    for i in range(8):
        mh = i // 4
        k = i % 4 + (4 if late else 0)
        values = []
        for j in range(COLS):
            taps = [proto_ref[p, j : j + 1, :] for p in range(TAPS)]
            pair = []
            for c in range(2):
                out = taps[0] * block(c, j, mh, k)
                for p in range(1, TAPS):
                    out = out + taps[p] * block(c, j, mh, k - p)
                pair.append(out)
            values.append(tuple(pair))
        for a, (re, im) in enumerate(fft(values, -1.0)):
            cs = tw_ref[0, a]
            sn = tw_ref[1, a]
            z_ref[0, a, i * 8 : i * 8 + 8, :] = re * cs - im * sn
            z_ref[1, a, i * 8 : i * 8 + 8, :] = re * sn + im * cs

    seg = lax.broadcasted_iota(jnp.int32, (1, 8, 2 * LANES), 2) % LANES // 16
    bits = [(seg // (1 << t)) % 2 == 1 for t in range(3)]

    def some_columns(i, _):
        a0 = i * 4
        parts = []
        for c in range(2):
            rows = [
                z_ref[c, a0 + ai, pl.ds(mu, 8, stride=8), :] for mu in range(8) for ai in range(4)
            ]
            parts.append(jnp.concatenate(rows, axis=0).astype(jnp.bfloat16))
        z = jnp.concatenate(parts, axis=1)
        out = jnp.dot(z, w_ref[...], preferred_element_type=jnp.float32)
        out = out.reshape(8, 4, 8, 2 * LANES)
        v = [out[r] for r in range(8)]
        for t in range(3):
            mask = jnp.broadcast_to(bits[t], (4, 8, 2 * LANES))
            v = [jnp.where(mask, v[(r + (1 << t)) % 8], v[r]) for r in range(8)]
        for b in range(8):
            w = v[(-b) % 8].astype(jnp.bfloat16)
            for ai in range(4):
                a = a0 + ai
                dest = (a % 16) * 16 + 2 * b + a // 16
                for c in range(2):
                    o_ref[dest, 0, c] = w[ai, :, c * LANES : (c + 1) * LANES]
        return 0

    lax.fori_loop(0, 8, some_columns, 0)


def analysis(place, samples, tables, hist=None, earlier=None):
    late = hist is None
    half = 1 if late else 0
    operands = [place, samples, *tables]
    scratch = [
        pltpu.VMEM((2, COLS, 64, LANES), jnp.float32),
        pltpu.VMEM((2, COLS, 8, LANES), jnp.float32),
    ]
    specs = [pl.BlockSpec(memory_space=pltpu.SMEM)]
    specs += [pl.BlockSpec(memory_space=pltpu.VMEM)] * 5
    aliases = {}
    if not late:
        operands += [hist, earlier]
        specs += [pl.BlockSpec(memory_space=pltpu.VMEM), pl.BlockSpec(memory_space=pl.ANY)]
        scratch.append(pltpu.VMEM((2, TAPS - 1, COLS, 16, LANES), jnp.float32))
        aliases = {7: 0}
    return pl.pallas_call(
        functools.partial(analysis_kernel, late),
        grid=(1,),
        in_specs=specs,
        out_specs=pl.BlockSpec((256, 1, 2, 8, LANES), lambda i: (0, half, 0, 0, 0)),
        out_shape=jax.ShapeDtypeStruct((256, 2, 2, 8, LANES), jnp.bfloat16),
        scratch_shapes=scratch,
        input_output_aliases=aliases,
        name="analysis_late" if late else "analysis_early",
        compiler_params=pltpu.CompilerParams(vmem_limit_bytes=VMEM_LIMIT),
    )(*operands)


def steer_kernel(b_ref, omega_ref, pos_ref, beam_ref, o_ref):
    e = pl.program_id(0)
    b = b_ref[0]
    lane = lax.broadcasted_iota(jnp.int32, (8, LANES), 1)
    inner = lane % 16

    def within(x, sh):
        return jnp.where(inner >= sh, pltpu.roll(x, sh, 1), pltpu.roll(x, sh + (LANES - 16), 1))

    coords = []
    for d in range(2):
        x = pltpu.roll(pos_ref[d], b * 16, 1)
        coords.append(jnp.where(lane // 16 < b, within(x, (e + 1) % 16), within(x, e)))
    omega = omega_ref[e]
    sin_b = jnp.broadcast_to(beam_ref[:, 0:1], (64, LANES))
    cos_b = jnp.broadcast_to(beam_ref[:, 1:2], (64, LANES))
    for i in range(8):
        turns = omega * (sin_b * coords[0][i : i + 1, :] + cos_b * coords[1][i : i + 1, :])
        rest = turns - jnp.round(turns)
        sq = rest * rest
        sn = rest * horner(SINE, sq)
        cs = horner(COSINE, sq)
        col = slice(i * LANES, (i + 1) * LANES)
        far = slice(1024 + i * LANES, 1024 + (i + 1) * LANES)
        o_ref[0, :, col] = (1.0 - 2.0 * sn * sn).astype(jnp.bfloat16)
        o_ref[0, :, far] = (-2.0 * sn * cs).astype(jnp.bfloat16)


def beam_kernel(b_ref, lam_ref, r_ref, s_ref, o_ref, x_ref, y_ref, m_ref):
    step = pl.program_id(0)

    @pl.when(step < 4)
    def _():
        b = b_ref[0]
        lane = lax.broadcasted_iota(jnp.int32, (8, LANES), 1)
        low = lax.broadcasted_iota(jnp.int32, (8, LANES), 0) < 4
        shift = (lane % 16 - jnp.where(lane // 16 < b, 1, 0) + 16) % 16
        bits = [(shift // (1 << t)) % 2 == 1 for t in range(4)]

        def network(section, half, c):
            v = [r_ref[section, step, g, half, c].astype(jnp.float32) for g in range(16)]
            for t in range(4):
                v = [jnp.where(bits[t], v[(r + (1 << t)) % 16], v[r]) for r in range(16)]
            return v

        def separate(pair, _):
            top = pl.ds(pl.multiple_of(pair * 16, 16), 16)
            bot = pl.ds(pl.multiple_of(32 + pair * 16, 16), 16)
            near = [pl.multiple_of(step * 256 + mh * LANES, LANES) for mh in range(2)]
            far = [pl.multiple_of(1024 + step * 256 + mh * LANES, LANES) for mh in range(2)]
            for c in range(2):
                tiles = [[None] * 16, [None] * 16]
                for one in range(2):
                    v0 = network(pair * 2 + one, 0, c)
                    v1 = network(pair * 2 + one, 1, c)
                    for r in range(16):
                        first = jnp.where(low, v0[r], pltpu.roll(v1[r], 4, 0))
                        second = jnp.where(low, pltpu.roll(v0[r], 4, 0), v1[r])
                        for mh, value in enumerate((first, second)):
                            if one == 0:
                                tiles[mh][r] = value
                            else:
                                tiles[mh][r] = jnp.concatenate([tiles[mh][r], value], axis=0)
                for mh in range(2):
                    for e in range(16):
                        w = tiles[mh][(-e) % 16]
                        w16 = w.astype(jnp.bfloat16)
                        if c == 0:
                            x_ref[e, top, pl.ds(near[mh], LANES)] = w16
                            x_ref[e, bot, pl.ds(far[mh], LANES)] = w16
                        else:
                            x_ref[e, top, pl.ds(far[mh], LANES)] = w16
                            x_ref[e, bot, pl.ds(near[mh], LANES)] = (-w).astype(jnp.bfloat16)
            return 0

        lax.fori_loop(0, 2, separate, 0)

    @pl.when(step >= 4)
    def _():
        total = 1024.0
        snapshots = 32.0
        sign = jnp.where(lax.broadcasted_iota(jnp.int32, (64, 64), 1) < 32, 1.0, -1.0)
        first = (step - 4) * 2
        order = [0, 1, 8, 9]
        ys = []
        dims = (((1,), (1,)), ((), ()))
        hs, gs = [], []
        for i in range(4):
            x = x_ref[first + order[i]]
            both = jnp.concatenate([s_ref[i], x], axis=0)
            out = lax.dot_general(both, x, dims, preferred_element_type=jnp.float32)
            hs.append(out[:64])
            gs.append(out[64:])
        ghs = [
            jnp.dot(h, g, precision=lax.Precision.HIGHEST, preferred_element_type=jnp.float32)
            for h, g in zip(hs, gs)
        ]
        for i in range(4):
            h, gh = hs[i], ghs[i]
            lam = lam_ref[first + order[i]]
            hh = jnp.sum(h * h, axis=1, keepdims=True)
            hgh = jnp.sum(h * gh, axis=1, keepdims=True)
            alpha = total / (hh / snapshots + lam * total)
            rho = 1.0 - alpha * lam
            t = alpha / snapshots
            new = rho * rho * total - 2.0 * rho * t * hh + t * t * hgh
            along = rho + new / total
            proj = along * h - t * gh
            size = along * along * total - 2.0 * along * t * hh + t * t * hgh
            curv = jnp.sum(proj * proj, axis=1, keepdims=True) / snapshots + lam * size
            alpha2 = new / curv
            main = alpha + alpha2 * along
            rest = alpha2 * t
            power = main * main * total - 2.0 * main * rest * hh + rest * rest * hgh
            norm = lax.rsqrt(power + total * 1e-6)
            ys.append(sign * ((norm * main) * h - (norm * rest) * gh))
        for i in range(2):
            y_ref[first + i] = jnp.concatenate([ys[i], ys[i + 2]], axis=1)

    @pl.when(step == 7)
    def _():
        v = swap_bits([y_ref[r] for r in range(8)], 8)
        near = lax.broadcasted_iota(jnp.int32, (64, LANES), 1) % 8 < 4
        for section in range(4):
            rows = [v[section], v[4 + section]]
            if section:
                rows.append(
                    jnp.where(near, pltpu.roll(v[section - 1], LANES - 4, 1), v[4 + section - 1])
                )
            else:
                rows.append(jnp.zeros((64, LANES), jnp.float32))
            rows.append(jnp.zeros((64, LANES), jnp.float32))
            for r in range(4):
                m_ref[pl.ds(section * 256 + r, 64, stride=4), :] = rows[r]
        o_ref[...] = m_ref[...].astype(jnp.bfloat16)


def synthesis_kernel(m_ref, proto_ref, tw_ref, w_ref, o_ref, r_ref, l_ref, z_ref, s_ref):
    r_ref[...] = m_ref[...].astype(jnp.float32)
    for a_hi in range(2):
        tiles = []
        for r in range(3):
            groups = []
            for group in range(2):
                v = [
                    r_ref[pl.ds((group * 128 + 2 * b + a_hi) * 4 + r, 8, stride=64), :]
                    for b in range(8)
                ]
                groups.append(swap_bits(v, 1))
            tiles.append(
                [jnp.concatenate([groups[0][k], groups[1][k]], axis=0) for k in range(8)]
            )
        for k in range(8):
            rows = slice(k * COLS + a_hi * 16, k * COLS + a_hi * 16 + 16)
            l_ref[rows, :LANES] = tiles[0][k].astype(jnp.bfloat16)
            l_ref[rows, LANES:] = tiles[1][k].astype(jnp.bfloat16)
        for k in range(4):
            rows = slice((8 + k) * COLS + a_hi * 16, (8 + k) * COLS + a_hi * 16 + 16)
            l_ref[rows, :LANES] = tiles[2][k].astype(jnp.bfloat16)
            l_ref[rows, LANES:] = tiles[2][4 + k].astype(jnp.bfloat16)
    full = jnp.dot(l_ref[...], w_ref[...], preferred_element_type=jnp.float32)
    for c in range(2):
        cut = slice(c * LANES, (c + 1) * LANES)
        z_ref[c, : 8 * COLS] = full[: 8 * COLS, cut]
        z_ref[c, 8 * COLS : 12 * COLS] = jnp.zeros((4 * COLS, LANES), jnp.float32)
        z_ref[c, 12 * COLS :] = full[8 * COLS :, cut]

    def half(i, _):
        values = []
        for a in range(COLS):
            rows = pl.ds(i * (8 * COLS) + a, 8, stride=COLS)
            re = z_ref[0, rows, :]
            im = z_ref[1, rows, :]
            cs = tw_ref[0, a : a + 1, :]
            sn = tw_ref[1, a : a + 1, :]
            values.append((re * cs - im * sn, re * sn + im * cs))
        for j, (re, im) in enumerate(fft(values, 1.0)):
            s_ref[0, i, j] = re.astype(jnp.bfloat16).astype(jnp.float32)
            s_ref[1, i, j] = im.astype(jnp.bfloat16).astype(jnp.float32)
        return 0

    for i in range(2):
        half(i, 0)
    for c in range(2):
        for j in range(COLS):
            taps = [proto_ref[TAPS - 1 - p, j : j + 1, :] for p in range(TAPS)]
            out = filtered_rows(s_ref[c, 0, j], s_ref[c, 1, j], taps, 8)
            o_ref[c, 0, :, j * LANES : (j + 1) * LANES] = out.astype(jnp.bfloat16)


def body(samples, positions, beam_dir, load_exp):
    sections = lax.axis_size("section")
    groups = lax.axis_size("gx")
    device = lax.axis_index(AXES).astype(jnp.int32)
    spot = (device % 16)[None]

    proto = jnp.asarray(prototype_table())
    w_forward = jnp.asarray(forward_columns(), jnp.bfloat16)
    w_inverse = jnp.asarray(lane_transform(1.0, 1.0 / 64.0), jnp.bfloat16)

    samples, last = unpack(spot, samples)
    hist = lax.ppermute(last, "section", [(i, i + 1) for i in range(sections - 1)])

    a_index, l_index = np.arange(COLS)[:, None], np.arange(LANES)[None, :]
    n_angle = 2.0 * np.pi / 4096.0 * a_index * l_index
    tw_inverse = jnp.asarray(np.stack([np.cos(n_angle), np.sin(n_angle)]), jnp.float32)
    turns = jnp.asarray(np.stack([np.cos(n_angle), -np.sin(n_angle)]), jnp.float32)
    s_angle = 2.0 * np.pi / LANES * ((np.arange(LANES)[:, None] * l_index) % LANES)
    shifts = jnp.asarray(np.stack([np.cos(s_angle), np.sin(s_angle)]), jnp.float32)
    tables = [proto, turns, shifts, w_forward]

    hist = pltpu.with_memory_space_constraint(hist, pltpu.VMEM)
    message = analysis(spot, samples, tables)
    message = analysis(spot, samples, tables, hist, message)

    message, positions, load_exp, beam_dir, device = lax.optimization_barrier(
        (message, positions, load_exp, beam_dir, device)
    )
    own_b = (device % 16) // 2
    own_a = device // 16 + 16 * (device % 2)
    received = lax.all_to_all(message, AXES, 0, 0, tiled=True)

    devices = sections * groups
    exponents = load_exp.astype(jnp.float32)
    rows = [exponents]
    for t in range(1, 16):
        rows.append(lax.ppermute(exponents, AXES, [(i, i ^ (16 * t)) for i in range(devices)]))
    own = device // 16
    slots = jnp.arange(16, dtype=jnp.int32)
    picked = jnp.sum(jnp.stack(rows) * (slots == own)[None, :], axis=1)
    mine = jnp.sum(jnp.where((slots ^ own)[:, None] == slots[None, :], picked[None, :], 0.0), axis=1)
    lam = jnp.exp2(mine)

    spread = positions.reshape(2, 4, 16, 2, 8).transpose(0, 1, 3, 4, 2).reshape(2, 8, LANES)
    channel = own_a + 32 * own_b + 256 * jnp.arange(16, dtype=jnp.int32)
    angular = 0.75 + 0.5 * channel.astype(jnp.float32) / 4096
    beams = beam_dir.shape[0]
    angle_beam = math.pi / beams * (beam_dir.astype(jnp.float32) + 0.5) - 0.5 * math.pi
    directions = jnp.stack([jnp.sin(angle_beam), jnp.cos(angle_beam)], axis=1)
    steer = pl.pallas_call(
        steer_kernel,
        grid=(16,),
        in_specs=[
            pl.BlockSpec(memory_space=pltpu.SMEM),
            pl.BlockSpec(memory_space=pltpu.SMEM),
            pl.BlockSpec((2, 8, LANES), lambda e: (0, 0, 0)),
            pl.BlockSpec((beams, 2), lambda e: (0, 0)),
        ],
        out_specs=pl.BlockSpec(
            (1, beams, 2048), lambda e: (4 * ((e % 8) // 2) + e % 2 + 2 * (e // 8), 0, 0)
        ),
        out_shape=jax.ShapeDtypeStruct((16, beams, 2048), jnp.bfloat16),
        name="steer",
        compiler_params=pltpu.CompilerParams(vmem_limit_bytes=VMEM_LIMIT),
    )(own_b[None], angular, spread, directions)

    steer = pltpu.with_memory_space_constraint(steer, pltpu.HBM)
    received = pltpu.with_memory_space_constraint(
        received.reshape(4, 4, 16, 2, 2, 8, LANES), pltpu.VMEM
    )
    back = pl.pallas_call(
        beam_kernel,
        grid=(8,),
        in_specs=[
            pl.BlockSpec(memory_space=pltpu.SMEM),
            pl.BlockSpec(memory_space=pltpu.SMEM),
            pl.BlockSpec(memory_space=pltpu.VMEM),
            pl.BlockSpec((4, beams, 2048), lambda i: (jnp.maximum(i - 4, 0), 0, 0)),
        ],
        out_specs=pl.BlockSpec((4 * devices, LANES), lambda i: (0, 0)),
        out_shape=jax.ShapeDtypeStruct((4 * devices, LANES), jnp.bfloat16),
        scratch_shapes=[
            pltpu.VMEM((16, 64, 2048), jnp.bfloat16),
            pltpu.VMEM((8, beams, LANES), jnp.float32),
            pltpu.VMEM((4 * devices, LANES), jnp.float32),
        ],
        name="beams",
        compiler_params=pltpu.CompilerParams(vmem_limit_bytes=VMEM_LIMIT),
    )(own_b[None], lam, received, steer)

    returned = lax.all_to_all(back.reshape(devices, 4, LANES), AXES, 0, 0, tiled=True)
    return pl.pallas_call(
        synthesis_kernel,
        in_specs=[pl.BlockSpec(memory_space=pltpu.VMEM)] * 4,
        out_specs=pl.BlockSpec(memory_space=pltpu.VMEM),
        out_shape=jax.ShapeDtypeStruct((2, 1, 8, 4096), jnp.bfloat16),
        scratch_shapes=[
            pltpu.VMEM((4 * devices, LANES), jnp.float32),
            pltpu.VMEM((12 * COLS, 2 * LANES), jnp.bfloat16),
            pltpu.VMEM((2, 16 * COLS, LANES), jnp.float32),
            pltpu.VMEM((2, 2, COLS, 8, LANES), jnp.float32),
        ],
        name="synthesis",
        compiler_params=pltpu.CompilerParams(vmem_limit_bytes=VMEM_LIMIT),
    )(returned.reshape(4 * devices, LANES), proto, tw_inverse, w_inverse)


def solution(mesh):
    placed = (P(None, "gx", "section", None), P(), P(), P(AXES))
    return jax.shard_map(
        body, mesh=mesh, in_specs=placed, out_specs=P(None, "gx", "section", None), check_vma=False
    )
```

```python
import functools
import math

import numpy as np
import jax
import jax.numpy as jnp
from jax import lax
from jax.experimental import pallas as pl
from jax.experimental.pallas import tpu as pltpu
from jax.sharding import PartitionSpec as P

TAPS = 4
LANES = 128
COLS = 32
AXES = ("section", "gx")
VMEM_LIMIT = 32 << 20
SINE = [(-1.0) ** i * math.pi ** (2 * i + 1) / math.factorial(2 * i + 1) for i in range(6)]
COSINE = [(-1.0) ** i * math.pi ** (2 * i) / math.factorial(2 * i) for i in range(6)]


def horner(coefficients, x):
    out = coefficients[-1]
    for value in reversed(coefficients[:-1]):
        out = out * x + value
    return out


def prototype_table():
    total = TAPS * COLS * LANES
    position = np.arange(total, dtype=np.float64) + 0.5
    window = 0.5 - 0.5 * np.cos(2.0 * np.pi / total * position)
    shaped = np.sinc((position - 0.5 * total) / (COLS * LANES)) * window
    return shaped.reshape(TAPS, COLS, LANES).astype(np.float32)


def lane_transform(sign, scale):
    l = np.arange(LANES)
    angle = 2.0 * np.pi * ((l[:, None] * l[None, :]) % LANES) / LANES
    c, s = np.cos(angle) * scale, sign * np.sin(angle) * scale
    return np.block([[c, s], [-s, c]])


def forward_columns():
    lane = np.arange(LANES)
    order = (lane // 16) + 8 * (lane % 16)
    table = lane_transform(-1.0, 1.0 / 64.0)
    return table[:, np.concatenate([order, LANES + order])]


def swap_bits(v, distance):
    lane = lax.broadcasted_iota(jnp.int32, v[0].shape, len(v[0].shape) - 1)
    for t in range(3):
        step = distance << t
        mask = (lane // step) % 2 == 1
        out = list(v)
        for low in range(8):
            if low & (1 << t):
                continue
            high = low | (1 << t)
            out[low] = jnp.where(mask, pltpu.roll(v[high], step, 1), v[low])
            out[high] = jnp.where(mask, v[high], pltpu.roll(v[low], LANES - step, 1))
        v = out
    return v


def twiddle(re, im, k, n, sign):
    k = k % n
    if k == 0:
        return re, im
    if 4 * k == n:
        return (im, -re) if sign < 0 else (-im, re)
    if 8 * k == n:
        c = math.sqrt(0.5)
        return ((re + im) * c, (im - re) * c) if sign < 0 else ((re - im) * c, (im + re) * c)
    if 8 * k == 3 * n:
        c = math.sqrt(0.5)
        return ((im - re) * c, (-im - re) * c) if sign < 0 else ((-re - im) * c, (re - im) * c)
    c, s = math.cos(2 * math.pi * k / n), sign * math.sin(2 * math.pi * k / n)
    return re * c - im * s, re * s + im * c


def fft(values, sign):
    n = len(values)
    if n == 1:
        return values
    even = fft(values[0::2], sign)
    odd = fft(values[1::2], sign)
    low, high = [], []
    for k in range(n // 2):
        tr, ti = twiddle(odd[k][0], odd[k][1], k, n, sign)
        er, ei = even[k]
        low.append((er + tr, ei + ti))
        high.append((er - tr, ei - ti))
    return low + high


def filtered_rows(now, before, taps, period):
    row = lax.broadcasted_iota(jnp.int32, now.shape, 0) % period
    out = taps[0] * now
    for p in range(1, TAPS):
        out = out + taps[p] * pltpu.roll(jnp.where(row >= period - p, before, now), p, 0)
    return out


def unpack_kernel(place_ref, x_ref, xs_ref, h_ref):
    i = pl.program_id(0)
    for j in range(8):
        for c in range(2):
            for m in range(16):
                value = x_ref[c, m, :, j * LANES : (j + 1) * LANES]
                xs_ref[c, i * 8 + j, m * 8 : m * 8 + 8, :] = value.astype(jnp.float32)
            for t in range(TAPS - 1):
                value = xs_ref[c, i * 8 + j, pl.ds(8 - (TAPS - 1) + t, 16, stride=8), :]
                cut = pl.ds(pl.multiple_of(i * 1024 + j * LANES, LANES), LANES)
                h_ref[c, t, :, cut] = value.astype(jnp.bfloat16)


def unpack(place, samples):
    return pl.pallas_call(
        unpack_kernel,
        grid=(4,),
        in_specs=[
            pl.BlockSpec(memory_space=pltpu.SMEM),
            pl.BlockSpec((2, 16, 8, 1024), lambda i: (0, 0, 0, i)),
        ],
        out_specs=[pl.BlockSpec(memory_space=pltpu.VMEM)] * 2,
        out_shape=[
            pltpu.VMEM((2, COLS, 128, LANES), jnp.float32),
            pltpu.VMEM((2, TAPS - 1, 16, COLS * LANES), jnp.bfloat16),
        ],
        name="unpack",
        compiler_params=pltpu.CompilerParams(vmem_limit_bytes=VMEM_LIMIT),
    )(place, samples)


def analysis_kernel(late, place_ref, x_ref, proto_ref, turn_ref, shift_ref, w_ref, *rest):
    if late:
        o_ref, z_ref, tw_ref, f_ref = rest
    else:
        h_ref, _, o_ref, z_ref, tw_ref, f_ref = rest
    start = 4 if late else 0

    def block(c, j, mh, k):
        if k < 0:
            cut = slice(j * LANES, (j + 1) * LANES)
            return h_ref[c, TAPS - 1 + k, mh * 8 : mh * 8 + 8, cut].astype(jnp.float32)
        return x_ref[c, j, pl.ds(mh * 64 + k, 8, stride=8), :]

    shifts = pl.ds(pl.multiple_of(place_ref[0] * 8, 8), 8)
    shift_re, shift_im = shift_ref[0, shifts, :], shift_ref[1, shifts, :]
    for a in range(COLS):
        cs, sn = turn_ref[0, a : a + 1, :], turn_ref[1, a : a + 1, :]
        tw_ref[0, a] = shift_re * cs - shift_im * sn
        tw_ref[1, a] = shift_re * sn + shift_im * cs

    for mh in range(2):
        for j in range(COLS):
            taps = [proto_ref[p, j : j + 1, :] for p in range(TAPS)]
            for c in range(2):
                blocks = [block(c, j, mh, start - (TAPS - 1) + t) for t in range(TAPS + 3)]
                for k in range(4):
                    out = taps[0] * blocks[k + 3]
                    for p in range(1, TAPS):
                        out = out + taps[p] * blocks[k + 3 - p]
                    f_ref[k, c, j] = out
        for k in range(4):
            values = [(f_ref[k, 0, j], f_ref[k, 1, j]) for j in range(COLS)]
            i = mh * 4 + k
            for a, (re, im) in enumerate(fft(values, -1.0)):
                cs = tw_ref[0, a]
                sn = tw_ref[1, a]
                z_ref[0, a, i * 8 : i * 8 + 8, :] = re * cs - im * sn
                z_ref[1, a, i * 8 : i * 8 + 8, :] = re * sn + im * cs

    seg = lax.broadcasted_iota(jnp.int32, (1, 8, 2 * LANES), 2) % LANES // 16
    bits = [(seg // (1 << t)) % 2 == 1 for t in range(3)]

    def some_columns(i, _):
        a0 = i * 4
        parts = []
        for c in range(2):
            rows = [
                z_ref[c, a0 + ai, pl.ds(mu, 8, stride=8), :] for mu in range(8) for ai in range(4)
            ]
            parts.append(jnp.concatenate(rows, axis=0).astype(jnp.bfloat16))
        z = jnp.concatenate(parts, axis=1)
        out = jnp.dot(z, w_ref[...], preferred_element_type=jnp.float32)
        out = out.reshape(8, 4, 8, 2 * LANES)
        v = [out[r] for r in range(8)]
        for t in range(3):
            mask = jnp.broadcast_to(bits[t], (4, 8, 2 * LANES))
            v = [jnp.where(mask, v[(r + (1 << t)) % 8], v[r]) for r in range(8)]
        for b in range(8):
            w = v[(-b) % 8].astype(jnp.bfloat16)
            for ai in range(4):
                a = a0 + ai
                dest = (a % 16) * 16 + 2 * b + a // 16
                for c in range(2):
                    o_ref[dest, 0, c] = w[ai, :, c * LANES : (c + 1) * LANES]
        return 0

    lax.fori_loop(0, 8, some_columns, 0)


def analysis(place, samples, tables, hist=None, earlier=None):
    late = hist is None
    half = 1 if late else 0
    operands = [place, samples, *tables]
    scratch = [
        pltpu.VMEM((2, COLS, 64, LANES), jnp.float32),
        pltpu.VMEM((2, COLS, 8, LANES), jnp.float32),
        pltpu.VMEM((4, 2, COLS, 8, LANES), jnp.float32),
    ]
    specs = [pl.BlockSpec(memory_space=pltpu.SMEM)]
    specs += [pl.BlockSpec(memory_space=pltpu.VMEM)] * 5
    aliases = {}
    if not late:
        operands += [hist, earlier]
        specs += [pl.BlockSpec(memory_space=pltpu.VMEM), pl.BlockSpec(memory_space=pl.ANY)]
        aliases = {7: 0}
    return pl.pallas_call(
        functools.partial(analysis_kernel, late),
        grid=(1,),
        in_specs=specs,
        out_specs=pl.BlockSpec((256, 1, 2, 8, LANES), lambda i: (0, half, 0, 0, 0)),
        out_shape=jax.ShapeDtypeStruct((256, 2, 2, 8, LANES), jnp.bfloat16),
        scratch_shapes=scratch,
        input_output_aliases=aliases,
        name="analysis_late" if late else "analysis_early",
        compiler_params=pltpu.CompilerParams(vmem_limit_bytes=VMEM_LIMIT),
    )(*operands)


def steer_kernel(b_ref, omega_ref, pos_ref, beam_ref, o_ref):
    e = pl.program_id(0)
    b = b_ref[0]
    lane = lax.broadcasted_iota(jnp.int32, (8, LANES), 1)
    inner = lane % 16

    def within(x, sh):
        return jnp.where(inner >= sh, pltpu.roll(x, sh, 1), pltpu.roll(x, sh + (LANES - 16), 1))

    coords = []
    for d in range(2):
        x = pltpu.roll(pos_ref[d], b * 16, 1)
        coords.append(jnp.where(lane // 16 < b, within(x, (e + 1) % 16), within(x, e)))
    omega = omega_ref[e]
    sin_b = jnp.broadcast_to(beam_ref[:, 0:1], (64, LANES))
    cos_b = jnp.broadcast_to(beam_ref[:, 1:2], (64, LANES))
    for i in range(8):
        turns = omega * (sin_b * coords[0][i : i + 1, :] + cos_b * coords[1][i : i + 1, :])
        rest = turns - jnp.round(turns)
        sq = rest * rest
        sn = rest * horner(SINE, sq)
        cs = horner(COSINE, sq)
        col = slice(i * LANES, (i + 1) * LANES)
        far = slice(1024 + i * LANES, 1024 + (i + 1) * LANES)
        o_ref[0, :, col] = (1.0 - 2.0 * sn * sn).astype(jnp.bfloat16)
        o_ref[0, :, far] = (-2.0 * sn * cs).astype(jnp.bfloat16)


def beam_kernel(b_ref, lam_ref, r_ref, s_ref, o_ref, x_ref, y_ref, m_ref):
    step = pl.program_id(0)

    @pl.when(step < 4)
    def _():
        b = b_ref[0]
        lane = lax.broadcasted_iota(jnp.int32, (8, LANES), 1)
        low = lax.broadcasted_iota(jnp.int32, (8, LANES), 0) < 4
        shift = (lane % 16 - jnp.where(lane // 16 < b, 1, 0) + 16) % 16
        bits = [(shift // (1 << t)) % 2 == 1 for t in range(4)]

        def network(section, half, c):
            v = [r_ref[section, step, g, half, c].astype(jnp.float32) for g in range(16)]
            for t in range(4):
                v = [jnp.where(bits[t], v[(r + (1 << t)) % 16], v[r]) for r in range(16)]
            return v

        def separate(pair, _):
            top = pl.ds(pl.multiple_of(pair * 16, 16), 16)
            bot = pl.ds(pl.multiple_of(32 + pair * 16, 16), 16)
            near = [pl.multiple_of(step * 256 + mh * LANES, LANES) for mh in range(2)]
            far = [pl.multiple_of(1024 + step * 256 + mh * LANES, LANES) for mh in range(2)]
            for c in range(2):
                tiles = [[None] * 16, [None] * 16]
                for one in range(2):
                    v0 = network(pair * 2 + one, 0, c)
                    v1 = network(pair * 2 + one, 1, c)
                    for r in range(16):
                        first = jnp.where(low, v0[r], pltpu.roll(v1[r], 4, 0))
                        second = jnp.where(low, pltpu.roll(v0[r], 4, 0), v1[r])
                        for mh, value in enumerate((first, second)):
                            if one == 0:
                                tiles[mh][r] = value
                            else:
                                tiles[mh][r] = jnp.concatenate([tiles[mh][r], value], axis=0)
                for mh in range(2):
                    for e in range(16):
                        w = tiles[mh][(-e) % 16]
                        w16 = w.astype(jnp.bfloat16)
                        if c == 0:
                            x_ref[e, top, pl.ds(near[mh], LANES)] = w16
                            x_ref[e, bot, pl.ds(far[mh], LANES)] = w16
                        else:
                            x_ref[e, top, pl.ds(far[mh], LANES)] = w16
                            x_ref[e, bot, pl.ds(near[mh], LANES)] = (-w).astype(jnp.bfloat16)
            return 0

        lax.fori_loop(0, 2, separate, 0)

    @pl.when(step >= 4)
    def _():
        total = 1024.0
        snapshots = 32.0
        left = lax.broadcasted_iota(jnp.int32, (64, LANES), 1) < 64
        sign = jnp.where(lax.broadcasted_iota(jnp.int32, (64, LANES), 0) < 32, 1.0, -1.0)
        first = (step - 4) * 2
        dims = (((1,), (1,)), ((), ()))
        hs, gs = [], []
        for i in range(2):
            x = x_ref[first + i]
            near = jnp.concatenate([s_ref[i], x], axis=0)
            near = lax.dot_general(x, near, dims, preferred_element_type=jnp.float32)
            x = x_ref[first + i + 8]
            far = jnp.concatenate([x, s_ref[i + 2]], axis=0)
            far = lax.dot_general(x, far, dims, preferred_element_type=jnp.float32)
            hs.append(jnp.where(left, near, far))
            gs.append(jnp.where(left, far, near))
        ghs = []
        for h, g in zip(hs, gs):
            both = jnp.concatenate([jnp.where(left, 0.0, h), jnp.where(left, h, 0.0)], axis=0)
            ghs.append(
                jnp.dot(g, both, precision=lax.Precision.HIGHEST, preferred_element_type=jnp.float32)
            )
        for i in range(2):
            h, gh = hs[i], ghs[i]
            lam = jnp.where(left[:1], lam_ref[first + i], lam_ref[first + i + 8])
            hh = jnp.sum(h * h, axis=0, keepdims=True)
            hgh = jnp.sum(h * gh, axis=0, keepdims=True)
            alpha = total / (hh / snapshots + lam * total)
            rho = 1.0 - alpha * lam
            t = alpha / snapshots
            new = rho * rho * total - 2.0 * rho * t * hh + t * t * hgh
            along = rho + new / total
            proj = along * h - t * gh
            size = along * along * total - 2.0 * along * t * hh + t * t * hgh
            curv = jnp.sum(proj * proj, axis=0, keepdims=True) / snapshots + lam * size
            alpha2 = new / curv
            main = alpha + alpha2 * along
            rest = alpha2 * t
            power = main * main * total - 2.0 * main * rest * hh + rest * rest * hgh
            norm = lax.rsqrt(power + total * 1e-6)
            y_ref[first + i] = sign * ((norm * main) * h - (norm * rest) * gh)

    @pl.when(step == 7)
    def _():
        left = lax.broadcasted_iota(jnp.int32, (64, LANES), 1) < 64
        lane = lax.broadcasted_iota(jnp.int32, (64, LANES), 1) % 64
        pick = jnp.where(lane == lax.broadcasted_iota(jnp.int32, (64, LANES), 0), 1.0, 0.0)
        pick = pick.astype(jnp.bfloat16)
        v = []
        for r in range(8):
            y = y_ref[r]
            both = jnp.concatenate([jnp.where(left, y, 0.0), jnp.where(left, 0.0, y)], axis=0)
            v.append(
                lax.dot_general(
                    pick,
                    both.astype(jnp.bfloat16),
                    (((1,), (1,)), ((), ())),
                    preferred_element_type=jnp.float32,
                )
            )
        v = swap_bits(v, 8)
        near = lax.broadcasted_iota(jnp.int32, (64, LANES), 1) % 8 < 4
        for section in range(4):
            rows = [v[section], v[4 + section]]
            if section:
                rows.append(
                    jnp.where(near, pltpu.roll(v[section - 1], LANES - 4, 1), v[4 + section - 1])
                )
            else:
                rows.append(jnp.zeros((64, LANES), jnp.float32))
            rows.append(jnp.zeros((64, LANES), jnp.float32))
            for r in range(4):
                m_ref[pl.ds(section * 256 + r, 64, stride=4), :] = rows[r]
        o_ref[...] = m_ref[...].astype(jnp.bfloat16)


def synthesis_kernel(m_ref, proto_ref, tw_ref, w_ref, o_ref, r_ref, l_ref, z_ref, s_ref):
    r_ref[...] = m_ref[...].astype(jnp.float32)
    for a_hi in range(2):
        tiles = []
        for r in range(3):
            groups = []
            for group in range(2):
                v = [
                    r_ref[pl.ds((group * 128 + 2 * b + a_hi) * 4 + r, 8, stride=64), :]
                    for b in range(8)
                ]
                groups.append(swap_bits(v, 1))
            tiles.append(
                [jnp.concatenate([groups[0][k], groups[1][k]], axis=0) for k in range(8)]
            )
        for k in range(8):
            rows = slice(k * COLS + a_hi * 16, k * COLS + a_hi * 16 + 16)
            l_ref[rows, :LANES] = tiles[0][k].astype(jnp.bfloat16)
            l_ref[rows, LANES:] = tiles[1][k].astype(jnp.bfloat16)
        for k in range(4):
            rows = slice((8 + k) * COLS + a_hi * 16, (8 + k) * COLS + a_hi * 16 + 16)
            l_ref[rows, :LANES] = tiles[2][k].astype(jnp.bfloat16)
            l_ref[rows, LANES:] = tiles[2][4 + k].astype(jnp.bfloat16)
    full = jnp.dot(l_ref[...], w_ref[...], preferred_element_type=jnp.float32)
    for c in range(2):
        cut = slice(c * LANES, (c + 1) * LANES)
        z_ref[c, : 8 * COLS] = full[: 8 * COLS, cut]
        z_ref[c, 8 * COLS : 12 * COLS] = jnp.zeros((4 * COLS, LANES), jnp.float32)
        z_ref[c, 12 * COLS :] = full[8 * COLS :, cut]

    def half(i, _):
        values = []
        for a in range(COLS):
            rows = pl.ds(i * (8 * COLS) + a, 8, stride=COLS)
            re = z_ref[0, rows, :]
            im = z_ref[1, rows, :]
            cs = tw_ref[0, a : a + 1, :]
            sn = tw_ref[1, a : a + 1, :]
            values.append((re * cs - im * sn, re * sn + im * cs))
        for j, (re, im) in enumerate(fft(values, 1.0)):
            s_ref[0, i, j] = re.astype(jnp.bfloat16).astype(jnp.float32)
            s_ref[1, i, j] = im.astype(jnp.bfloat16).astype(jnp.float32)
        return 0

    for i in range(2):
        half(i, 0)
    for c in range(2):
        for j in range(COLS):
            taps = [proto_ref[TAPS - 1 - p, j : j + 1, :] for p in range(TAPS)]
            out = filtered_rows(s_ref[c, 0, j], s_ref[c, 1, j], taps, 8)
            o_ref[c, 0, :, j * LANES : (j + 1) * LANES] = out.astype(jnp.bfloat16)


def body(samples, positions, beam_dir, load_exp):
    sections = lax.axis_size("section")
    groups = lax.axis_size("gx")
    device = lax.axis_index(AXES).astype(jnp.int32)
    spot = (device % 16)[None]

    proto = jnp.asarray(prototype_table())
    w_forward = jnp.asarray(forward_columns(), jnp.bfloat16)
    w_inverse = jnp.asarray(lane_transform(1.0, 1.0 / 64.0), jnp.bfloat16)

    samples, last = unpack(spot, pltpu.with_memory_space_constraint(samples, pltpu.HBM))
    hist = lax.ppermute(last, "section", [(i, i + 1) for i in range(sections - 1)])

    a_index, l_index = np.arange(COLS)[:, None], np.arange(LANES)[None, :]
    n_angle = 2.0 * np.pi / 4096.0 * a_index * l_index
    tw_inverse = jnp.asarray(np.stack([np.cos(n_angle), np.sin(n_angle)]), jnp.float32)
    turns = jnp.asarray(np.stack([np.cos(n_angle), -np.sin(n_angle)]), jnp.float32)
    s_angle = 2.0 * np.pi / LANES * ((np.arange(LANES)[:, None] * l_index) % LANES)
    shifts = jnp.asarray(np.stack([np.cos(s_angle), np.sin(s_angle)]), jnp.float32)
    tables = [proto, turns, shifts, w_forward]

    hist = pltpu.with_memory_space_constraint(hist, pltpu.VMEM)
    message = analysis(spot, samples, tables)
    message = analysis(spot, samples, tables, hist, message)

    message, positions, load_exp, beam_dir, device = lax.optimization_barrier(
        (message, positions, load_exp, beam_dir, device)
    )
    own_b = (device % 16) // 2
    own_a = device // 16 + 16 * (device % 2)
    received = lax.all_to_all(message, AXES, 0, 0, tiled=True)

    devices = sections * groups
    exponents = load_exp.astype(jnp.float32)
    rows = [exponents]
    for t in range(1, 16):
        rows.append(lax.ppermute(exponents, AXES, [(i, i ^ (16 * t)) for i in range(devices)]))
    own = device // 16
    slots = jnp.arange(16, dtype=jnp.int32)
    picked = jnp.sum(jnp.stack(rows) * (slots == own)[None, :], axis=1)
    mine = jnp.sum(jnp.where((slots ^ own)[:, None] == slots[None, :], picked[None, :], 0.0), axis=1)
    lam = jnp.exp2(mine)

    spread = positions.reshape(2, 4, 16, 2, 8).transpose(0, 1, 3, 4, 2).reshape(2, 8, LANES)
    channel = own_a + 32 * own_b + 256 * jnp.arange(16, dtype=jnp.int32)
    angular = 0.75 + 0.5 * channel.astype(jnp.float32) / 4096
    beams = beam_dir.shape[0]
    angle_beam = math.pi / beams * (beam_dir.astype(jnp.float32) + 0.5) - 0.5 * math.pi
    directions = jnp.stack([jnp.sin(angle_beam), jnp.cos(angle_beam)], axis=1)
    steer = pl.pallas_call(
        steer_kernel,
        grid=(16,),
        in_specs=[
            pl.BlockSpec(memory_space=pltpu.SMEM),
            pl.BlockSpec(memory_space=pltpu.SMEM),
            pl.BlockSpec((2, 8, LANES), lambda e: (0, 0, 0)),
            pl.BlockSpec((beams, 2), lambda e: (0, 0)),
        ],
        out_specs=pl.BlockSpec(
            (1, beams, 2048), lambda e: (4 * ((e % 8) // 2) + e % 2 + 2 * (e // 8), 0, 0)
        ),
        out_shape=jax.ShapeDtypeStruct((16, beams, 2048), jnp.bfloat16),
        name="steer",
        compiler_params=pltpu.CompilerParams(vmem_limit_bytes=VMEM_LIMIT),
    )(own_b[None], angular, spread, directions)

    steer = pltpu.with_memory_space_constraint(steer, pltpu.HBM)
    received = pltpu.with_memory_space_constraint(
        received.reshape(4, 4, 16, 2, 2, 8, LANES), pltpu.VMEM
    )
    back = pl.pallas_call(
        beam_kernel,
        grid=(8,),
        in_specs=[
            pl.BlockSpec(memory_space=pltpu.SMEM),
            pl.BlockSpec(memory_space=pltpu.SMEM),
            pl.BlockSpec(memory_space=pltpu.VMEM),
            pl.BlockSpec((4, beams, 2048), lambda i: (jnp.maximum(i - 4, 0), 0, 0)),
        ],
        out_specs=pl.BlockSpec((4 * devices, LANES), lambda i: (0, 0)),
        out_shape=jax.ShapeDtypeStruct((4 * devices, LANES), jnp.bfloat16),
        scratch_shapes=[
            pltpu.VMEM((16, 64, 2048), jnp.bfloat16),
            pltpu.VMEM((8, 64, LANES), jnp.float32),
            pltpu.VMEM((4 * devices, LANES), jnp.float32),
        ],
        name="beams",
        compiler_params=pltpu.CompilerParams(vmem_limit_bytes=VMEM_LIMIT),
    )(own_b[None], lam, received, steer)

    returned = lax.all_to_all(back.reshape(devices, 4, LANES), AXES, 0, 0, tiled=True)
    return pl.pallas_call(
        synthesis_kernel,
        in_specs=[pl.BlockSpec(memory_space=pltpu.VMEM)] * 4,
        out_specs=pl.BlockSpec(memory_space=pltpu.VMEM),
        out_shape=jax.ShapeDtypeStruct((2, 1, 8, 4096), jnp.bfloat16),
        scratch_shapes=[
            pltpu.VMEM((4 * devices, LANES), jnp.float32),
            pltpu.VMEM((12 * COLS, 2 * LANES), jnp.bfloat16),
            pltpu.VMEM((2, 16 * COLS, LANES), jnp.float32),
            pltpu.VMEM((2, 2, COLS, 8, LANES), jnp.float32),
        ],
        name="synthesis",
        compiler_params=pltpu.CompilerParams(vmem_limit_bytes=VMEM_LIMIT),
    )(returned.reshape(4 * devices, LANES), proto, tw_inverse, w_inverse)


def solution(mesh):
    placed = (P(None, "gx", "section", None), P(), P(), P(AXES))
    return jax.shard_map(
        body, mesh=mesh, in_specs=placed, out_specs=P(None, "gx", "section", None), check_vma=False
    )
```

```python
import math

import numpy as np
import jax
import jax.numpy as jnp
from jax import lax
from jax.experimental import pallas as pl
from jax.experimental.pallas import tpu as pltpu
from jax.sharding import PartitionSpec as P

TAPS = 4
LANES = 128
COLS = 32
AXES = ("section", "gx")
VMEM_LIMIT = 32 << 20
SINE = [(-1.0) ** i * math.pi ** (2 * i + 1) / math.factorial(2 * i + 1) for i in range(6)]
COSINE = [(-1.0) ** i * math.pi ** (2 * i) / math.factorial(2 * i) for i in range(6)]


def horner(coefficients, x):
    out = coefficients[-1]
    for value in reversed(coefficients[:-1]):
        out = out * x + value
    return out


def prototype_table():
    total = TAPS * COLS * LANES
    position = np.arange(total, dtype=np.float64) + 0.5
    window = 0.5 - 0.5 * np.cos(2.0 * np.pi / total * position)
    shaped = np.sinc((position - 0.5 * total) / (COLS * LANES)) * window
    return shaped.reshape(TAPS, COLS, LANES).astype(np.float32)


def lane_transform(sign, scale):
    l = np.arange(LANES)
    angle = 2.0 * np.pi * ((l[:, None] * l[None, :]) % LANES) / LANES
    c, s = np.cos(angle) * scale, sign * np.sin(angle) * scale
    return np.block([[c, s], [-s, c]])


def forward_columns():
    lane = np.arange(LANES)
    order = (lane // 16) + 8 * (lane % 16)
    table = lane_transform(-1.0, 1.0 / 64.0)
    return table[:, np.concatenate([order, LANES + order])]


def swap_bits(v, distance):
    lane = lax.broadcasted_iota(jnp.int32, v[0].shape, len(v[0].shape) - 1)
    for t in range(3):
        step = distance << t
        mask = (lane // step) % 2 == 1
        out = list(v)
        for low in range(8):
            if low & (1 << t):
                continue
            high = low | (1 << t)
            out[low] = jnp.where(mask, pltpu.roll(v[high], step, 1), v[low])
            out[high] = jnp.where(mask, v[high], pltpu.roll(v[low], LANES - step, 1))
        v = out
    return v


def twiddle(re, im, k, n, sign):
    k = k % n
    if k == 0:
        return re, im
    if 4 * k == n:
        return (im, -re) if sign < 0 else (-im, re)
    if 8 * k == n:
        c = math.sqrt(0.5)
        return ((re + im) * c, (im - re) * c) if sign < 0 else ((re - im) * c, (im + re) * c)
    if 8 * k == 3 * n:
        c = math.sqrt(0.5)
        return ((im - re) * c, (-im - re) * c) if sign < 0 else ((-re - im) * c, (re - im) * c)
    c, s = math.cos(2 * math.pi * k / n), sign * math.sin(2 * math.pi * k / n)
    return re * c - im * s, re * s + im * c


def fft(values, sign):
    n = len(values)
    if n == 1:
        return values
    even = fft(values[0::2], sign)
    odd = fft(values[1::2], sign)
    low, high = [], []
    for k in range(n // 2):
        tr, ti = twiddle(odd[k][0], odd[k][1], k, n, sign)
        er, ei = even[k]
        low.append((er + tr, ei + ti))
        high.append((er - tr, ei - ti))
    return low + high


def filtered_rows(now, before, taps, period):
    row = lax.broadcasted_iota(jnp.int32, now.shape, 0) % period
    out = taps[0] * now
    for p in range(1, TAPS):
        out = out + taps[p] * pltpu.roll(jnp.where(row >= period - p, before, now), p, 0)
    return out


def unpack_kernel(place_ref, x_ref, xs_ref, h_ref):
    i = pl.program_id(0)
    for j in range(COLS // 2):
        at = i * (COLS // 2) + j
        for c in range(2):
            for m in range(8):
                value = x_ref[c, m, :, j * LANES : (j + 1) * LANES]
                xs_ref[c, at, m * 8 : m * 8 + 8, :] = value.astype(jnp.float32)
            for t in range(TAPS - 1):
                value = xs_ref[c, at, pl.ds(8 - (TAPS - 1) + t, 8, stride=8), :]
                h_ref[c, t, :, pl.ds(pl.multiple_of(at * LANES, LANES), LANES)] = value.astype(
                    jnp.bfloat16
                )


def unpack(place, samples, group):
    return pl.pallas_call(
        unpack_kernel,
        grid=(2,),
        in_specs=[
            pl.BlockSpec(memory_space=pltpu.SMEM),
            pl.BlockSpec((2, 8, 8, COLS // 2 * LANES), lambda i: (0, group, 0, i)),
        ],
        out_specs=[pl.BlockSpec(memory_space=pltpu.VMEM)] * 2,
        out_shape=[
            pltpu.VMEM((2, COLS, 64, LANES), jnp.float32),
            pltpu.VMEM((2, TAPS - 1, 8, COLS * LANES), jnp.bfloat16),
        ],
        name=f"unpack_{group}",
        compiler_params=pltpu.CompilerParams(vmem_limit_bytes=VMEM_LIMIT),
    )(place, samples)


def transform_group(start, x_ref, h_ref, proto_ref, tw_ref, f_ref, z_ref, first_row):
    def block(c, j, k):
        if k < 0:
            cut = slice(j * LANES, (j + 1) * LANES)
            return h_ref[c, TAPS - 1 + k, :, cut].astype(jnp.float32)
        return x_ref[c, j, pl.ds(k, 8, stride=8), :]

    for j in range(COLS):
        taps = [proto_ref[p, j : j + 1, :] for p in range(TAPS)]
        for c in range(2):
            blocks = [block(c, j, start - (TAPS - 1) + t) for t in range(TAPS + 3)]
            for k in range(4):
                out = taps[0] * blocks[k + 3]
                for p in range(1, TAPS):
                    out = out + taps[p] * blocks[k + 3 - p]
                f_ref[k, c, j] = out
    for k in range(4):
        values = [(f_ref[k, 0, j], f_ref[k, 1, j]) for j in range(COLS)]
        rows = slice(first_row + k * 8, first_row + k * 8 + 8)
        for a, (re, im) in enumerate(fft(values, -1.0)):
            cs = tw_ref[0, a]
            sn = tw_ref[1, a]
            z_ref[0, a, rows, :] = re * cs - im * sn
            z_ref[1, a, rows, :] = re * sn + im * cs


def twist(place_ref, turn_ref, shift_ref, tw_ref):
    shifts = pl.ds(pl.multiple_of(place_ref[0] * 8, 8), 8)
    shift_re, shift_im = shift_ref[0, shifts, :], shift_ref[1, shifts, :]
    for a in range(COLS):
        cs, sn = turn_ref[0, a : a + 1, :], turn_ref[1, a : a + 1, :]
        tw_ref[0, a] = shift_re * cs - shift_im * sn
        tw_ref[1, a] = shift_re * sn + shift_im * cs


def late_kernel(
    place_ref, proto_ref, turn_ref, shift_ref, w_ref, x0_ref, x1_ref, o_ref, z_ref, tw_ref, f_ref
):
    twist(place_ref, turn_ref, shift_ref, tw_ref)
    transform_group(4, x0_ref, None, proto_ref, tw_ref, f_ref, z_ref, 0)
    transform_group(4, x1_ref, None, proto_ref, tw_ref, f_ref, z_ref, 32)
    send_columns(w_ref, z_ref, o_ref)


def first_kernel(
    place_ref, proto_ref, turn_ref, shift_ref, x_ref, h_ref, z_ref, tw_ref, f_ref
):
    twist(place_ref, turn_ref, shift_ref, tw_ref)
    transform_group(0, x_ref, h_ref, proto_ref, tw_ref, f_ref, z_ref, 0)


def second_kernel(
    place_ref,
    proto_ref,
    turn_ref,
    shift_ref,
    w_ref,
    x_ref,
    h_ref,
    first_ref,
    _,
    o_ref,
    z_ref,
    tw_ref,
    f_ref,
):
    twist(place_ref, turn_ref, shift_ref, tw_ref)
    for c in range(2):
        for a in range(COLS):
            z_ref[c, a, :32, :] = first_ref[c, a]
    transform_group(0, x_ref, h_ref, proto_ref, tw_ref, f_ref, z_ref, 32)
    send_columns(w_ref, z_ref, o_ref)


def send_columns(w_ref, z_ref, o_ref):
    seg = lax.broadcasted_iota(jnp.int32, (1, 8, 2 * LANES), 2) % LANES // 16
    bits = [(seg // (1 << t)) % 2 == 1 for t in range(3)]

    def some_columns(i, _):
        a0 = i * 4
        parts = []
        for c in range(2):
            rows = [
                z_ref[c, a0 + ai, pl.ds(mu, 8, stride=8), :] for mu in range(8) for ai in range(4)
            ]
            parts.append(jnp.concatenate(rows, axis=0).astype(jnp.bfloat16))
        z = jnp.concatenate(parts, axis=1)
        out = jnp.dot(z, w_ref[...], preferred_element_type=jnp.float32)
        out = out.reshape(8, 4, 8, 2 * LANES)
        v = [out[r] for r in range(8)]
        for t in range(3):
            mask = jnp.broadcast_to(bits[t], (4, 8, 2 * LANES))
            v = [jnp.where(mask, v[(r + (1 << t)) % 8], v[r]) for r in range(8)]
        for b in range(8):
            w = v[(-b) % 8].astype(jnp.bfloat16)
            for ai in range(4):
                a = a0 + ai
                dest = (a % 16) * 16 + 2 * b + a // 16
                for c in range(2):
                    o_ref[dest, 0, c] = w[ai, :, c * LANES : (c + 1) * LANES]
        return 0

    lax.fori_loop(0, 8, some_columns, 0)


def analysis(kernel, operands, half, earlier=None):
    specs = [pl.BlockSpec(memory_space=pltpu.SMEM)]
    specs += [pl.BlockSpec(memory_space=pltpu.VMEM)] * (len(operands) - 1)
    scratch = [
        pltpu.VMEM((2, COLS, 64, LANES), jnp.float32),
        pltpu.VMEM((2, COLS, 8, LANES), jnp.float32),
        pltpu.VMEM((4, 2, COLS, 8, LANES), jnp.float32),
    ]
    aliases = {}
    if half is None:
        out_spec = pl.BlockSpec(memory_space=pltpu.VMEM)
        out_shape = pltpu.VMEM((2, COLS, 32, LANES), jnp.float32)
        scratch = scratch[1:]
    else:
        out_spec = pl.BlockSpec((256, 1, 2, 8, LANES), lambda i: (0, half, 0, 0, 0))
        out_shape = jax.ShapeDtypeStruct((256, 2, 2, 8, LANES), jnp.bfloat16)
    if earlier is not None:
        aliases = {len(operands): 0}
        operands = [*operands, earlier]
        specs.append(pl.BlockSpec(memory_space=pl.ANY))
    return pl.pallas_call(
        kernel,
        grid=(1,),
        in_specs=specs,
        out_specs=out_spec,
        out_shape=out_shape,
        scratch_shapes=scratch,
        input_output_aliases=aliases,
        name=kernel.__name__,
        compiler_params=pltpu.CompilerParams(vmem_limit_bytes=VMEM_LIMIT),
    )(*operands)


def steer_kernel(b_ref, omega_ref, pos_ref, beam_ref, o_ref):
    e = pl.program_id(0)
    b = b_ref[0]
    lane = lax.broadcasted_iota(jnp.int32, (8, LANES), 1)
    inner = lane % 16

    def within(x, sh):
        return jnp.where(inner >= sh, pltpu.roll(x, sh, 1), pltpu.roll(x, sh + (LANES - 16), 1))

    coords = []
    for d in range(2):
        x = pltpu.roll(pos_ref[d], b * 16, 1)
        coords.append(jnp.where(lane // 16 < b, within(x, (e + 1) % 16), within(x, e)))
    omega = omega_ref[e]
    sin_b = jnp.broadcast_to(beam_ref[:, 0:1], (64, LANES))
    cos_b = jnp.broadcast_to(beam_ref[:, 1:2], (64, LANES))
    for i in range(8):
        turns = omega * (sin_b * coords[0][i : i + 1, :] + cos_b * coords[1][i : i + 1, :])
        rest = turns - jnp.round(turns)
        sq = rest * rest
        sn = rest * horner(SINE, sq)
        cs = horner(COSINE, sq)
        col = slice(i * LANES, (i + 1) * LANES)
        far = slice(1024 + i * LANES, 1024 + (i + 1) * LANES)
        o_ref[0, :, col] = (1.0 - 2.0 * sn * sn).astype(jnp.bfloat16)
        o_ref[0, :, far] = (-2.0 * sn * cs).astype(jnp.bfloat16)


def beam_kernel(b_ref, lam_ref, r_ref, far_ref, o_ref, x_ref, y_ref, m_ref, s_ref, sem_ref):
    step = pl.program_id(0)

    def steering(part):
        rows = pl.ds(part * 4, 4)
        return pltpu.make_async_copy(far_ref.at[rows], s_ref.at[rows], sem_ref.at[part])

    @pl.when(step == 0)
    def _():
        for part in range(4):
            steering(part).start()

    @pl.when(step < 4)
    def _():
        b = b_ref[0]
        lane = lax.broadcasted_iota(jnp.int32, (8, LANES), 1)
        low = lax.broadcasted_iota(jnp.int32, (8, LANES), 0) < 4
        shift = (lane % 16 - jnp.where(lane // 16 < b, 1, 0) + 16) % 16
        bits = [(shift // (1 << t)) % 2 == 1 for t in range(4)]

        def network(section, half, c):
            v = [r_ref[section, step, g, half, c].astype(jnp.float32) for g in range(16)]
            for t in range(4):
                v = [jnp.where(bits[t], v[(r + (1 << t)) % 16], v[r]) for r in range(16)]
            return v

        def separate(pair, _):
            top = pl.ds(pl.multiple_of(pair * 16, 16), 16)
            bot = pl.ds(pl.multiple_of(32 + pair * 16, 16), 16)
            near = [pl.multiple_of(step * 256 + mh * LANES, LANES) for mh in range(2)]
            far = [pl.multiple_of(1024 + step * 256 + mh * LANES, LANES) for mh in range(2)]
            for c in range(2):
                tiles = [[None] * 16, [None] * 16]
                for one in range(2):
                    v0 = network(pair * 2 + one, 0, c)
                    v1 = network(pair * 2 + one, 1, c)
                    for r in range(16):
                        first = jnp.where(low, v0[r], pltpu.roll(v1[r], 4, 0))
                        second = jnp.where(low, pltpu.roll(v0[r], 4, 0), v1[r])
                        for mh, value in enumerate((first, second)):
                            if one == 0:
                                tiles[mh][r] = value
                            else:
                                tiles[mh][r] = jnp.concatenate([tiles[mh][r], value], axis=0)
                for mh in range(2):
                    for e in range(16):
                        w = tiles[mh][(-e) % 16]
                        w16 = w.astype(jnp.bfloat16)
                        if c == 0:
                            x_ref[e, top, pl.ds(near[mh], LANES)] = w16
                            x_ref[e, bot, pl.ds(far[mh], LANES)] = w16
                        else:
                            x_ref[e, top, pl.ds(far[mh], LANES)] = w16
                            x_ref[e, bot, pl.ds(near[mh], LANES)] = (-w).astype(jnp.bfloat16)
            return 0

        lax.fori_loop(0, 2, separate, 0)

    @pl.when(step >= 4)
    def _():
        total = 1024.0
        snapshots = 32.0
        left = lax.broadcasted_iota(jnp.int32, (64, LANES), 1) < 64
        sign = jnp.where(lax.broadcasted_iota(jnp.int32, (64, LANES), 0) < 32, 1.0, -1.0)
        first = (step - 4) * 2
        steering(step - 4).wait()
        dims = (((1,), (1,)), ((), ()))
        hs, gs = [], []
        for i in range(2):
            x = x_ref[first + i]
            near = jnp.concatenate([s_ref[2 * first + i], x], axis=0)
            near = lax.dot_general(x, near, dims, preferred_element_type=jnp.float32)
            x = x_ref[first + i + 8]
            far = jnp.concatenate([x, s_ref[2 * first + i + 2]], axis=0)
            far = lax.dot_general(x, far, dims, preferred_element_type=jnp.float32)
            hs.append(jnp.where(left, near, far))
            gs.append(jnp.where(left, far, near))
        ghs = []
        for h, g in zip(hs, gs):
            both = jnp.concatenate([jnp.where(left, 0.0, h), jnp.where(left, h, 0.0)], axis=0)
            ghs.append(
                jnp.dot(g, both, precision=lax.Precision.HIGHEST, preferred_element_type=jnp.float32)
            )
        for i in range(2):
            h, gh = hs[i], ghs[i]
            lam = jnp.where(left[:1], lam_ref[first + i], lam_ref[first + i + 8])
            hh = jnp.sum(h * h, axis=0, keepdims=True)
            hgh = jnp.sum(h * gh, axis=0, keepdims=True)
            alpha = total / (hh / snapshots + lam * total)
            rho = 1.0 - alpha * lam
            t = alpha / snapshots
            new = rho * rho * total - 2.0 * rho * t * hh + t * t * hgh
            along = rho + new / total
            proj = along * h - t * gh
            size = along * along * total - 2.0 * along * t * hh + t * t * hgh
            curv = jnp.sum(proj * proj, axis=0, keepdims=True) / snapshots + lam * size
            alpha2 = new / curv
            main = alpha + alpha2 * along
            rest = alpha2 * t
            power = main * main * total - 2.0 * main * rest * hh + rest * rest * hgh
            norm = lax.rsqrt(power + total * 1e-6)
            y_ref[first + i] = sign * ((norm * main) * h - (norm * rest) * gh)

    @pl.when(step == 7)
    def _():
        left = lax.broadcasted_iota(jnp.int32, (64, LANES), 1) < 64
        lane = lax.broadcasted_iota(jnp.int32, (64, LANES), 1) % 64
        pick = jnp.where(lane == lax.broadcasted_iota(jnp.int32, (64, LANES), 0), 1.0, 0.0)
        pick = pick.astype(jnp.bfloat16)
        v = []
        for r in range(8):
            y = y_ref[r]
            both = jnp.concatenate([jnp.where(left, y, 0.0), jnp.where(left, 0.0, y)], axis=0)
            v.append(
                lax.dot_general(
                    pick,
                    both.astype(jnp.bfloat16),
                    (((1,), (1,)), ((), ())),
                    preferred_element_type=jnp.float32,
                )
            )
        v = swap_bits(v, 8)
        near = lax.broadcasted_iota(jnp.int32, (64, LANES), 1) % 8 < 4
        for section in range(4):
            rows = [v[section], v[4 + section]]
            if section:
                rows.append(
                    jnp.where(near, pltpu.roll(v[section - 1], LANES - 4, 1), v[4 + section - 1])
                )
            else:
                rows.append(jnp.zeros((64, LANES), jnp.float32))
            rows.append(jnp.zeros((64, LANES), jnp.float32))
            for r in range(4):
                m_ref[pl.ds(section * 256 + r, 64, stride=4), :] = rows[r]
        o_ref[...] = m_ref[...].astype(jnp.bfloat16)


def synthesis_kernel(m_ref, proto_ref, tw_ref, w_ref, o_ref, r_ref, l_ref, z_ref, s_ref):
    r_ref[...] = m_ref[...].astype(jnp.float32)
    for a_hi in range(2):
        tiles = []
        for r in range(3):
            groups = []
            for group in range(2):
                v = [
                    r_ref[pl.ds((group * 128 + 2 * b + a_hi) * 4 + r, 8, stride=64), :]
                    for b in range(8)
                ]
                groups.append(swap_bits(v, 1))
            tiles.append(
                [jnp.concatenate([groups[0][k], groups[1][k]], axis=0) for k in range(8)]
            )
        for k in range(8):
            rows = slice(k * COLS + a_hi * 16, k * COLS + a_hi * 16 + 16)
            l_ref[rows, :LANES] = tiles[0][k].astype(jnp.bfloat16)
            l_ref[rows, LANES:] = tiles[1][k].astype(jnp.bfloat16)
        for k in range(4):
            rows = slice((8 + k) * COLS + a_hi * 16, (8 + k) * COLS + a_hi * 16 + 16)
            l_ref[rows, :LANES] = tiles[2][k].astype(jnp.bfloat16)
            l_ref[rows, LANES:] = tiles[2][4 + k].astype(jnp.bfloat16)
    full = jnp.dot(l_ref[...], w_ref[...], preferred_element_type=jnp.float32)
    for c in range(2):
        cut = slice(c * LANES, (c + 1) * LANES)
        z_ref[c, : 8 * COLS] = full[: 8 * COLS, cut]
        z_ref[c, 8 * COLS : 12 * COLS] = jnp.zeros((4 * COLS, LANES), jnp.float32)
        z_ref[c, 12 * COLS :] = full[8 * COLS :, cut]

    def half(i, _):
        values = []
        for a in range(COLS):
            rows = pl.ds(i * (8 * COLS) + a, 8, stride=COLS)
            re = z_ref[0, rows, :]
            im = z_ref[1, rows, :]
            cs = tw_ref[0, a : a + 1, :]
            sn = tw_ref[1, a : a + 1, :]
            values.append((re * cs - im * sn, re * sn + im * cs))
        for j, (re, im) in enumerate(fft(values, 1.0)):
            s_ref[0, i, j] = re.astype(jnp.bfloat16).astype(jnp.float32)
            s_ref[1, i, j] = im.astype(jnp.bfloat16).astype(jnp.float32)
        return 0

    for i in range(2):
        half(i, 0)
    for c in range(2):
        for j in range(COLS):
            taps = [proto_ref[TAPS - 1 - p, j : j + 1, :] for p in range(TAPS)]
            out = filtered_rows(s_ref[c, 0, j], s_ref[c, 1, j], taps, 8)
            o_ref[c, 0, :, j * LANES : (j + 1) * LANES] = out.astype(jnp.bfloat16)


def body(samples, positions, beam_dir, load_exp):
    sections = lax.axis_size("section")
    groups = lax.axis_size("gx")
    device = lax.axis_index(AXES).astype(jnp.int32)
    spot = (device % 16)[None]

    proto = jnp.asarray(prototype_table())
    w_forward = jnp.asarray(forward_columns(), jnp.bfloat16)
    w_inverse = jnp.asarray(lane_transform(1.0, 1.0 / 64.0), jnp.bfloat16)

    samples = pltpu.with_memory_space_constraint(samples, pltpu.HBM)
    onward = [(i, i + 1) for i in range(sections - 1)]
    groups_x, groups_h = [], []
    for group in range(2):
        unpacked, last = unpack(spot, samples, group)
        hist = lax.ppermute(last, "section", onward)
        groups_x.append(unpacked)
        groups_h.append(pltpu.with_memory_space_constraint(hist, pltpu.VMEM))

    a_index, l_index = np.arange(COLS)[:, None], np.arange(LANES)[None, :]
    n_angle = 2.0 * np.pi / 4096.0 * a_index * l_index
    tw_inverse = jnp.asarray(np.stack([np.cos(n_angle), np.sin(n_angle)]), jnp.float32)
    turns = jnp.asarray(np.stack([np.cos(n_angle), -np.sin(n_angle)]), jnp.float32)
    s_angle = 2.0 * np.pi / LANES * ((np.arange(LANES)[:, None] * l_index) % LANES)
    shifts = jnp.asarray(np.stack([np.cos(s_angle), np.sin(s_angle)]), jnp.float32)
    tables = [spot, proto, turns, shifts]
    message = analysis(late_kernel, [*tables, w_forward, *groups_x], 1)
    first = analysis(first_kernel, [*tables, groups_x[0], groups_h[0]], None)
    message = analysis(
        second_kernel, [*tables, w_forward, groups_x[1], groups_h[1], first], 0, message
    )

    message, positions, load_exp, beam_dir, device = lax.optimization_barrier(
        (message, positions, load_exp, beam_dir, device)
    )
    own_b = (device % 16) // 2
    own_a = device // 16 + 16 * (device % 2)
    received = lax.all_to_all(message, AXES, 0, 0, tiled=True)

    devices = sections * groups
    exponents = load_exp.astype(jnp.float32)
    rows = [exponents]
    for t in range(1, 16):
        rows.append(lax.ppermute(exponents, AXES, [(i, i ^ (16 * t)) for i in range(devices)]))
    own = device // 16
    slots = jnp.arange(16, dtype=jnp.int32)
    picked = jnp.sum(jnp.stack(rows) * (slots == own)[None, :], axis=1)
    mine = jnp.sum(jnp.where((slots ^ own)[:, None] == slots[None, :], picked[None, :], 0.0), axis=1)
    lam = jnp.exp2(mine)

    spread = positions.reshape(2, 4, 16, 2, 8).transpose(0, 1, 3, 4, 2).reshape(2, 8, LANES)
    channel = own_a + 32 * own_b + 256 * jnp.arange(16, dtype=jnp.int32)
    angular = 0.75 + 0.5 * channel.astype(jnp.float32) / 4096
    beams = beam_dir.shape[0]
    angle_beam = math.pi / beams * (beam_dir.astype(jnp.float32) + 0.5) - 0.5 * math.pi
    directions = jnp.stack([jnp.sin(angle_beam), jnp.cos(angle_beam)], axis=1)
    steer = pl.pallas_call(
        steer_kernel,
        grid=(16,),
        in_specs=[
            pl.BlockSpec(memory_space=pltpu.SMEM),
            pl.BlockSpec(memory_space=pltpu.SMEM),
            pl.BlockSpec((2, 8, LANES), lambda e: (0, 0, 0)),
            pl.BlockSpec((beams, 2), lambda e: (0, 0)),
        ],
        out_specs=pl.BlockSpec(
            (1, beams, 2048), lambda e: (4 * ((e % 8) // 2) + e % 2 + 2 * (e // 8), 0, 0)
        ),
        out_shape=jax.ShapeDtypeStruct((16, beams, 2048), jnp.bfloat16),
        name="steer",
        compiler_params=pltpu.CompilerParams(vmem_limit_bytes=VMEM_LIMIT),
    )(own_b[None], angular, spread, directions)

    steer = pltpu.with_memory_space_constraint(steer, pltpu.HBM)
    received = pltpu.with_memory_space_constraint(
        received.reshape(4, 4, 16, 2, 2, 8, LANES), pltpu.VMEM
    )
    back = pl.pallas_call(
        beam_kernel,
        grid=(8,),
        in_specs=[
            pl.BlockSpec(memory_space=pltpu.SMEM),
            pl.BlockSpec(memory_space=pltpu.SMEM),
            pl.BlockSpec(memory_space=pltpu.VMEM),
            pl.BlockSpec(memory_space=pl.ANY),
        ],
        out_specs=pl.BlockSpec((4 * devices, LANES), lambda i: (0, 0)),
        out_shape=jax.ShapeDtypeStruct((4 * devices, LANES), jnp.bfloat16),
        scratch_shapes=[
            pltpu.VMEM((16, 64, 2048), jnp.bfloat16),
            pltpu.VMEM((8, 64, LANES), jnp.float32),
            pltpu.VMEM((4 * devices, LANES), jnp.float32),
            pltpu.VMEM((16, beams, 2048), jnp.bfloat16),
            pltpu.SemaphoreType.DMA((4,)),
        ],
        name="beams",
        compiler_params=pltpu.CompilerParams(vmem_limit_bytes=VMEM_LIMIT),
    )(own_b[None], lam, received, steer)

    returned = lax.all_to_all(back.reshape(devices, 4, LANES), AXES, 0, 0, tiled=True)
    return pl.pallas_call(
        synthesis_kernel,
        in_specs=[pl.BlockSpec(memory_space=pltpu.VMEM)] * 4,
        out_specs=pl.BlockSpec(memory_space=pltpu.VMEM),
        out_shape=jax.ShapeDtypeStruct((2, 1, 8, 4096), jnp.bfloat16),
        scratch_shapes=[
            pltpu.VMEM((4 * devices, LANES), jnp.float32),
            pltpu.VMEM((12 * COLS, 2 * LANES), jnp.bfloat16),
            pltpu.VMEM((2, 16 * COLS, LANES), jnp.float32),
            pltpu.VMEM((2, 2, COLS, 8, LANES), jnp.float32),
        ],
        name="synthesis",
        compiler_params=pltpu.CompilerParams(vmem_limit_bytes=VMEM_LIMIT),
    )(returned.reshape(4 * devices, LANES), proto, tw_inverse, w_inverse)


def solution(mesh):
    placed = (P(None, "gx", "section", None), P(), P(), P(AXES))
    return jax.shard_map(
        body, mesh=mesh, in_specs=placed, out_specs=P(None, "gx", "section", None), check_vma=False
    )
```

```python
import math

import numpy as np
import jax
import jax.numpy as jnp
from jax import lax
from jax.experimental import pallas as pl
from jax.experimental.pallas import tpu as pltpu
from jax.sharding import PartitionSpec as P

TAPS = 4
LANES = 128
COLS = 32
AXES = ("section", "gx")
VMEM_LIMIT = 32 << 20
SINE = [(-1.0) ** i * math.pi ** (2 * i + 1) / math.factorial(2 * i + 1) for i in range(6)]
COSINE = [(-1.0) ** i * math.pi ** (2 * i) / math.factorial(2 * i) for i in range(6)]


def horner(coefficients, x):
    out = coefficients[-1]
    for value in reversed(coefficients[:-1]):
        out = out * x + value
    return out


def prototype_table():
    total = TAPS * COLS * LANES
    position = np.arange(total, dtype=np.float64) + 0.5
    window = 0.5 - 0.5 * np.cos(2.0 * np.pi / total * position)
    shaped = np.sinc((position - 0.5 * total) / (COLS * LANES)) * window
    return shaped.reshape(TAPS, COLS, LANES).astype(np.float32)


def lane_transform(sign, scale):
    l = np.arange(LANES)
    angle = 2.0 * np.pi * ((l[:, None] * l[None, :]) % LANES) / LANES
    c, s = np.cos(angle) * scale, sign * np.sin(angle) * scale
    return np.block([[c, s], [-s, c]])


def forward_columns():
    lane = np.arange(LANES)
    order = (lane // 16) + 8 * (lane % 16)
    table = lane_transform(-1.0, 1.0 / 64.0)
    return table[:, np.concatenate([order, LANES + order])]


def swap_bits(v, distance):
    lane = lax.broadcasted_iota(jnp.int32, v[0].shape, len(v[0].shape) - 1)
    for t in range(3):
        step = distance << t
        mask = (lane // step) % 2 == 1
        out = list(v)
        for low in range(8):
            if low & (1 << t):
                continue
            high = low | (1 << t)
            out[low] = jnp.where(mask, pltpu.roll(v[high], step, 1), v[low])
            out[high] = jnp.where(mask, v[high], pltpu.roll(v[low], LANES - step, 1))
        v = out
    return v


def twiddle(re, im, k, n, sign):
    k = k % n
    if k == 0:
        return re, im
    if 4 * k == n:
        return (im, -re) if sign < 0 else (-im, re)
    if 8 * k == n:
        c = math.sqrt(0.5)
        return ((re + im) * c, (im - re) * c) if sign < 0 else ((re - im) * c, (im + re) * c)
    if 8 * k == 3 * n:
        c = math.sqrt(0.5)
        return ((im - re) * c, (-im - re) * c) if sign < 0 else ((-re - im) * c, (re - im) * c)
    c, s = math.cos(2 * math.pi * k / n), sign * math.sin(2 * math.pi * k / n)
    return re * c - im * s, re * s + im * c


def fft(values, sign):
    n = len(values)
    if n == 1:
        return values
    even = fft(values[0::2], sign)
    odd = fft(values[1::2], sign)
    low, high = [], []
    for k in range(n // 2):
        tr, ti = twiddle(odd[k][0], odd[k][1], k, n, sign)
        er, ei = even[k]
        low.append((er + tr, ei + ti))
        high.append((er - tr, ei - ti))
    return low + high


def filtered_rows(now, before, taps, period):
    row = lax.broadcasted_iota(jnp.int32, now.shape, 0) % period
    out = taps[0] * now
    for p in range(1, TAPS):
        out = out + taps[p] * pltpu.roll(jnp.where(row >= period - p, before, now), p, 0)
    return out


def unpack_kernel(place_ref, x_ref, xs_ref, h_ref):
    i = pl.program_id(0)
    for j in range(COLS // 2):
        at = i * (COLS // 2) + j
        for c in range(2):
            for m in range(8):
                value = x_ref[c, m, :, j * LANES : (j + 1) * LANES]
                xs_ref[c, at, m * 8 : m * 8 + 8, :] = value.astype(jnp.float32)
            for t in range(TAPS - 1):
                value = xs_ref[c, at, pl.ds(8 - (TAPS - 1) + t, 8, stride=8), :]
                h_ref[c, t, :, pl.ds(pl.multiple_of(at * LANES, LANES), LANES)] = value.astype(
                    jnp.bfloat16
                )


def unpack(place, samples, group):
    return pl.pallas_call(
        unpack_kernel,
        grid=(2,),
        in_specs=[
            pl.BlockSpec(memory_space=pltpu.SMEM),
            pl.BlockSpec((2, 8, 8, COLS // 2 * LANES), lambda i: (0, group, 0, i)),
        ],
        out_specs=[pl.BlockSpec(memory_space=pltpu.VMEM)] * 2,
        out_shape=[
            pltpu.VMEM((2, COLS, 64, LANES), jnp.float32),
            pltpu.VMEM((2, TAPS - 1, 8, COLS * LANES), jnp.bfloat16),
        ],
        name=f"unpack_{group}",
        compiler_params=pltpu.CompilerParams(vmem_limit_bytes=VMEM_LIMIT),
    )(place, samples)


def transform_group(start, x_ref, h_ref, proto_ref, tw_ref, f_ref, z_ref, first_row):
    def block(c, j, k):
        if k < 0:
            cut = slice(j * LANES, (j + 1) * LANES)
            return h_ref[c, TAPS - 1 + k, :, cut].astype(jnp.float32)
        return x_ref[c, j, pl.ds(k, 8, stride=8), :]

    for j in range(COLS):
        taps = [proto_ref[p, j : j + 1, :] for p in range(TAPS)]
        for c in range(2):
            blocks = [block(c, j, start - (TAPS - 1) + t) for t in range(TAPS + 3)]
            for k in range(4):
                out = taps[0] * blocks[k + 3]
                for p in range(1, TAPS):
                    out = out + taps[p] * blocks[k + 3 - p]
                f_ref[k, c, j] = out
    for k in range(4):
        values = [(f_ref[k, 0, j], f_ref[k, 1, j]) for j in range(COLS)]
        rows = slice(first_row + k * 8, first_row + k * 8 + 8)
        for a, (re, im) in enumerate(fft(values, -1.0)):
            cs = tw_ref[0, a]
            sn = tw_ref[1, a]
            z_ref[0, a, rows, :] = re * cs - im * sn
            z_ref[1, a, rows, :] = re * sn + im * cs


def twist(place_ref, turn_ref, shift_ref, tw_ref):
    shifts = pl.ds(pl.multiple_of(place_ref[0] * 8, 8), 8)
    shift_re, shift_im = shift_ref[0, shifts, :], shift_ref[1, shifts, :]
    for a in range(COLS):
        cs, sn = turn_ref[0, a : a + 1, :], turn_ref[1, a : a + 1, :]
        tw_ref[0, a] = shift_re * cs - shift_im * sn
        tw_ref[1, a] = shift_re * sn + shift_im * cs


def late_kernel(
    place_ref,
    proto_ref,
    turn_ref,
    shift_ref,
    w_ref,
    x0_ref,
    x1_ref,
    o_ref,
    z_ref,
    tw_ref,
    f_ref,
    stage_ref,
    sem_ref,
):
    twist(place_ref, turn_ref, shift_ref, tw_ref)
    transform_group(4, x0_ref, None, proto_ref, tw_ref, f_ref, z_ref, 0)
    transform_group(4, x1_ref, None, proto_ref, tw_ref, f_ref, z_ref, 32)
    send_columns(w_ref, z_ref, o_ref, 1, stage_ref, sem_ref)


def first_kernel(
    place_ref, proto_ref, turn_ref, shift_ref, x_ref, h_ref, z_ref, tw_ref, f_ref
):
    twist(place_ref, turn_ref, shift_ref, tw_ref)
    transform_group(0, x_ref, h_ref, proto_ref, tw_ref, f_ref, z_ref, 0)


def second_kernel(
    place_ref,
    proto_ref,
    turn_ref,
    shift_ref,
    w_ref,
    x_ref,
    h_ref,
    first_ref,
    _,
    o_ref,
    z_ref,
    tw_ref,
    f_ref,
    stage_ref,
    sem_ref,
):
    twist(place_ref, turn_ref, shift_ref, tw_ref)
    for c in range(2):
        for a in range(COLS):
            z_ref[c, a, :32, :] = first_ref[c, a]
    transform_group(0, x_ref, h_ref, proto_ref, tw_ref, f_ref, z_ref, 32)
    send_columns(w_ref, z_ref, o_ref, 0, stage_ref, sem_ref)


def send_columns(w_ref, z_ref, o_ref, half, stage_ref, sem_ref):
    def leave(i):
        rows = pl.ds((i % 4) * 4, 4)
        return pltpu.make_async_copy(
            stage_ref.at[i], o_ref.at[rows, :, i // 4, half], sem_ref.at[i]
        )

    seg = lax.broadcasted_iota(jnp.int32, (1, 8, 2 * LANES), 2) % LANES // 16
    bits = [(seg // (1 << t)) % 2 == 1 for t in range(3)]

    def some_columns(i, _):
        a0 = i * 4
        parts = []
        for c in range(2):
            rows = [
                z_ref[c, a0 + ai, pl.ds(mu, 8, stride=8), :] for mu in range(8) for ai in range(4)
            ]
            parts.append(jnp.concatenate(rows, axis=0).astype(jnp.bfloat16))
        z = jnp.concatenate(parts, axis=1)
        out = jnp.dot(z, w_ref[...], preferred_element_type=jnp.float32)
        out = out.reshape(8, 4, 8, 2 * LANES)
        v = [out[r] for r in range(8)]
        for t in range(3):
            mask = jnp.broadcast_to(bits[t], (4, 8, 2 * LANES))
            v = [jnp.where(mask, v[(r + (1 << t)) % 8], v[r]) for r in range(8)]
        for b in range(8):
            w = v[(-b) % 8].astype(jnp.bfloat16)
            for ai in range(4):
                for c in range(2):
                    stage_ref[i, ai, b, c] = w[ai, :, c * LANES : (c + 1) * LANES]
        leave(i).start()
        return 0

    lax.fori_loop(0, 8, some_columns, 0)
    for i in range(8):
        leave(i).wait()


def analysis(kernel, operands, sends, earlier=None):
    specs = [pl.BlockSpec(memory_space=pltpu.SMEM)]
    specs += [pl.BlockSpec(memory_space=pltpu.VMEM)] * (len(operands) - 1)
    scratch = [
        pltpu.VMEM((2, COLS, 64, LANES), jnp.float32),
        pltpu.VMEM((2, COLS, 8, LANES), jnp.float32),
        pltpu.VMEM((4, 2, COLS, 8, LANES), jnp.float32),
    ]
    aliases = {}
    if not sends:
        out_spec = pl.BlockSpec(memory_space=pltpu.VMEM)
        out_shape = pltpu.VMEM((2, COLS, 32, LANES), jnp.float32)
        scratch = scratch[1:]
    else:
        out_spec = pl.BlockSpec(memory_space=pl.ANY)
        out_shape = jax.ShapeDtypeStruct((16, 8, 2, 2, 2, 8, LANES), jnp.bfloat16)
        scratch.append(pltpu.VMEM((8, 4, 8, 2, 8, LANES), jnp.bfloat16))
        scratch.append(pltpu.SemaphoreType.DMA((8,)))
    if earlier is not None:
        aliases = {len(operands): 0}
        operands = [*operands, earlier]
        specs.append(pl.BlockSpec(memory_space=pl.ANY))
    return pl.pallas_call(
        kernel,
        grid=(1,),
        in_specs=specs,
        out_specs=out_spec,
        out_shape=out_shape,
        scratch_shapes=scratch,
        input_output_aliases=aliases,
        name=kernel.__name__,
        compiler_params=pltpu.CompilerParams(vmem_limit_bytes=VMEM_LIMIT),
    )(*operands)


def steer_kernel(b_ref, omega_ref, pos_ref, beam_ref, o_ref):
    e = pl.program_id(0)
    b = b_ref[0]
    lane = lax.broadcasted_iota(jnp.int32, (8, LANES), 1)
    inner = lane % 16

    def within(x, sh):
        return jnp.where(inner >= sh, pltpu.roll(x, sh, 1), pltpu.roll(x, sh + (LANES - 16), 1))

    coords = []
    for d in range(2):
        x = pltpu.roll(pos_ref[d], b * 16, 1)
        coords.append(jnp.where(lane // 16 < b, within(x, (e + 1) % 16), within(x, e)))
    omega = omega_ref[e]
    sin_b = jnp.broadcast_to(beam_ref[:, 0:1], (64, LANES))
    cos_b = jnp.broadcast_to(beam_ref[:, 1:2], (64, LANES))
    for i in range(8):
        turns = omega * (sin_b * coords[0][i : i + 1, :] + cos_b * coords[1][i : i + 1, :])
        rest = turns - jnp.round(turns)
        sq = rest * rest
        sn = rest * horner(SINE, sq)
        cs = horner(COSINE, sq)
        col = slice(i * LANES, (i + 1) * LANES)
        far = slice(1024 + i * LANES, 1024 + (i + 1) * LANES)
        o_ref[0, :, col] = (1.0 - 2.0 * sn * sn).astype(jnp.bfloat16)
        o_ref[0, :, far] = (-2.0 * sn * cs).astype(jnp.bfloat16)


def beam_kernel(b_ref, lam_ref, r_ref, far_ref, o_ref, x_ref, y_ref, m_ref, s_ref, sem_ref):
    step = pl.program_id(0)

    def steering(part):
        rows = pl.ds(part * 4, 4)
        return pltpu.make_async_copy(far_ref.at[rows], s_ref.at[rows], sem_ref.at[part])

    @pl.when(step == 0)
    def _():
        for part in range(4):
            steering(part).start()

    @pl.when(step < 4)
    def _():
        b = b_ref[0]
        lane = lax.broadcasted_iota(jnp.int32, (8, LANES), 1)
        low = lax.broadcasted_iota(jnp.int32, (8, LANES), 0) < 4
        shift = (lane % 16 - jnp.where(lane // 16 < b, 1, 0) + 16) % 16
        bits = [(shift // (1 << t)) % 2 == 1 for t in range(4)]

        def network(section, half, c):
            v = [r_ref[section, step, g, half, c].astype(jnp.float32) for g in range(16)]
            for t in range(4):
                v = [jnp.where(bits[t], v[(r + (1 << t)) % 16], v[r]) for r in range(16)]
            return v

        def separate(pair, _):
            top = pl.ds(pl.multiple_of(pair * 16, 16), 16)
            bot = pl.ds(pl.multiple_of(32 + pair * 16, 16), 16)
            near = [pl.multiple_of(step * 256 + mh * LANES, LANES) for mh in range(2)]
            far = [pl.multiple_of(1024 + step * 256 + mh * LANES, LANES) for mh in range(2)]
            for c in range(2):
                tiles = [[None] * 16, [None] * 16]
                for one in range(2):
                    v0 = network(pair * 2 + one, 0, c)
                    v1 = network(pair * 2 + one, 1, c)
                    for r in range(16):
                        first = jnp.where(low, v0[r], pltpu.roll(v1[r], 4, 0))
                        second = jnp.where(low, pltpu.roll(v0[r], 4, 0), v1[r])
                        for mh, value in enumerate((first, second)):
                            if one == 0:
                                tiles[mh][r] = value
                            else:
                                tiles[mh][r] = jnp.concatenate([tiles[mh][r], value], axis=0)
                for mh in range(2):
                    for e in range(16):
                        w = tiles[mh][(-e) % 16]
                        w16 = w.astype(jnp.bfloat16)
                        if c == 0:
                            x_ref[e, top, pl.ds(near[mh], LANES)] = w16
                            x_ref[e, bot, pl.ds(far[mh], LANES)] = w16
                        else:
                            x_ref[e, top, pl.ds(far[mh], LANES)] = w16
                            x_ref[e, bot, pl.ds(near[mh], LANES)] = (-w).astype(jnp.bfloat16)
            return 0

        lax.fori_loop(0, 2, separate, 0)

    @pl.when(step >= 4)
    def _():
        total = 1024.0
        snapshots = 32.0
        left = lax.broadcasted_iota(jnp.int32, (64, LANES), 1) < 64
        sign = jnp.where(lax.broadcasted_iota(jnp.int32, (64, LANES), 0) < 32, 1.0, -1.0)
        base = (step - 4) * 4
        for part in range(2):
            steering((step - 4) * 2 + part).wait()
        dims = (((1,), (1,)), ((), ()))
        hs, gs = [], []
        for i in range(4):
            spot = (step - 4) * 8 + (i // 2) * 4 + i % 2
            x = x_ref[base + i]
            near = jnp.concatenate([s_ref[spot], x], axis=0)
            near = lax.dot_general(x, near, dims, preferred_element_type=jnp.float32)
            x = x_ref[base + i + 8]
            far = jnp.concatenate([x, s_ref[spot + 2]], axis=0)
            far = lax.dot_general(x, far, dims, preferred_element_type=jnp.float32)
            hs.append(jnp.where(left, near, far))
            gs.append(jnp.where(left, far, near))
        ghs = []
        for h, g in zip(hs, gs):
            g_high = g.astype(jnp.bfloat16)
            g_low = (g - g_high.astype(jnp.float32)).astype(jnp.bfloat16)
            high = h.astype(jnp.bfloat16).astype(jnp.float32)
            parts = []
            for part in (high, h - high):
                both = [jnp.where(left, 0.0, part), jnp.where(left, part, 0.0)]
                parts.append(jnp.concatenate(both, axis=0).astype(jnp.bfloat16))
            left_side = jnp.concatenate([g_high, g_high, g_low], axis=1)
            right_side = jnp.concatenate([parts[0], parts[1], parts[0]], axis=0)
            ghs.append(jnp.dot(left_side, right_side, preferred_element_type=jnp.float32))
        for i in range(4):
            h, gh = hs[i], ghs[i]
            lam = jnp.where(left[:1], lam_ref[base + i], lam_ref[base + i + 8])
            hh = jnp.sum(h * h, axis=0, keepdims=True)
            hgh = jnp.sum(h * gh, axis=0, keepdims=True)
            alpha = total / (hh / snapshots + lam * total)
            rho = 1.0 - alpha * lam
            t = alpha / snapshots
            new = rho * rho * total - 2.0 * rho * t * hh + t * t * hgh
            along = rho + new / total
            proj = along * h - t * gh
            size = along * along * total - 2.0 * along * t * hh + t * t * hgh
            curv = jnp.sum(proj * proj, axis=0, keepdims=True) / snapshots + lam * size
            alpha2 = new / curv
            main = alpha + alpha2 * along
            rest = alpha2 * t
            power = main * main * total - 2.0 * main * rest * hh + rest * rest * hgh
            norm = lax.rsqrt(power + total * 1e-6)
            y_ref[base + i] = sign * ((norm * main) * h - (norm * rest) * gh)

    @pl.when(step == 5)
    def _():
        left = lax.broadcasted_iota(jnp.int32, (64, LANES), 1) < 64
        lane = lax.broadcasted_iota(jnp.int32, (64, LANES), 1) % 64
        pick = jnp.where(lane == lax.broadcasted_iota(jnp.int32, (64, LANES), 0), 1.0, 0.0)
        pick = pick.astype(jnp.bfloat16)
        v = []
        for r in range(8):
            y = y_ref[r]
            both = jnp.concatenate([jnp.where(left, y, 0.0), jnp.where(left, 0.0, y)], axis=0)
            v.append(
                lax.dot_general(
                    pick,
                    both.astype(jnp.bfloat16),
                    (((1,), (1,)), ((), ())),
                    preferred_element_type=jnp.float32,
                )
            )
        v = swap_bits(v, 8)
        near = lax.broadcasted_iota(jnp.int32, (64, LANES), 1) % 8 < 4
        for section in range(4):
            rows = [v[section], v[4 + section]]
            if section:
                rows.append(
                    jnp.where(near, pltpu.roll(v[section - 1], LANES - 4, 1), v[4 + section - 1])
                )
            else:
                rows.append(jnp.zeros((64, LANES), jnp.float32))
            rows.append(jnp.zeros((64, LANES), jnp.float32))
            for r in range(4):
                m_ref[pl.ds(section * 256 + r, 64, stride=4), :] = rows[r]
        o_ref[...] = m_ref[...].astype(jnp.bfloat16)


def synthesis_kernel(m_ref, proto_ref, tw_ref, w_ref, o_ref, r_ref, l_ref, z_ref, s_ref):
    r_ref[...] = m_ref[...].astype(jnp.float32)
    for a_hi in range(2):
        tiles = []
        for r in range(3):
            groups = []
            for group in range(2):
                v = [
                    r_ref[pl.ds((group * 128 + 2 * b + a_hi) * 4 + r, 8, stride=64), :]
                    for b in range(8)
                ]
                groups.append(swap_bits(v, 1))
            tiles.append(
                [jnp.concatenate([groups[0][k], groups[1][k]], axis=0) for k in range(8)]
            )
        for k in range(8):
            rows = slice(k * COLS + a_hi * 16, k * COLS + a_hi * 16 + 16)
            l_ref[rows, :LANES] = tiles[0][k].astype(jnp.bfloat16)
            l_ref[rows, LANES:] = tiles[1][k].astype(jnp.bfloat16)
        for k in range(4):
            rows = slice((8 + k) * COLS + a_hi * 16, (8 + k) * COLS + a_hi * 16 + 16)
            l_ref[rows, :LANES] = tiles[2][k].astype(jnp.bfloat16)
            l_ref[rows, LANES:] = tiles[2][4 + k].astype(jnp.bfloat16)
    full = jnp.dot(l_ref[...], w_ref[...], preferred_element_type=jnp.float32)
    for c in range(2):
        cut = slice(c * LANES, (c + 1) * LANES)
        z_ref[c, : 8 * COLS] = full[: 8 * COLS, cut]
        z_ref[c, 8 * COLS : 12 * COLS] = jnp.zeros((4 * COLS, LANES), jnp.float32)
        z_ref[c, 12 * COLS :] = full[8 * COLS :, cut]

    def half(i, _):
        values = []
        for a in range(COLS):
            rows = pl.ds(i * (8 * COLS) + a, 8, stride=COLS)
            re = z_ref[0, rows, :]
            im = z_ref[1, rows, :]
            cs = tw_ref[0, a : a + 1, :]
            sn = tw_ref[1, a : a + 1, :]
            values.append((re * cs - im * sn, re * sn + im * cs))
        for j, (re, im) in enumerate(fft(values, 1.0)):
            s_ref[0, i, j] = re.astype(jnp.bfloat16).astype(jnp.float32)
            s_ref[1, i, j] = im.astype(jnp.bfloat16).astype(jnp.float32)
        return 0

    for i in range(2):
        half(i, 0)
    for c in range(2):
        for j in range(COLS):
            taps = [proto_ref[TAPS - 1 - p, j : j + 1, :] for p in range(TAPS)]
            out = filtered_rows(s_ref[c, 0, j], s_ref[c, 1, j], taps, 8)
            o_ref[c, 0, :, j * LANES : (j + 1) * LANES] = out.astype(jnp.bfloat16)


def body(samples, positions, beam_dir, load_exp):
    sections = lax.axis_size("section")
    groups = lax.axis_size("gx")
    device = lax.axis_index(AXES).astype(jnp.int32)
    spot = (device % 16)[None]

    proto = jnp.asarray(prototype_table())
    w_forward = jnp.asarray(forward_columns(), jnp.bfloat16)
    w_inverse = jnp.asarray(lane_transform(1.0, 1.0 / 64.0), jnp.bfloat16)

    samples = pltpu.with_memory_space_constraint(samples, pltpu.HBM)
    onward = [(i, i + 1) for i in range(sections - 1)]
    groups_x, groups_h = [], []
    for group in range(2):
        unpacked, last = unpack(spot, samples, group)
        hist = lax.ppermute(last, "section", onward)
        groups_x.append(unpacked)
        groups_h.append(pltpu.with_memory_space_constraint(hist, pltpu.VMEM))

    a_index, l_index = np.arange(COLS)[:, None], np.arange(LANES)[None, :]
    n_angle = 2.0 * np.pi / 4096.0 * a_index * l_index
    tw_inverse = jnp.asarray(np.stack([np.cos(n_angle), np.sin(n_angle)]), jnp.float32)
    turns = jnp.asarray(np.stack([np.cos(n_angle), -np.sin(n_angle)]), jnp.float32)
    s_angle = 2.0 * np.pi / LANES * ((np.arange(LANES)[:, None] * l_index) % LANES)
    shifts = jnp.asarray(np.stack([np.cos(s_angle), np.sin(s_angle)]), jnp.float32)
    tables = [spot, proto, turns, shifts]
    message = analysis(late_kernel, [*tables, w_forward, *groups_x], True)
    first = analysis(first_kernel, [*tables, groups_x[0], groups_h[0]], False)
    message = analysis(
        second_kernel, [*tables, w_forward, groups_x[1], groups_h[1], first], True, message
    )

    message, positions, load_exp, beam_dir, device = lax.optimization_barrier(
        (message, positions, load_exp, beam_dir, device)
    )
    own_b = (device % 16) // 2
    own_a = device // 16 + 16 * (device % 2)
    received = lax.all_to_all(
        message.reshape(256, 2, 2, 8, LANES), AXES, 0, 0, tiled=True
    )

    devices = sections * groups
    exponents = load_exp.astype(jnp.float32)
    rows = [exponents]
    for t in range(1, 16):
        rows.append(lax.ppermute(exponents, AXES, [(i, i ^ (16 * t)) for i in range(devices)]))
    own = device // 16
    slots = jnp.arange(16, dtype=jnp.int32)
    picked = jnp.sum(jnp.stack(rows) * (slots == own)[None, :], axis=1)
    mine = jnp.sum(jnp.where((slots ^ own)[:, None] == slots[None, :], picked[None, :], 0.0), axis=1)
    lam = jnp.exp2(mine)

    spread = positions.reshape(2, 4, 16, 2, 8).transpose(0, 1, 3, 4, 2).reshape(2, 8, LANES)
    channel = own_a + 32 * own_b + 256 * jnp.arange(16, dtype=jnp.int32)
    angular = 0.75 + 0.5 * channel.astype(jnp.float32) / 4096
    beams = beam_dir.shape[0]
    angle_beam = math.pi / beams * (beam_dir.astype(jnp.float32) + 0.5) - 0.5 * math.pi
    directions = jnp.stack([jnp.sin(angle_beam), jnp.cos(angle_beam)], axis=1)
    steer = pl.pallas_call(
        steer_kernel,
        grid=(16,),
        in_specs=[
            pl.BlockSpec(memory_space=pltpu.SMEM),
            pl.BlockSpec(memory_space=pltpu.SMEM),
            pl.BlockSpec((2, 8, LANES), lambda e: (0, 0, 0)),
            pl.BlockSpec((beams, 2), lambda e: (0, 0)),
        ],
        out_specs=pl.BlockSpec(
            (1, beams, 2048), lambda e: (4 * ((e % 8) // 2) + e % 2 + 2 * (e // 8), 0, 0)
        ),
        out_shape=jax.ShapeDtypeStruct((16, beams, 2048), jnp.bfloat16),
        name="steer",
        compiler_params=pltpu.CompilerParams(vmem_limit_bytes=VMEM_LIMIT),
    )(own_b[None], angular, spread, directions)

    steer = pltpu.with_memory_space_constraint(steer, pltpu.HBM)
    received = pltpu.with_memory_space_constraint(
        received.reshape(4, 4, 16, 2, 2, 8, LANES), pltpu.VMEM
    )
    back = pl.pallas_call(
        beam_kernel,
        grid=(6,),
        in_specs=[
            pl.BlockSpec(memory_space=pltpu.SMEM),
            pl.BlockSpec(memory_space=pltpu.SMEM),
            pl.BlockSpec(memory_space=pltpu.VMEM),
            pl.BlockSpec(memory_space=pl.ANY),
        ],
        out_specs=pl.BlockSpec((4 * devices, LANES), lambda i: (0, 0)),
        out_shape=jax.ShapeDtypeStruct((4 * devices, LANES), jnp.bfloat16),
        scratch_shapes=[
            pltpu.VMEM((16, 64, 2048), jnp.bfloat16),
            pltpu.VMEM((8, 64, LANES), jnp.float32),
            pltpu.VMEM((4 * devices, LANES), jnp.float32),
            pltpu.VMEM((16, beams, 2048), jnp.bfloat16),
            pltpu.SemaphoreType.DMA((4,)),
        ],
        name="beams",
        compiler_params=pltpu.CompilerParams(vmem_limit_bytes=VMEM_LIMIT),
    )(own_b[None], lam, received, steer)

    returned = lax.all_to_all(back.reshape(devices, 4, LANES), AXES, 0, 0, tiled=True)
    return pl.pallas_call(
        synthesis_kernel,
        in_specs=[pl.BlockSpec(memory_space=pltpu.VMEM)] * 4,
        out_specs=pl.BlockSpec(memory_space=pltpu.VMEM),
        out_shape=jax.ShapeDtypeStruct((2, 1, 8, 4096), jnp.bfloat16),
        scratch_shapes=[
            pltpu.VMEM((4 * devices, LANES), jnp.float32),
            pltpu.VMEM((12 * COLS, 2 * LANES), jnp.bfloat16),
            pltpu.VMEM((2, 16 * COLS, LANES), jnp.float32),
            pltpu.VMEM((2, 2, COLS, 8, LANES), jnp.float32),
        ],
        name="synthesis",
        compiler_params=pltpu.CompilerParams(vmem_limit_bytes=VMEM_LIMIT),
    )(returned.reshape(4 * devices, LANES), proto, tw_inverse, w_inverse)


def solution(mesh):
    placed = (P(None, "gx", "section", None), P(), P(), P(AXES))
    return jax.shard_map(
        body, mesh=mesh, in_specs=placed, out_specs=P(None, "gx", "section", None), check_vma=False
    )
```

```python
import math

import numpy as np
import jax
import jax.numpy as jnp
from jax import lax
from jax.experimental import pallas as pl
from jax.experimental.pallas import tpu as pltpu
from jax.sharding import PartitionSpec as P

TAPS = 4
LANES = 128
COLS = 32
AXES = ("section", "gx")
VMEM_LIMIT = 32 << 20
SINE = [(-1.0) ** i * math.pi ** (2 * i + 1) / math.factorial(2 * i + 1) for i in range(6)]
COSINE = [(-1.0) ** i * math.pi ** (2 * i) / math.factorial(2 * i) for i in range(6)]


def horner(coefficients, x):
    out = coefficients[-1]
    for value in reversed(coefficients[:-1]):
        out = out * x + value
    return out


def prototype_table():
    total = TAPS * COLS * LANES
    position = np.arange(total, dtype=np.float64) + 0.5
    window = 0.5 - 0.5 * np.cos(2.0 * np.pi / total * position)
    shaped = np.sinc((position - 0.5 * total) / (COLS * LANES)) * window
    return shaped.reshape(TAPS, COLS, LANES).astype(np.float32)


def lane_transform(sign, scale):
    l = np.arange(LANES)
    angle = 2.0 * np.pi * ((l[:, None] * l[None, :]) % LANES) / LANES
    c, s = np.cos(angle) * scale, sign * np.sin(angle) * scale
    return np.block([[c, s], [-s, c]])


def forward_columns():
    lane = np.arange(LANES)
    order = (lane // 16) + 8 * (lane % 16)
    table = lane_transform(-1.0, 1.0 / 64.0)
    return table[:, np.concatenate([order, LANES + order])]


def swap_bits(v, distance):
    lane = lax.broadcasted_iota(jnp.int32, v[0].shape, len(v[0].shape) - 1)
    for t in range(3):
        step = distance << t
        mask = (lane // step) % 2 == 1
        out = list(v)
        for low in range(8):
            if low & (1 << t):
                continue
            high = low | (1 << t)
            out[low] = jnp.where(mask, pltpu.roll(v[high], step, 1), v[low])
            out[high] = jnp.where(mask, v[high], pltpu.roll(v[low], LANES - step, 1))
        v = out
    return v


def twiddle(re, im, k, n, sign):
    k = k % n
    if k == 0:
        return re, im
    if 4 * k == n:
        return (im, -re) if sign < 0 else (-im, re)
    if 8 * k == n:
        c = math.sqrt(0.5)
        return ((re + im) * c, (im - re) * c) if sign < 0 else ((re - im) * c, (im + re) * c)
    if 8 * k == 3 * n:
        c = math.sqrt(0.5)
        return ((im - re) * c, (-im - re) * c) if sign < 0 else ((-re - im) * c, (re - im) * c)
    c, s = math.cos(2 * math.pi * k / n), sign * math.sin(2 * math.pi * k / n)
    return re * c - im * s, re * s + im * c


def fft(values, sign):
    n = len(values)
    if n == 1:
        return values
    even = fft(values[0::2], sign)
    odd = fft(values[1::2], sign)
    low, high = [], []
    for k in range(n // 2):
        tr, ti = twiddle(odd[k][0], odd[k][1], k, n, sign)
        er, ei = even[k]
        low.append((er + tr, ei + ti))
        high.append((er - tr, ei - ti))
    return low + high


def filtered_rows(now, before, taps, period):
    row = lax.broadcasted_iota(jnp.int32, now.shape, 0) % period
    out = taps[0] * now
    for p in range(1, TAPS):
        out = out + taps[p] * pltpu.roll(jnp.where(row >= period - p, before, now), p, 0)
    return out


def unpack_kernel(place_ref, x_ref, xs_ref, *h_refs):
    i = pl.program_id(0)
    for j in range(COLS // 2):
        at = i * (COLS // 2) + j
        for c in range(2):
            for m in range(8):
                value = x_ref[c, m, :, j * LANES : (j + 1) * LANES]
                xs_ref[c, at, m * 8 : m * 8 + 8, :] = value.astype(jnp.float32)
            for t in range(TAPS - 1):
                value = xs_ref[c, at, pl.ds(8 - (TAPS - 1) + t, 8, stride=8), :]
                cut = pl.ds(pl.multiple_of(at * LANES, LANES), LANES)
                if len(h_refs) == 1:
                    h_refs[0][c, t, :, cut] = value.astype(jnp.bfloat16)
                else:
                    h_refs[c][t, :, cut] = value.astype(jnp.bfloat16)


def unpack(place, samples, group):
    return pl.pallas_call(
        unpack_kernel,
        grid=(2,),
        in_specs=[
            pl.BlockSpec(memory_space=pltpu.SMEM),
            pl.BlockSpec((2, 8, 8, COLS // 2 * LANES), lambda i: (0, group, 0, i)),
        ],
        out_specs=[pl.BlockSpec(memory_space=pltpu.VMEM)] * (2 + group),
        out_shape=[pltpu.VMEM((2, COLS, 64, LANES), jnp.float32)]
        + (
            [pltpu.VMEM((TAPS - 1, 8, COLS * LANES), jnp.bfloat16)] * 2
            if group
            else [pltpu.VMEM((2, TAPS - 1, 8, COLS * LANES), jnp.bfloat16)]
        ),
        name=f"unpack_{group}",
        compiler_params=pltpu.CompilerParams(vmem_limit_bytes=VMEM_LIMIT),
    )(place, samples)


def transform_group(start, x_ref, earlier, proto_ref, tw_ref, f_ref, z_ref, first_row):
    def block(c, j, k):
        if k < 0:
            cut = slice(j * LANES, (j + 1) * LANES)
            return earlier(c, TAPS - 1 + k, cut).astype(jnp.float32)
        return x_ref[c, j, pl.ds(k, 8, stride=8), :]

    for j in range(COLS):
        taps = [proto_ref[p, j : j + 1, :] for p in range(TAPS)]
        for c in range(2):
            blocks = [block(c, j, start - (TAPS - 1) + t) for t in range(TAPS + 3)]
            for k in range(4):
                out = taps[0] * blocks[k + 3]
                for p in range(1, TAPS):
                    out = out + taps[p] * blocks[k + 3 - p]
                f_ref[k, c, j] = out
    for k in range(4):
        values = [(f_ref[k, 0, j], f_ref[k, 1, j]) for j in range(COLS)]
        rows = slice(first_row + k * 8, first_row + k * 8 + 8)
        for a, (re, im) in enumerate(fft(values, -1.0)):
            cs = tw_ref[0, a]
            sn = tw_ref[1, a]
            z_ref[0, a, rows, :] = re * cs - im * sn
            z_ref[1, a, rows, :] = re * sn + im * cs


def twist(place_ref, turn_ref, shift_ref, tw_ref):
    shifts = pl.ds(pl.multiple_of(place_ref[0] * 8, 8), 8)
    shift_re, shift_im = shift_ref[0, shifts, :], shift_ref[1, shifts, :]
    for a in range(COLS):
        cs, sn = turn_ref[0, a : a + 1, :], turn_ref[1, a : a + 1, :]
        tw_ref[0, a] = shift_re * cs - shift_im * sn
        tw_ref[1, a] = shift_re * sn + shift_im * cs


def late_kernel(
    place_ref,
    proto_ref,
    turn_ref,
    shift_ref,
    w_ref,
    x0_ref,
    x1_ref,
    o_ref,
    z_ref,
    tw_ref,
    f_ref,
    stage_ref,
    sem_ref,
):
    twist(place_ref, turn_ref, shift_ref, tw_ref)
    transform_group(4, x0_ref, None, proto_ref, tw_ref, f_ref, z_ref, 0)
    transform_group(4, x1_ref, None, proto_ref, tw_ref, f_ref, z_ref, 32)
    send_columns(w_ref, z_ref, o_ref, 1, stage_ref, sem_ref)


def first_kernel(
    place_ref, proto_ref, turn_ref, shift_ref, x_ref, h_ref, z_ref, tw_ref, f_ref
):
    twist(place_ref, turn_ref, shift_ref, tw_ref)
    def earlier(c, t, cut):
        return h_ref[c, t, :, cut]

    transform_group(0, x_ref, earlier, proto_ref, tw_ref, f_ref, z_ref, 0)


def second_kernel(
    place_ref,
    proto_ref,
    turn_ref,
    shift_ref,
    w_ref,
    x_ref,
    direct_ref,
    near_ref,
    far_ref,
    first_ref,
    _,
    o_ref,
    z_ref,
    tw_ref,
    f_ref,
    stage_ref,
    sem_ref,
):
    twist(place_ref, turn_ref, shift_ref, tw_ref)
    for c in range(2):
        for a in range(COLS):
            z_ref[c, a, :32, :] = first_ref[c, a]
    odd = jnp.broadcast_to(place_ref[1], (8, LANES)) == 1

    def earlier(c, t, cut):
        if c == 0:
            return direct_ref[t, :, cut]
        near = near_ref[t, :, cut].astype(jnp.float32)
        return jnp.where(odd, near, far_ref[t, :, cut].astype(jnp.float32))

    transform_group(0, x_ref, earlier, proto_ref, tw_ref, f_ref, z_ref, 32)
    send_columns(w_ref, z_ref, o_ref, 0, stage_ref, sem_ref)


def send_columns(w_ref, z_ref, o_ref, half, stage_ref, sem_ref):
    def leave(i):
        rows = pl.ds((i % 4) * 4, 4)
        return pltpu.make_async_copy(
            stage_ref.at[i], o_ref.at[rows, :, i // 4, half], sem_ref.at[i]
        )

    seg = lax.broadcasted_iota(jnp.int32, (1, 8, 2 * LANES), 2) % LANES // 16
    bits = [(seg // (1 << t)) % 2 == 1 for t in range(3)]

    def some_columns(i, _):
        a0 = i * 4
        parts = []
        for c in range(2):
            rows = [
                z_ref[c, a0 + ai, pl.ds(mu, 8, stride=8), :] for mu in range(8) for ai in range(4)
            ]
            parts.append(jnp.concatenate(rows, axis=0).astype(jnp.bfloat16))
        z = jnp.concatenate(parts, axis=1)
        out = jnp.dot(z, w_ref[...], preferred_element_type=jnp.float32)
        out = out.reshape(8, 4, 8, 2 * LANES)
        v = [out[r] for r in range(8)]
        for t in range(3):
            mask = jnp.broadcast_to(bits[t], (4, 8, 2 * LANES))
            v = [jnp.where(mask, v[(r + (1 << t)) % 8], v[r]) for r in range(8)]
        for b in range(8):
            w = v[(-b) % 8].astype(jnp.bfloat16)
            for ai in range(4):
                for c in range(2):
                    stage_ref[i, ai, b, c] = w[ai, :, c * LANES : (c + 1) * LANES]
        leave(i).start()
        return 0

    lax.fori_loop(0, 8, some_columns, 0)
    for i in range(8):
        leave(i).wait()


def analysis(kernel, operands, sends, earlier=None):
    specs = [pl.BlockSpec(memory_space=pltpu.SMEM)]
    specs += [pl.BlockSpec(memory_space=pltpu.VMEM)] * (len(operands) - 1)
    scratch = [
        pltpu.VMEM((2, COLS, 64, LANES), jnp.float32),
        pltpu.VMEM((2, COLS, 8, LANES), jnp.float32),
        pltpu.VMEM((4, 2, COLS, 8, LANES), jnp.float32),
    ]
    aliases = {}
    if not sends:
        out_spec = pl.BlockSpec(memory_space=pltpu.VMEM)
        out_shape = pltpu.VMEM((2, COLS, 32, LANES), jnp.float32)
        scratch = scratch[1:]
    else:
        out_spec = pl.BlockSpec(memory_space=pl.ANY)
        out_shape = jax.ShapeDtypeStruct((16, 8, 2, 2, 2, 8, LANES), jnp.bfloat16)
        scratch.append(pltpu.VMEM((8, 4, 8, 2, 8, LANES), jnp.bfloat16))
        scratch.append(pltpu.SemaphoreType.DMA((8,)))
    if earlier is not None:
        aliases = {len(operands): 0}
        operands = [*operands, earlier]
        specs.append(pl.BlockSpec(memory_space=pl.ANY))
    return pl.pallas_call(
        kernel,
        grid=(1,),
        in_specs=specs,
        out_specs=out_spec,
        out_shape=out_shape,
        scratch_shapes=scratch,
        input_output_aliases=aliases,
        name=kernel.__name__,
        compiler_params=pltpu.CompilerParams(vmem_limit_bytes=VMEM_LIMIT),
    )(*operands)


def steer_kernel(b_ref, omega_ref, pos_ref, beam_ref, o_ref):
    e = pl.program_id(0)
    b = b_ref[0]
    lane = lax.broadcasted_iota(jnp.int32, (8, LANES), 1)
    inner = lane % 16

    def within(x, sh):
        return jnp.where(inner >= sh, pltpu.roll(x, sh, 1), pltpu.roll(x, sh + (LANES - 16), 1))

    coords = []
    for d in range(2):
        x = pltpu.roll(pos_ref[d], b * 16, 1)
        coords.append(jnp.where(lane // 16 < b, within(x, (e + 1) % 16), within(x, e)))
    omega = omega_ref[e]
    sin_b = jnp.broadcast_to(beam_ref[:, 0:1], (64, LANES))
    cos_b = jnp.broadcast_to(beam_ref[:, 1:2], (64, LANES))
    for i in range(8):
        turns = omega * (sin_b * coords[0][i : i + 1, :] + cos_b * coords[1][i : i + 1, :])
        rest = turns - jnp.round(turns)
        sq = rest * rest
        sn = rest * horner(SINE, sq)
        cs = horner(COSINE, sq)
        col = slice(i * LANES, (i + 1) * LANES)
        far = slice(1024 + i * LANES, 1024 + (i + 1) * LANES)
        o_ref[0, :, col] = (1.0 - 2.0 * sn * sn).astype(jnp.bfloat16)
        o_ref[0, :, far] = (-2.0 * sn * cs).astype(jnp.bfloat16)


def beam_kernel(b_ref, lam_ref, r_ref, far_ref, o_ref, x_ref, y_ref, m_ref, s_ref, sem_ref):
    step = pl.program_id(0)

    def steering(part):
        rows = pl.ds(part * 4, 4)
        return pltpu.make_async_copy(far_ref.at[rows], s_ref.at[rows], sem_ref.at[part])

    @pl.when(step == 0)
    def _():
        for part in range(4):
            steering(part).start()

    @pl.when(step < 4)
    def _():
        b = b_ref[0]
        lane = lax.broadcasted_iota(jnp.int32, (8, LANES), 1)
        low = lax.broadcasted_iota(jnp.int32, (8, LANES), 0) < 4
        shift = (lane % 16 - jnp.where(lane // 16 < b, 1, 0) + 16) % 16
        bits = [(shift // (1 << t)) % 2 == 1 for t in range(4)]

        def network(section, half, c):
            v = [r_ref[section, step, g, half, c].astype(jnp.float32) for g in range(16)]
            for t in range(4):
                v = [jnp.where(bits[t], v[(r + (1 << t)) % 16], v[r]) for r in range(16)]
            return v

        def separate(pair, _):
            top = pl.ds(pl.multiple_of(pair * 16, 16), 16)
            bot = pl.ds(pl.multiple_of(32 + pair * 16, 16), 16)
            near = [pl.multiple_of(step * 256 + mh * LANES, LANES) for mh in range(2)]
            far = [pl.multiple_of(1024 + step * 256 + mh * LANES, LANES) for mh in range(2)]
            for c in range(2):
                tiles = [[None] * 16, [None] * 16]
                for one in range(2):
                    v0 = network(pair * 2 + one, 0, c)
                    v1 = network(pair * 2 + one, 1, c)
                    for r in range(16):
                        first = jnp.where(low, v0[r], pltpu.roll(v1[r], 4, 0))
                        second = jnp.where(low, pltpu.roll(v0[r], 4, 0), v1[r])
                        for mh, value in enumerate((first, second)):
                            if one == 0:
                                tiles[mh][r] = value
                            else:
                                tiles[mh][r] = jnp.concatenate([tiles[mh][r], value], axis=0)
                for mh in range(2):
                    for e in range(16):
                        w = tiles[mh][(-e) % 16]
                        w16 = w.astype(jnp.bfloat16)
                        if c == 0:
                            x_ref[e, top, pl.ds(near[mh], LANES)] = w16
                            x_ref[e, bot, pl.ds(far[mh], LANES)] = w16
                        else:
                            x_ref[e, top, pl.ds(far[mh], LANES)] = w16
                            x_ref[e, bot, pl.ds(near[mh], LANES)] = (-w).astype(jnp.bfloat16)
            return 0

        lax.fori_loop(0, 2, separate, 0)

    @pl.when(step >= 4)
    def _():
        total = 1024.0
        snapshots = 32.0
        left = lax.broadcasted_iota(jnp.int32, (64, LANES), 1) < 64
        sign = jnp.where(lax.broadcasted_iota(jnp.int32, (64, LANES), 0) < 32, 1.0, -1.0)
        base = (step - 4) * 4
        for part in range(2):
            steering((step - 4) * 2 + part).wait()
        dims = (((1,), (1,)), ((), ()))
        hs, gs = [], []
        for i in range(4):
            spot = (step - 4) * 8 + (i // 2) * 4 + i % 2
            x = x_ref[base + i]
            near = jnp.concatenate([s_ref[spot], x], axis=0)
            near = lax.dot_general(x, near, dims, preferred_element_type=jnp.float32)
            x = x_ref[base + i + 8]
            far = jnp.concatenate([x, s_ref[spot + 2]], axis=0)
            far = lax.dot_general(x, far, dims, preferred_element_type=jnp.float32)
            hs.append(jnp.where(left, near, far))
            gs.append(jnp.where(left, far, near))
        ghs = []
        for h, g in zip(hs, gs):
            g_high = g.astype(jnp.bfloat16)
            g_low = (g - g_high.astype(jnp.float32)).astype(jnp.bfloat16)
            high = h.astype(jnp.bfloat16).astype(jnp.float32)
            parts = []
            for part in (high, h - high):
                both = [jnp.where(left, 0.0, part), jnp.where(left, part, 0.0)]
                parts.append(jnp.concatenate(both, axis=0).astype(jnp.bfloat16))
            left_side = jnp.concatenate([g_high, g_high, g_low], axis=1)
            right_side = jnp.concatenate([parts[0], parts[1], parts[0]], axis=0)
            ghs.append(jnp.dot(left_side, right_side, preferred_element_type=jnp.float32))
        for i in range(4):
            h, gh = hs[i], ghs[i]
            lam = jnp.where(left[:1], lam_ref[base + i], lam_ref[base + i + 8])
            hh = jnp.sum(h * h, axis=0, keepdims=True)
            hgh = jnp.sum(h * gh, axis=0, keepdims=True)
            alpha = total / (hh / snapshots + lam * total)
            rho = 1.0 - alpha * lam
            t = alpha / snapshots
            new = rho * rho * total - 2.0 * rho * t * hh + t * t * hgh
            along = rho + new / total
            proj = along * h - t * gh
            size = along * along * total - 2.0 * along * t * hh + t * t * hgh
            curv = jnp.sum(proj * proj, axis=0, keepdims=True) / snapshots + lam * size
            alpha2 = new / curv
            main = alpha + alpha2 * along
            rest = alpha2 * t
            power = main * main * total - 2.0 * main * rest * hh + rest * rest * hgh
            norm = lax.rsqrt(power + total * 1e-6)
            y_ref[base + i] = sign * ((norm * main) * h - (norm * rest) * gh)

    @pl.when(step == 5)
    def _():
        left = lax.broadcasted_iota(jnp.int32, (64, LANES), 1) < 64
        lane = lax.broadcasted_iota(jnp.int32, (64, LANES), 1) % 64
        pick = jnp.where(lane == lax.broadcasted_iota(jnp.int32, (64, LANES), 0), 1.0, 0.0)
        pick = pick.astype(jnp.bfloat16)
        v = []
        for r in range(8):
            y = y_ref[r]
            both = jnp.concatenate([jnp.where(left, y, 0.0), jnp.where(left, 0.0, y)], axis=0)
            v.append(
                lax.dot_general(
                    pick,
                    both.astype(jnp.bfloat16),
                    (((1,), (1,)), ((), ())),
                    preferred_element_type=jnp.float32,
                )
            )
        v = swap_bits(v, 8)
        near = lax.broadcasted_iota(jnp.int32, (64, LANES), 1) % 8 < 4
        for section in range(4):
            rows = [v[section], v[4 + section]]
            if section:
                rows.append(
                    jnp.where(near, pltpu.roll(v[section - 1], LANES - 4, 1), v[4 + section - 1])
                )
            else:
                rows.append(jnp.zeros((64, LANES), jnp.float32))
            rows.append(jnp.zeros((64, LANES), jnp.float32))
            for r in range(4):
                m_ref[pl.ds(section * 256 + r, 64, stride=4), :] = rows[r]
        o_ref[...] = m_ref[...].astype(jnp.bfloat16)


def synthesis_kernel(m_ref, proto_ref, tw_ref, w_ref, o_ref, r_ref, l_ref, z_ref, s_ref):
    r_ref[...] = m_ref[...].astype(jnp.float32)
    for a_hi in range(2):
        tiles = []
        for r in range(3):
            groups = []
            for group in range(2):
                v = [
                    r_ref[pl.ds((group * 128 + 2 * b + a_hi) * 4 + r, 8, stride=64), :]
                    for b in range(8)
                ]
                groups.append(swap_bits(v, 1))
            tiles.append(
                [jnp.concatenate([groups[0][k], groups[1][k]], axis=0) for k in range(8)]
            )
        for k in range(8):
            rows = slice(k * COLS + a_hi * 16, k * COLS + a_hi * 16 + 16)
            l_ref[rows, :LANES] = tiles[0][k].astype(jnp.bfloat16)
            l_ref[rows, LANES:] = tiles[1][k].astype(jnp.bfloat16)
        for k in range(4):
            rows = slice((8 + k) * COLS + a_hi * 16, (8 + k) * COLS + a_hi * 16 + 16)
            l_ref[rows, :LANES] = tiles[2][k].astype(jnp.bfloat16)
            l_ref[rows, LANES:] = tiles[2][4 + k].astype(jnp.bfloat16)
    full = jnp.dot(l_ref[...], w_ref[...], preferred_element_type=jnp.float32)
    for c in range(2):
        cut = slice(c * LANES, (c + 1) * LANES)
        z_ref[c, : 8 * COLS] = full[: 8 * COLS, cut]
        z_ref[c, 8 * COLS : 12 * COLS] = jnp.zeros((4 * COLS, LANES), jnp.float32)
        z_ref[c, 12 * COLS :] = full[8 * COLS :, cut]

    def half(i, _):
        values = []
        for a in range(COLS):
            rows = pl.ds(i * (8 * COLS) + a, 8, stride=COLS)
            re = z_ref[0, rows, :]
            im = z_ref[1, rows, :]
            cs = tw_ref[0, a : a + 1, :]
            sn = tw_ref[1, a : a + 1, :]
            values.append((re * cs - im * sn, re * sn + im * cs))
        for j, (re, im) in enumerate(fft(values, 1.0)):
            s_ref[0, i, j] = re.astype(jnp.bfloat16).astype(jnp.float32)
            s_ref[1, i, j] = im.astype(jnp.bfloat16).astype(jnp.float32)
        return 0

    for i in range(2):
        half(i, 0)
    for c in range(2):
        for j in range(COLS):
            taps = [proto_ref[TAPS - 1 - p, j : j + 1, :] for p in range(TAPS)]
            out = filtered_rows(s_ref[c, 0, j], s_ref[c, 1, j], taps, 8)
            o_ref[c, 0, :, j * LANES : (j + 1) * LANES] = out.astype(jnp.bfloat16)


def body(samples, positions, beam_dir, load_exp):
    sections = lax.axis_size("section")
    groups = lax.axis_size("gx")
    device = lax.axis_index(AXES).astype(jnp.int32)
    spot = jnp.stack([device % 16, device // groups % 2])

    proto = jnp.asarray(prototype_table())
    w_forward = jnp.asarray(forward_columns(), jnp.bfloat16)
    w_inverse = jnp.asarray(lane_transform(1.0, 1.0 / 64.0), jnp.bfloat16)

    samples = pltpu.with_memory_space_constraint(samples, pltpu.HBM)
    onward = [(i, i + 1) for i in range(sections - 1)]
    x_first, last = unpack(spot, samples, 0)
    h_first = lax.ppermute(last, "section", onward)
    x_second, last, relayed = unpack(spot, samples, 1)
    low = [g for g in range(groups) if g % 8 < 4]
    near = [(i * groups + g, (i + 1) * groups + g) for i in (0, 2) for g in range(groups)]
    near += [(groups + g, 2 * groups + g + 4) for g in low]
    near += [(groups + g + 4, g) for g in low]
    far = [(2 * groups + g + 4, 2 * groups + g) for g in low]
    far += [(g, 2 * groups + g + 4) for g in low]
    h_near = lax.ppermute(relayed, AXES, near)
    h_direct = lax.ppermute(last, "section", onward)
    h_far = lax.ppermute(h_near, AXES, far)

    def in_vmem(value):
        return pltpu.with_memory_space_constraint(value, pltpu.VMEM)

    a_index, l_index = np.arange(COLS)[:, None], np.arange(LANES)[None, :]
    n_angle = 2.0 * np.pi / 4096.0 * a_index * l_index
    tw_inverse = jnp.asarray(np.stack([np.cos(n_angle), np.sin(n_angle)]), jnp.float32)
    turns = jnp.asarray(np.stack([np.cos(n_angle), -np.sin(n_angle)]), jnp.float32)
    s_angle = 2.0 * np.pi / LANES * ((np.arange(LANES)[:, None] * l_index) % LANES)
    shifts = jnp.asarray(np.stack([np.cos(s_angle), np.sin(s_angle)]), jnp.float32)
    tables = [spot, proto, turns, shifts]
    message = analysis(late_kernel, [*tables, w_forward, x_first, x_second], True)
    first = analysis(first_kernel, [*tables, x_first, in_vmem(h_first)], False)
    hists = [in_vmem(h) for h in (h_direct, h_near, h_far)]
    message = analysis(
        second_kernel, [*tables, w_forward, x_second, *hists, first], True, message
    )

    message, positions, load_exp, beam_dir, device = lax.optimization_barrier(
        (message, positions, load_exp, beam_dir, device)
    )
    own_b = (device % 16) // 2
    own_a = device // 16 + 16 * (device % 2)
    received = lax.all_to_all(
        message.reshape(256, 2, 2, 8, LANES), AXES, 0, 0, tiled=True
    )

    devices = sections * groups
    exponents = load_exp.astype(jnp.float32)
    rows = [exponents]
    for t in range(1, 16):
        rows.append(lax.ppermute(exponents, AXES, [(i, i ^ (16 * t)) for i in range(devices)]))
    own = device // 16
    slots = jnp.arange(16, dtype=jnp.int32)
    picked = jnp.sum(jnp.stack(rows) * (slots == own)[None, :], axis=1)
    mine = jnp.sum(jnp.where((slots ^ own)[:, None] == slots[None, :], picked[None, :], 0.0), axis=1)
    lam = jnp.exp2(mine)

    spread = positions.reshape(2, 4, 16, 2, 8).transpose(0, 1, 3, 4, 2).reshape(2, 8, LANES)
    channel = own_a + 32 * own_b + 256 * jnp.arange(16, dtype=jnp.int32)
    angular = 0.75 + 0.5 * channel.astype(jnp.float32) / 4096
    beams = beam_dir.shape[0]
    angle_beam = math.pi / beams * (beam_dir.astype(jnp.float32) + 0.5) - 0.5 * math.pi
    directions = jnp.stack([jnp.sin(angle_beam), jnp.cos(angle_beam)], axis=1)
    steer = pl.pallas_call(
        steer_kernel,
        grid=(16,),
        in_specs=[
            pl.BlockSpec(memory_space=pltpu.SMEM),
            pl.BlockSpec(memory_space=pltpu.SMEM),
            pl.BlockSpec((2, 8, LANES), lambda e: (0, 0, 0)),
            pl.BlockSpec((beams, 2), lambda e: (0, 0)),
        ],
        out_specs=pl.BlockSpec(
            (1, beams, 2048), lambda e: (4 * ((e % 8) // 2) + e % 2 + 2 * (e // 8), 0, 0)
        ),
        out_shape=jax.ShapeDtypeStruct((16, beams, 2048), jnp.bfloat16),
        name="steer",
        compiler_params=pltpu.CompilerParams(vmem_limit_bytes=VMEM_LIMIT),
    )(own_b[None], angular, spread, directions)

    steer = pltpu.with_memory_space_constraint(steer, pltpu.HBM)
    received = pltpu.with_memory_space_constraint(
        received.reshape(4, 4, 16, 2, 2, 8, LANES), pltpu.VMEM
    )
    back = pl.pallas_call(
        beam_kernel,
        grid=(6,),
        in_specs=[
            pl.BlockSpec(memory_space=pltpu.SMEM),
            pl.BlockSpec(memory_space=pltpu.SMEM),
            pl.BlockSpec(memory_space=pltpu.VMEM),
            pl.BlockSpec(memory_space=pl.ANY),
        ],
        out_specs=pl.BlockSpec((4 * devices, LANES), lambda i: (0, 0)),
        out_shape=jax.ShapeDtypeStruct((4 * devices, LANES), jnp.bfloat16),
        scratch_shapes=[
            pltpu.VMEM((16, 64, 2048), jnp.bfloat16),
            pltpu.VMEM((8, 64, LANES), jnp.float32),
            pltpu.VMEM((4 * devices, LANES), jnp.float32),
            pltpu.VMEM((16, beams, 2048), jnp.bfloat16),
            pltpu.SemaphoreType.DMA((4,)),
        ],
        name="beams",
        compiler_params=pltpu.CompilerParams(vmem_limit_bytes=VMEM_LIMIT),
    )(own_b[None], lam, received, steer)

    returned = lax.all_to_all(back.reshape(devices, 4, LANES), AXES, 0, 0, tiled=True)
    return pl.pallas_call(
        synthesis_kernel,
        in_specs=[pl.BlockSpec(memory_space=pltpu.VMEM)] * 4,
        out_specs=pl.BlockSpec(memory_space=pltpu.VMEM),
        out_shape=jax.ShapeDtypeStruct((2, 1, 8, 4096), jnp.bfloat16),
        scratch_shapes=[
            pltpu.VMEM((4 * devices, LANES), jnp.float32),
            pltpu.VMEM((12 * COLS, 2 * LANES), jnp.bfloat16),
            pltpu.VMEM((2, 16 * COLS, LANES), jnp.float32),
            pltpu.VMEM((2, 2, COLS, 8, LANES), jnp.float32),
        ],
        name="synthesis",
        compiler_params=pltpu.CompilerParams(vmem_limit_bytes=VMEM_LIMIT),
    )(returned.reshape(4 * devices, LANES), proto, tw_inverse, w_inverse)


def solution(mesh):
    placed = (P(None, "gx", "section", None), P(), P(), P(AXES))
    return jax.shard_map(
        body, mesh=mesh, in_specs=placed, out_specs=P(None, "gx", "section", None), check_vma=False
    )
```

```python
import math

import numpy as np
import jax
import jax.numpy as jnp
from jax import lax
from jax.experimental import pallas as pl
from jax.experimental.pallas import tpu as pltpu
from jax.sharding import PartitionSpec as P

TAPS = 4
LANES = 128
COLS = 32
AXES = ("section", "gx")
VMEM_LIMIT = 32 << 20
SINE = [(-1.0) ** i * math.pi ** (2 * i + 1) / math.factorial(2 * i + 1) for i in range(6)]
COSINE = [(-1.0) ** i * math.pi ** (2 * i) / math.factorial(2 * i) for i in range(6)]


def horner(coefficients, x):
    out = coefficients[-1]
    for value in reversed(coefficients[:-1]):
        out = out * x + value
    return out


def prototype_table():
    total = TAPS * COLS * LANES
    position = np.arange(total, dtype=np.float64) + 0.5
    window = 0.5 - 0.5 * np.cos(2.0 * np.pi / total * position)
    shaped = np.sinc((position - 0.5 * total) / (COLS * LANES)) * window
    return shaped.reshape(TAPS, COLS, LANES).astype(np.float32)


def lane_transform(sign, scale):
    l = np.arange(LANES)
    angle = 2.0 * np.pi * ((l[:, None] * l[None, :]) % LANES) / LANES
    c, s = np.cos(angle) * scale, sign * np.sin(angle) * scale
    return np.block([[c, s], [-s, c]])


def forward_columns():
    lane = np.arange(LANES)
    order = (lane // 16) + 8 * (lane % 16)
    table = lane_transform(-1.0, 1.0 / 64.0)
    return table[:, np.concatenate([order, LANES + order])]


def swap_bits(v, distance):
    lane = lax.broadcasted_iota(jnp.int32, v[0].shape, len(v[0].shape) - 1)
    for t in range(3):
        step = distance << t
        mask = (lane // step) % 2 == 1
        out = list(v)
        for low in range(8):
            if low & (1 << t):
                continue
            high = low | (1 << t)
            out[low] = jnp.where(mask, pltpu.roll(v[high], step, 1), v[low])
            out[high] = jnp.where(mask, v[high], pltpu.roll(v[low], LANES - step, 1))
        v = out
    return v


def twiddle(re, im, k, n, sign):
    k = k % n
    if k == 0:
        return re, im
    if 4 * k == n:
        return (im, -re) if sign < 0 else (-im, re)
    if 8 * k == n:
        c = math.sqrt(0.5)
        return ((re + im) * c, (im - re) * c) if sign < 0 else ((re - im) * c, (im + re) * c)
    if 8 * k == 3 * n:
        c = math.sqrt(0.5)
        return ((im - re) * c, (-im - re) * c) if sign < 0 else ((-re - im) * c, (re - im) * c)
    c, s = math.cos(2 * math.pi * k / n), sign * math.sin(2 * math.pi * k / n)
    return re * c - im * s, re * s + im * c


def fft(values, sign):
    n = len(values)
    if n == 1:
        return values
    even = fft(values[0::2], sign)
    odd = fft(values[1::2], sign)
    low, high = [], []
    for k in range(n // 2):
        tr, ti = twiddle(odd[k][0], odd[k][1], k, n, sign)
        er, ei = even[k]
        low.append((er + tr, ei + ti))
        high.append((er - tr, ei - ti))
    return low + high


def filtered_rows(now, before, taps, period):
    row = lax.broadcasted_iota(jnp.int32, now.shape, 0) % period
    out = taps[0] * now
    for p in range(1, TAPS):
        out = out + taps[p] * pltpu.roll(jnp.where(row >= period - p, before, now), p, 0)
    return out


def unpack_kernel(place_ref, x_ref, xs_ref, h_ref):
    c = pl.program_id(0)
    for j in range(COLS):
        cut = slice(j * LANES, (j + 1) * LANES)
        for m in range(8):
            xs_ref[c, j, m * 8 : m * 8 + 8, :] = x_ref[0, m, :, cut].astype(jnp.float32)
        for t in range(TAPS - 1):
            value = xs_ref[c, j, pl.ds(8 - (TAPS - 1) + t, 8, stride=8), :]
            h_ref[c, t, :, cut] = value.astype(jnp.bfloat16)


def unpack(place, samples, group):
    return pl.pallas_call(
        unpack_kernel,
        grid=(2,),
        in_specs=[
            pl.BlockSpec(memory_space=pltpu.SMEM),
            pl.BlockSpec((1, 8, 8, COLS * LANES), lambda c: (c, group, 0, 0)),
        ],
        out_specs=[pl.BlockSpec(memory_space=pltpu.VMEM)] * 2,
        out_shape=[
            pltpu.VMEM((2, COLS, 64, LANES), jnp.float32),
            pltpu.VMEM((2, TAPS - 1, 8, COLS * LANES), jnp.bfloat16),
        ],
        name=f"unpack_{group}",
        compiler_params=pltpu.CompilerParams(vmem_limit_bytes=VMEM_LIMIT),
    )(place, samples)


def transform_group(start, x_ref, h_ref, proto_ref, tw_ref, f_ref, z_ref, first_row):
    def block(c, j, k):
        if k < 0:
            cut = slice(j * LANES, (j + 1) * LANES)
            return h_ref[c, TAPS - 1 + k, :, cut].astype(jnp.float32)
        return x_ref[c, j, pl.ds(k, 8, stride=8), :]

    for j in range(COLS):
        taps = [proto_ref[p, j : j + 1, :] for p in range(TAPS)]
        for c in range(2):
            blocks = [block(c, j, start - (TAPS - 1) + t) for t in range(TAPS + 3)]
            for k in range(4):
                out = taps[0] * blocks[k + 3]
                for p in range(1, TAPS):
                    out = out + taps[p] * blocks[k + 3 - p]
                f_ref[k, c, j] = out
    for k in range(4):
        values = [(f_ref[k, 0, j], f_ref[k, 1, j]) for j in range(COLS)]
        rows = slice(first_row + k * 8, first_row + k * 8 + 8)
        for a, (re, im) in enumerate(fft(values, -1.0)):
            cs = tw_ref[0, a]
            sn = tw_ref[1, a]
            z_ref[0, a, rows, :] = re * cs - im * sn
            z_ref[1, a, rows, :] = re * sn + im * cs


def twist(place_ref, turn_ref, shift_ref, tw_ref):
    shifts = pl.ds(pl.multiple_of(place_ref[0] * 8, 8), 8)
    shift_re, shift_im = shift_ref[0, shifts, :], shift_ref[1, shifts, :]
    for a in range(COLS):
        cs, sn = turn_ref[0, a : a + 1, :], turn_ref[1, a : a + 1, :]
        tw_ref[0, a] = shift_re * cs - shift_im * sn
        tw_ref[1, a] = shift_re * sn + shift_im * cs


def late_kernel(
    place_ref,
    proto_ref,
    turn_ref,
    shift_ref,
    w_ref,
    x0_ref,
    x1_ref,
    o_ref,
    z_ref,
    tw_ref,
    f_ref,
    stage_ref,
    sem_ref,
):
    twist(place_ref, turn_ref, shift_ref, tw_ref)
    transform_group(4, x0_ref, None, proto_ref, tw_ref, f_ref, z_ref, 0)
    transform_group(4, x1_ref, None, proto_ref, tw_ref, f_ref, z_ref, 32)
    send_columns(w_ref, z_ref, o_ref, 1, stage_ref, sem_ref)


def first_kernel(
    place_ref, proto_ref, turn_ref, shift_ref, x_ref, h_ref, z_ref, tw_ref, f_ref
):
    twist(place_ref, turn_ref, shift_ref, tw_ref)
    transform_group(0, x_ref, h_ref, proto_ref, tw_ref, f_ref, z_ref, 0)


def second_kernel(
    place_ref,
    proto_ref,
    turn_ref,
    shift_ref,
    w_ref,
    x_ref,
    h_ref,
    first_ref,
    _,
    o_ref,
    z_ref,
    tw_ref,
    f_ref,
    stage_ref,
    sem_ref,
):
    twist(place_ref, turn_ref, shift_ref, tw_ref)
    for c in range(2):
        for a in range(COLS):
            z_ref[c, a, :32, :] = first_ref[c, a]
    transform_group(0, x_ref, h_ref, proto_ref, tw_ref, f_ref, z_ref, 32)
    send_columns(w_ref, z_ref, o_ref, 0, stage_ref, sem_ref)


def send_columns(w_ref, z_ref, o_ref, half, stage_ref, sem_ref):
    def leave(i):
        rows = pl.ds((i % 4) * 4, 4)
        return pltpu.make_async_copy(
            stage_ref.at[i], o_ref.at[rows, :, i // 4, half], sem_ref.at[i]
        )

    seg = lax.broadcasted_iota(jnp.int32, (1, 8, 2 * LANES), 2) % LANES // 16
    bits = [(seg // (1 << t)) % 2 == 1 for t in range(3)]

    def some_columns(i, _):
        a0 = i * 4
        parts = []
        for c in range(2):
            rows = [
                z_ref[c, a0 + ai, pl.ds(mu, 8, stride=8), :] for mu in range(8) for ai in range(4)
            ]
            parts.append(jnp.concatenate(rows, axis=0).astype(jnp.bfloat16))
        z = jnp.concatenate(parts, axis=1)
        out = jnp.dot(z, w_ref[...], preferred_element_type=jnp.float32)
        out = out.reshape(8, 4, 8, 2 * LANES)
        v = [out[r] for r in range(8)]
        for t in range(3):
            mask = jnp.broadcast_to(bits[t], (4, 8, 2 * LANES))
            v = [jnp.where(mask, v[(r + (1 << t)) % 8], v[r]) for r in range(8)]
        for b in range(8):
            w = v[(-b) % 8].astype(jnp.bfloat16)
            for ai in range(4):
                for c in range(2):
                    stage_ref[i, ai, b, c] = w[ai, :, c * LANES : (c + 1) * LANES]
        leave(i).start()
        return 0

    lax.fori_loop(0, 8, some_columns, 0)
    for i in range(8):
        leave(i).wait()


def analysis(kernel, operands, sends, earlier=None):
    specs = [pl.BlockSpec(memory_space=pltpu.SMEM)]
    specs += [pl.BlockSpec(memory_space=pltpu.VMEM)] * (len(operands) - 1)
    scratch = [
        pltpu.VMEM((2, COLS, 64, LANES), jnp.float32),
        pltpu.VMEM((2, COLS, 8, LANES), jnp.float32),
        pltpu.VMEM((4, 2, COLS, 8, LANES), jnp.float32),
    ]
    aliases = {}
    if not sends:
        out_spec = pl.BlockSpec(memory_space=pltpu.VMEM)
        out_shape = pltpu.VMEM((2, COLS, 32, LANES), jnp.float32)
        scratch = scratch[1:]
    else:
        out_spec = pl.BlockSpec(memory_space=pl.ANY)
        out_shape = jax.ShapeDtypeStruct((16, 8, 2, 2, 2, 8, LANES), jnp.bfloat16)
        scratch.append(pltpu.VMEM((8, 4, 8, 2, 8, LANES), jnp.bfloat16))
        scratch.append(pltpu.SemaphoreType.DMA((8,)))
    if earlier is not None:
        aliases = {len(operands): 0}
        operands = [*operands, earlier]
        specs.append(pl.BlockSpec(memory_space=pl.ANY))
    return pl.pallas_call(
        kernel,
        grid=(1,),
        in_specs=specs,
        out_specs=out_spec,
        out_shape=out_shape,
        scratch_shapes=scratch,
        input_output_aliases=aliases,
        name=kernel.__name__,
        compiler_params=pltpu.CompilerParams(vmem_limit_bytes=VMEM_LIMIT),
    )(*operands)


def steer_kernel(b_ref, omega_ref, pos_ref, beam_ref, o_ref):
    e = pl.program_id(0)
    b = b_ref[0]
    lane = lax.broadcasted_iota(jnp.int32, (8, LANES), 1)
    inner = lane % 16

    def within(x, sh):
        return jnp.where(inner >= sh, pltpu.roll(x, sh, 1), pltpu.roll(x, sh + (LANES - 16), 1))

    coords = []
    for d in range(2):
        x = pltpu.roll(pos_ref[d], b * 16, 1)
        coords.append(jnp.where(lane // 16 < b, within(x, (e + 1) % 16), within(x, e)))
    omega = omega_ref[e]
    sin_b = jnp.broadcast_to(beam_ref[:, 0:1], (64, LANES))
    cos_b = jnp.broadcast_to(beam_ref[:, 1:2], (64, LANES))
    for i in range(8):
        turns = omega * (sin_b * coords[0][i : i + 1, :] + cos_b * coords[1][i : i + 1, :])
        rest = turns - jnp.round(turns)
        sq = rest * rest
        sn = rest * horner(SINE, sq)
        cs = horner(COSINE, sq)
        col = slice(i * LANES, (i + 1) * LANES)
        far = slice(1024 + i * LANES, 1024 + (i + 1) * LANES)
        o_ref[0, :, col] = (1.0 - 2.0 * sn * sn).astype(jnp.bfloat16)
        o_ref[0, :, far] = (-2.0 * sn * cs).astype(jnp.bfloat16)


def beam_kernel(b_ref, lam_ref, r_ref, far_ref, o_ref, x_ref, y_ref, m_ref, s_ref, sem_ref):
    step = pl.program_id(0)

    def steering(part):
        rows = pl.ds(part * 4, 4)
        return pltpu.make_async_copy(far_ref.at[rows], s_ref.at[rows], sem_ref.at[part])

    @pl.when(step == 0)
    def _():
        for part in range(4):
            steering(part).start()

    @pl.when(step < 4)
    def _():
        b = b_ref[0]
        lane = lax.broadcasted_iota(jnp.int32, (8, LANES), 1)
        low = lax.broadcasted_iota(jnp.int32, (8, LANES), 0) < 4
        shift = (lane % 16 - jnp.where(lane // 16 < b, 1, 0) + 16) % 16
        bits = [(shift // (1 << t)) % 2 == 1 for t in range(4)]

        def network(section, half, c):
            v = [r_ref[section, step, g, half, c].astype(jnp.float32) for g in range(16)]
            for t in range(4):
                v = [jnp.where(bits[t], v[(r + (1 << t)) % 16], v[r]) for r in range(16)]
            return v

        def separate(pair, _):
            top = pl.ds(pl.multiple_of(pair * 16, 16), 16)
            bot = pl.ds(pl.multiple_of(32 + pair * 16, 16), 16)
            near = [pl.multiple_of(step * 256 + mh * LANES, LANES) for mh in range(2)]
            far = [pl.multiple_of(1024 + step * 256 + mh * LANES, LANES) for mh in range(2)]
            for c in range(2):
                tiles = [[None] * 16, [None] * 16]
                for one in range(2):
                    v0 = network(pair * 2 + one, 0, c)
                    v1 = network(pair * 2 + one, 1, c)
                    for r in range(16):
                        first = jnp.where(low, v0[r], pltpu.roll(v1[r], 4, 0))
                        second = jnp.where(low, pltpu.roll(v0[r], 4, 0), v1[r])
                        for mh, value in enumerate((first, second)):
                            if one == 0:
                                tiles[mh][r] = value
                            else:
                                tiles[mh][r] = jnp.concatenate([tiles[mh][r], value], axis=0)
                for mh in range(2):
                    for e in range(16):
                        w = tiles[mh][(-e) % 16]
                        w16 = w.astype(jnp.bfloat16)
                        if c == 0:
                            x_ref[e, top, pl.ds(near[mh], LANES)] = w16
                            x_ref[e, bot, pl.ds(far[mh], LANES)] = w16
                        else:
                            x_ref[e, top, pl.ds(far[mh], LANES)] = w16
                            x_ref[e, bot, pl.ds(near[mh], LANES)] = (-w).astype(jnp.bfloat16)
            return 0

        lax.fori_loop(0, 2, separate, 0)

    @pl.when(step >= 4)
    def _():
        total = 1024.0
        snapshots = 32.0
        left = lax.broadcasted_iota(jnp.int32, (64, LANES), 1) < 64
        sign = jnp.where(lax.broadcasted_iota(jnp.int32, (64, LANES), 0) < 32, 1.0, -1.0)
        base = (step - 4) * 4
        for part in range(2):
            steering((step - 4) * 2 + part).wait()
        dims = (((1,), (1,)), ((), ()))
        hs, gs = [], []
        for i in range(4):
            spot = (step - 4) * 8 + (i // 2) * 4 + i % 2
            x = x_ref[base + i]
            near = jnp.concatenate([s_ref[spot], x], axis=0)
            near = lax.dot_general(x, near, dims, preferred_element_type=jnp.float32)
            x = x_ref[base + i + 8]
            far = jnp.concatenate([x, s_ref[spot + 2]], axis=0)
            far = lax.dot_general(x, far, dims, preferred_element_type=jnp.float32)
            hs.append(jnp.where(left, near, far))
            gs.append(jnp.where(left, far, near))
        ghs = []
        for h, g in zip(hs, gs):
            g_high = g.astype(jnp.bfloat16)
            g_low = (g - g_high.astype(jnp.float32)).astype(jnp.bfloat16)
            high = h.astype(jnp.bfloat16).astype(jnp.float32)
            parts = []
            for part in (high, h - high):
                both = [jnp.where(left, 0.0, part), jnp.where(left, part, 0.0)]
                parts.append(jnp.concatenate(both, axis=0).astype(jnp.bfloat16))
            left_side = jnp.concatenate([g_high, g_high, g_low], axis=1)
            right_side = jnp.concatenate([parts[0], parts[1], parts[0]], axis=0)
            ghs.append(jnp.dot(left_side, right_side, preferred_element_type=jnp.float32))
        for i in range(4):
            h, gh = hs[i], ghs[i]
            lam = jnp.where(left[:1], lam_ref[base + i], lam_ref[base + i + 8])
            hh = jnp.sum(h * h, axis=0, keepdims=True)
            hgh = jnp.sum(h * gh, axis=0, keepdims=True)
            alpha = total / (hh / snapshots + lam * total)
            rho = 1.0 - alpha * lam
            t = alpha / snapshots
            new = rho * rho * total - 2.0 * rho * t * hh + t * t * hgh
            along = rho + new / total
            proj = along * h - t * gh
            size = along * along * total - 2.0 * along * t * hh + t * t * hgh
            curv = jnp.sum(proj * proj, axis=0, keepdims=True) / snapshots + lam * size
            alpha2 = new / curv
            main = alpha + alpha2 * along
            rest = alpha2 * t
            power = main * main * total - 2.0 * main * rest * hh + rest * rest * hgh
            norm = lax.rsqrt(power + total * 1e-6)
            y_ref[base + i] = sign * ((norm * main) * h - (norm * rest) * gh)

    @pl.when(step == 5)
    def _():
        left = lax.broadcasted_iota(jnp.int32, (64, LANES), 1) < 64
        lane = lax.broadcasted_iota(jnp.int32, (64, LANES), 1) % 64
        pick = jnp.where(lane == lax.broadcasted_iota(jnp.int32, (64, LANES), 0), 1.0, 0.0)
        pick = pick.astype(jnp.bfloat16)
        v = []
        for r in range(8):
            y = y_ref[r]
            both = jnp.concatenate([jnp.where(left, y, 0.0), jnp.where(left, 0.0, y)], axis=0)
            v.append(
                lax.dot_general(
                    pick,
                    both.astype(jnp.bfloat16),
                    (((1,), (1,)), ((), ())),
                    preferred_element_type=jnp.float32,
                )
            )
        v = swap_bits(v, 8)
        near = lax.broadcasted_iota(jnp.int32, (64, LANES), 1) % 8 < 4
        for section in range(4):
            rows = [v[section], v[4 + section]]
            if section:
                rows.append(
                    jnp.where(near, pltpu.roll(v[section - 1], LANES - 4, 1), v[4 + section - 1])
                )
            else:
                rows.append(jnp.zeros((64, LANES), jnp.float32))
            rows.append(jnp.zeros((64, LANES), jnp.float32))
            for r in range(4):
                m_ref[pl.ds(section * 256 + r, 64, stride=4), :] = rows[r]
        o_ref[...] = m_ref[...].astype(jnp.bfloat16)


def synthesis_kernel(m_ref, proto_ref, tw_ref, w_ref, o_ref, r_ref, l_ref, z_ref, s_ref):
    r_ref[...] = m_ref[...].astype(jnp.float32)
    for a_hi in range(2):
        tiles = []
        for r in range(3):
            groups = []
            for group in range(2):
                v = [
                    r_ref[pl.ds((group * 128 + 2 * b + a_hi) * 4 + r, 8, stride=64), :]
                    for b in range(8)
                ]
                groups.append(swap_bits(v, 1))
            tiles.append(
                [jnp.concatenate([groups[0][k], groups[1][k]], axis=0) for k in range(8)]
            )
        for k in range(8):
            rows = slice(k * COLS + a_hi * 16, k * COLS + a_hi * 16 + 16)
            l_ref[rows, :LANES] = tiles[0][k].astype(jnp.bfloat16)
            l_ref[rows, LANES:] = tiles[1][k].astype(jnp.bfloat16)
        for k in range(4):
            rows = slice((8 + k) * COLS + a_hi * 16, (8 + k) * COLS + a_hi * 16 + 16)
            l_ref[rows, :LANES] = tiles[2][k].astype(jnp.bfloat16)
            l_ref[rows, LANES:] = tiles[2][4 + k].astype(jnp.bfloat16)
    full = jnp.dot(l_ref[...], w_ref[...], preferred_element_type=jnp.float32)
    for c in range(2):
        cut = slice(c * LANES, (c + 1) * LANES)
        z_ref[c, : 8 * COLS] = full[: 8 * COLS, cut]
        z_ref[c, 8 * COLS : 12 * COLS] = jnp.zeros((4 * COLS, LANES), jnp.float32)
        z_ref[c, 12 * COLS :] = full[8 * COLS :, cut]

    def half(i, _):
        values = []
        for a in range(COLS):
            rows = pl.ds(i * (8 * COLS) + a, 8, stride=COLS)
            re = z_ref[0, rows, :]
            im = z_ref[1, rows, :]
            cs = tw_ref[0, a : a + 1, :]
            sn = tw_ref[1, a : a + 1, :]
            values.append((re * cs - im * sn, re * sn + im * cs))
        for j, (re, im) in enumerate(fft(values, 1.0)):
            s_ref[0, i, j] = re.astype(jnp.bfloat16).astype(jnp.float32)
            s_ref[1, i, j] = im.astype(jnp.bfloat16).astype(jnp.float32)
        return 0

    for i in range(2):
        half(i, 0)
    for c in range(2):
        for j in range(COLS):
            taps = [proto_ref[TAPS - 1 - p, j : j + 1, :] for p in range(TAPS)]
            out = filtered_rows(s_ref[c, 0, j], s_ref[c, 1, j], taps, 8)
            o_ref[c, 0, :, j * LANES : (j + 1) * LANES] = out.astype(jnp.bfloat16)


def body(samples, positions, beam_dir, load_exp):
    sections = lax.axis_size("section")
    groups = lax.axis_size("gx")
    device = lax.axis_index(AXES).astype(jnp.int32)
    spot = (device % 16)[None]

    proto = jnp.asarray(prototype_table())
    w_forward = jnp.asarray(forward_columns(), jnp.bfloat16)
    w_inverse = jnp.asarray(lane_transform(1.0, 1.0 / 64.0), jnp.bfloat16)

    samples = pltpu.with_memory_space_constraint(samples, pltpu.HBM)
    onward = [(i, i + 1) for i in range(sections - 1)]
    groups_x, groups_h = [], []
    for group in range(2):
        unpacked, last = unpack(spot, samples, group)
        hist = lax.ppermute(last, "section", onward)
        groups_x.append(unpacked)
        groups_h.append(pltpu.with_memory_space_constraint(hist, pltpu.VMEM))

    a_index, l_index = np.arange(COLS)[:, None], np.arange(LANES)[None, :]
    n_angle = 2.0 * np.pi / 4096.0 * a_index * l_index
    tw_inverse = jnp.asarray(np.stack([np.cos(n_angle), np.sin(n_angle)]), jnp.float32)
    turns = jnp.asarray(np.stack([np.cos(n_angle), -np.sin(n_angle)]), jnp.float32)
    s_angle = 2.0 * np.pi / LANES * ((np.arange(LANES)[:, None] * l_index) % LANES)
    shifts = jnp.asarray(np.stack([np.cos(s_angle), np.sin(s_angle)]), jnp.float32)
    tables = [spot, proto, turns, shifts]
    message = analysis(late_kernel, [*tables, w_forward, *groups_x], True)
    first = analysis(first_kernel, [*tables, groups_x[0], groups_h[0]], False)
    message = analysis(
        second_kernel, [*tables, w_forward, groups_x[1], groups_h[1], first], True, message
    )

    message, positions, load_exp, beam_dir, device = lax.optimization_barrier(
        (message, positions, load_exp, beam_dir, device)
    )
    own_b = (device % 16) // 2
    own_a = device // 16 + 16 * (device % 2)
    received = lax.all_to_all(
        message.reshape(256, 2, 2, 8, LANES), AXES, 0, 0, tiled=True
    )

    devices = sections * groups
    exponents = load_exp.astype(jnp.float32)
    rows = [exponents]
    for t in range(1, 16):
        rows.append(lax.ppermute(exponents, AXES, [(i, i ^ (16 * t)) for i in range(devices)]))
    own = device // 16
    slots = jnp.arange(16, dtype=jnp.int32)
    picked = jnp.sum(jnp.stack(rows) * (slots == own)[None, :], axis=1)
    mine = jnp.sum(jnp.where((slots ^ own)[:, None] == slots[None, :], picked[None, :], 0.0), axis=1)
    lam = jnp.exp2(mine)

    spread = positions.reshape(2, 4, 16, 2, 8).transpose(0, 1, 3, 4, 2).reshape(2, 8, LANES)
    channel = own_a + 32 * own_b + 256 * jnp.arange(16, dtype=jnp.int32)
    angular = 0.75 + 0.5 * channel.astype(jnp.float32) / 4096
    beams = beam_dir.shape[0]
    angle_beam = math.pi / beams * (beam_dir.astype(jnp.float32) + 0.5) - 0.5 * math.pi
    directions = jnp.stack([jnp.sin(angle_beam), jnp.cos(angle_beam)], axis=1)
    steer = pl.pallas_call(
        steer_kernel,
        grid=(16,),
        in_specs=[
            pl.BlockSpec(memory_space=pltpu.SMEM),
            pl.BlockSpec(memory_space=pltpu.SMEM),
            pl.BlockSpec((2, 8, LANES), lambda e: (0, 0, 0)),
            pl.BlockSpec((beams, 2), lambda e: (0, 0)),
        ],
        out_specs=pl.BlockSpec(
            (1, beams, 2048), lambda e: (4 * ((e % 8) // 2) + e % 2 + 2 * (e // 8), 0, 0)
        ),
        out_shape=jax.ShapeDtypeStruct((16, beams, 2048), jnp.bfloat16),
        name="steer",
        compiler_params=pltpu.CompilerParams(vmem_limit_bytes=VMEM_LIMIT),
    )(own_b[None], angular, spread, directions)

    steer = pltpu.with_memory_space_constraint(steer, pltpu.HBM)
    received = pltpu.with_memory_space_constraint(
        received.reshape(4, 4, 16, 2, 2, 8, LANES), pltpu.VMEM
    )
    back = pl.pallas_call(
        beam_kernel,
        grid=(6,),
        in_specs=[
            pl.BlockSpec(memory_space=pltpu.SMEM),
            pl.BlockSpec(memory_space=pltpu.SMEM),
            pl.BlockSpec(memory_space=pltpu.VMEM),
            pl.BlockSpec(memory_space=pl.ANY),
        ],
        out_specs=pl.BlockSpec((4 * devices, LANES), lambda i: (0, 0)),
        out_shape=jax.ShapeDtypeStruct((4 * devices, LANES), jnp.bfloat16),
        scratch_shapes=[
            pltpu.VMEM((16, 64, 2048), jnp.bfloat16),
            pltpu.VMEM((8, 64, LANES), jnp.float32),
            pltpu.VMEM((4 * devices, LANES), jnp.float32),
            pltpu.VMEM((16, beams, 2048), jnp.bfloat16),
            pltpu.SemaphoreType.DMA((4,)),
        ],
        name="beams",
        compiler_params=pltpu.CompilerParams(vmem_limit_bytes=VMEM_LIMIT),
    )(own_b[None], lam, received, steer)

    returned = lax.all_to_all(back.reshape(devices, 4, LANES), AXES, 0, 0, tiled=True)
    return pl.pallas_call(
        synthesis_kernel,
        in_specs=[pl.BlockSpec(memory_space=pltpu.VMEM)] * 4,
        out_specs=pl.BlockSpec(memory_space=pltpu.VMEM),
        out_shape=jax.ShapeDtypeStruct((2, 1, 8, 4096), jnp.bfloat16),
        scratch_shapes=[
            pltpu.VMEM((4 * devices, LANES), jnp.float32),
            pltpu.VMEM((12 * COLS, 2 * LANES), jnp.bfloat16),
            pltpu.VMEM((2, 16 * COLS, LANES), jnp.float32),
            pltpu.VMEM((2, 2, COLS, 8, LANES), jnp.float32),
        ],
        name="synthesis",
        compiler_params=pltpu.CompilerParams(vmem_limit_bytes=VMEM_LIMIT),
    )(returned.reshape(4 * devices, LANES), proto, tw_inverse, w_inverse)


def solution(mesh):
    placed = (P(None, "gx", "section", None), P(), P(), P(AXES))
    return jax.shard_map(
        body, mesh=mesh, in_specs=placed, out_specs=P(None, "gx", "section", None), check_vma=False
    )
```
